32 devices in a mesh: groups: 2 (over x), gx: 8 (over z, y), gy: 2 (over core).
Axes of the slice: x: 2, y: 2, z: 4, core: 2. Of those that a mesh axis runs over, the one named last changes fastest.
Arguments:
- features: bfloat16 [64, 512, 1280], P(('groups', 'gy'), 'gx'), parts along dimension 0, may hold values from -600 to 600
- probe_weight: bfloat16 [1280, 32], replicated, may hold values from -0.15625 to 0.15625
- probe_bias: float32 [32], replicated, may hold values from -4 to 4
- labels: int32 [896, 7168], P(('groups', 'gy'), 'gx'), parts along dimension 0, may hold values from 0 to 31
- valid_mask: int32 [896, 7168], P(('groups', 'gy'), 'gx'), parts along dimension 0, may hold values 0 or 1
- valid_count: int32 [4, 8], P(('groups', 'gy'), 'gx'), parts along dimension 0, may hold values from 50176 to 301056
Outputs:
- loss: float32 [2], P('groups'), parts along dimension 0
- grad_weight: float32 [2560, 32], P('groups'), parts along dimension 0
- grad_bias: float32 [64], P('groups'), parts along dimension 0
The draws below stay inside these ranges and needn't reach their ends.
There are 2 independent parts, one for each index of `groups`. The reference program is written for one: setup_inputs(seed, part) draws one part's arguments, and reference() takes and returns one part's arrays. A program takes and returns all parts, laid end to end along the dimension named above; an argument that names none is the same for every part. Nothing has to cross between parts.
All inputs are finite; a program needn't handle non-finite values. No bound on the sum of `valid_mask` on one device may be relied on, other than what follows from the above.
Results may differ from the reference program's by a relative error of at most 0.0016.
Values sent between devices are 32-bit elements; how exact they have to be, the bound alone decides.
No kernel may reach another device: no remote copies, remote signals or barrier semaphores. Data moves between devices by JAX's collectives and lax.ppermute only.
A program may use at most 128 MiB of HBM per device.

```python
import jax
import jax.numpy as jnp
from jax import lax

D = 1280
PATCH = 14
CLASSES = 32
ROWBLOCK = 4
PH = 16
PW = 64
HP = 32
WP = 512
N_GX = 8
N_GY = 2


def draw_features(key, part):
    shape = (PH * N_GY, PW * N_GX, D)
    base = jax.random.truncated_normal(key, -6.0, 6.0, shape, jnp.float32)
    return base.astype(jnp.bfloat16)


def draw_valid_count(key, part):
    base = jax.random.randint(key, (N_GY, N_GX), 49 * PH * PW, 98 * PH * PW + 1, jnp.int32)
    column = jnp.arange(N_GX, dtype=jnp.int32)[None, :]
    return base * (N_GX - 1 + 2 * column) // (N_GX - 1)


def with_ends(values, key, least, top_value):
    extent = values.shape
    index_at = [jax.random.randint(jax.random.fold_in(key, axis), (), 0, extent[axis]) for axis in range(len(extent))]
    values = values.at[tuple(index_at)].set(least)
    longest = extent.index(max(extent))
    index_at[longest] = (index_at[longest] + 1) % extent[longest]
    return values.at[tuple(index_at)].set(top_value)


def noise(key, shape, spread, most, kind=jnp.bfloat16):
    drawn = spread * jax.random.normal(key, shape, jnp.float32)
    return jnp.clip(drawn, min=-most, max=most).astype(kind)


def setup_inputs(seed: int = 0, part: int = 0) -> dict:
    streams_of = jax.random.split(jax.random.key(seed), 7)
    own_keys = jax.random.split(jax.random.fold_in(streams_of[6], part), 7)
    features = draw_features(jax.random.fold_in(jax.random.fold_in(streams_of[6], part), 71), part)
    probe_weight = noise(streams_of[1], (D, CLASSES), D ** -0.5, 0.15625)
    probe_bias = noise(streams_of[2], (CLASSES,), 1.0, 4.0, jnp.float32)
    labels = with_ends(jax.random.randint(own_keys[3], (HP * PATCH, WP * PATCH), 0, CLASSES), jax.random.fold_in(own_keys[3], 1), 0, CLASSES - 1).astype(jnp.int32)
    valid_mask = with_ends((jax.random.randint(own_keys[4], (HP * PATCH, WP * PATCH), 0, 4) < 3).astype(jnp.int32), jax.random.fold_in(own_keys[4], 1), 0, 1)
    valid_count = draw_valid_count(jax.random.fold_in(jax.random.fold_in(streams_of[6], part), 71), part)
    return {"features": features, "probe_weight": probe_weight, "probe_bias": probe_bias, "labels": labels, "valid_mask": valid_mask, "valid_count": valid_count}


def weights_table():
    offset = jnp.arange(PATCH, dtype=jnp.float32)
    shift = (offset + 0.5) / PATCH - 0.5
    return jnp.maximum(-shift, 0.0), jnp.abs(shift) * -1.0 + 1.0, jnp.maximum(shift, 0.0)


def widen_cols(padded):
    before, centre, after = weights_table()
    chans, height, width = padded.shape[0], padded.shape[1], padded.shape[2] - 2
    out = padded[:, :, 1:-1, None] * centre + padded[:, :, :-2, None] * before + padded[:, :, 2:, None] * after
    return out.reshape(chans, height, width * PATCH)


def narrow_cols(grad):
    before, centre, after = weights_table()
    chans, height, span = grad.shape
    parts = grad.reshape(chans, height, span // PATCH, PATCH)
    mid = jnp.sum(parts * centre, axis=3)
    low = jnp.sum(parts * before, axis=3)
    high = jnp.sum(parts * after, axis=3)
    return jnp.pad(mid, ((0, 0), (0, 0), (1, 1))) + jnp.pad(low, ((0, 0), (0, 0), (0, 2))) + jnp.pad(high, ((0, 0), (0, 0), (2, 0)))


def widen_rows(slab):
    before, centre, after = weights_table()
    chans, count, span = slab.shape[0], slab.shape[1] - 2, slab.shape[2]
    out = slab[:, 1:-1, None, :] * centre[:, None] + slab[:, :-2, None, :] * before[:, None] + slab[:, 2:, None, :] * after[:, None]
    return out.reshape(chans, count * PATCH, span)


def narrow_rows(grad):
    before, centre, after = weights_table()
    chans, pixrows, span = grad.shape
    parts = grad.reshape(chans, pixrows // PATCH, PATCH, span)
    mid = jnp.sum(parts * centre[:, None], axis=2)
    low = jnp.sum(parts * before[:, None], axis=2)
    high = jnp.sum(parts * after[:, None], axis=2)
    return jnp.pad(mid, ((0, 0), (1, 1), (0, 0))) + jnp.pad(low, ((0, 0), (0, 2), (0, 0))) + jnp.pad(high, ((0, 0), (2, 0), (0, 0)))


def run_blocks(widened, labels, valid_mask):
    chans = widened.shape[0]
    blocks = (labels.shape[0] // PATCH) // ROWBLOCK
    classes = jnp.arange(chans, dtype=jnp.int32)

    def step(carry, index):
        grad_pad, total = carry
        start = (index * ROWBLOCK).astype(jnp.int32)
        slab = lax.dynamic_slice_in_dim(widened, start, ROWBLOCK + 2, 1)
        label_rows = lax.dynamic_slice_in_dim(labels, (start * PATCH).astype(jnp.int32), ROWBLOCK * PATCH, 0)
        mask_rows = lax.dynamic_slice_in_dim(valid_mask, (start * PATCH).astype(jnp.int32), ROWBLOCK * PATCH, 0)
        scores = widen_rows(slab)
        top = jnp.max(scores, axis=0)
        lse = top + jnp.log(jnp.sum(jnp.exp(scores - top[None]), axis=0))
        onehot = (classes[:, None, None] == label_rows[None]).astype(jnp.float32)
        weight = mask_rows.astype(jnp.float32)
        picked = jnp.sum(onehot * scores, axis=0)
        total = total + jnp.sum(weight * (lse - picked))
        pixel_grad = weight[None] * (jnp.exp(scores - lse[None]) - onehot)
        back = narrow_rows(pixel_grad)
        old = lax.dynamic_slice_in_dim(grad_pad, start, ROWBLOCK + 2, 1)
        grad_pad = lax.dynamic_update_slice_in_dim(grad_pad, old + back, start, 1)
        return (grad_pad, total), None

    init = (jnp.zeros(widened.shape, jnp.float32), jnp.zeros((), jnp.float32))
    (grad_pad, total), unused = lax.scan(step, init, jnp.arange(blocks, dtype=jnp.int32))
    return grad_pad, total


def fold_edges(grad):
    grad = jnp.concatenate([grad[:, 1:2] + grad[:, 0:1], grad[:, 2:-2], grad[:, -2:-1] + grad[:, -1:]], axis=1)
    return jnp.concatenate([grad[:, :, 1:2] + grad[:, :, 0:1], grad[:, :, 2:-2], grad[:, :, -2:-1] + grad[:, :, -1:]], axis=2)


def reference(features, probe_weight, probe_bias, labels, valid_mask, valid_count):
    rows, cols, width = features.shape
    flat = features.reshape(rows * cols, width)
    logits = jnp.dot(flat, probe_weight, preferred_element_type=jnp.float32) + probe_bias[None, :]
    chans = logits.shape[1]
    logits = logits.reshape(rows, cols, chans).transpose(2, 0, 1)
    padded = jnp.pad(logits, ((0, 0), (1, 1), (1, 1)), mode="edge")
    widened = widen_cols(padded)
    grad_pad, loss_sum = run_blocks(widened, labels, valid_mask)
    patch_grad = fold_edges(narrow_cols(grad_pad))
    rounded = patch_grad.astype(jnp.bfloat16).reshape(chans, rows * cols).T
    total = jnp.sum(valid_count).astype(jnp.float32)
    grad_weight = lax.dot_general(flat, rounded, (((0,), (0,)), ((), ())), preferred_element_type=jnp.float32) / total
    grad_bias = jnp.sum(patch_grad, axis=(1, 2)) / total
    return (loss_sum / total).reshape(1), grad_weight, grad_bias
```

```python
import functools
import math

import jax
import jax.numpy as jnp
import numpy as np
from jax import lax
from jax.experimental import pallas as pl
from jax.experimental.pallas import tpu as pltpu
from jax.sharding import PartitionSpec as P

PATCH = 14
HALF = PATCH // 2
STEP = 2 * PATCH
LANES = 128
SUB = 8
LOG2E = 1.0 / math.log(2.0)
LN2 = math.log(2.0)
FLOOR = -100.0
f32 = jnp.float32
bf16 = jnp.bfloat16
VMEM = pl.BlockSpec(memory_space=pltpu.VMEM)
SMEM = pl.BlockSpec(memory_space=pltpu.SMEM)


def whole(shape):
    return pl.BlockSpec(shape, lambda *ids: (0,) * len(shape))


def column_tables(cols):
    near = np.array([STEP - abs(2 * j + 1 - PATCH) for j in range(PATCH)])
    far = STEP - near
    inner = np.zeros((cols, cols * PATCH), np.float32)
    for q in range(cols * PATCH):
        i, j = divmod(q, PATCH)
        inner[i, q] += near[j]
        k = i - 1 if j < HALF else i + 1
        if 0 <= k < cols:
            inner[k, q] += far[j]
    own = np.zeros((cols, LANES), np.float32)
    halo = np.zeros((2, LANES), np.float32)
    for lane in range(4 * HALF):
        side, k = divmod(lane, HALF)
        j = k + HALF if side in (0, 2) else k
        edge = 0 if side < 2 else cols - 1
        outside = side in (0, 3)
        own[edge, lane] = far[j] if outside else near[j]
        halo[int(side > 1), lane] = near[j] if outside else far[j]
    return inner, own, halo


def split3(x):
    hi = x.astype(bf16)
    rest = x - hi.astype(f32)
    mid = rest.astype(bf16)
    return hi, mid, (rest - mid.astype(f32)).astype(bf16)


def stack3(x, cols):
    lane = lax.broadcasted_iota(jnp.int32, x.shape, 1)
    hi, mid, low = (part.astype(f32) for part in split3(jnp.where(lane < cols, x, 0.0)))
    first = jnp.where(lane < cols, hi, pltpu.roll(mid, cols, 1))
    return jnp.concatenate([first.astype(bf16), low.astype(bf16)], axis=1)


def logits_kernel(
    rows, cols, chans, slots, per, f_ref, w_ref, bias_ref, ll_ref, lr_ref, ml_ref, mr_ref, sel_ref,
    x_ref, e_ref, sa_ref, sb_ref,
):
    step = pl.program_id(0)
    steps = pl.num_programs(0)

    @pl.when(step == 0)
    def _():
        x_ref[...] = jnp.zeros_like(x_ref)

    block = f_ref[...].reshape(per * cols, f_ref.shape[2])
    score = lax.dot_general(w_ref[...], block, (((1,), (1,)), ((), ())), preferred_element_type=f32)
    score = score + bias_ref[...]
    score = (score - jnp.max(score, axis=0, keepdims=True)) * (LOG2E / STEP)
    lane = lax.broadcasted_iota(jnp.int32, (chans, LANES), 1)
    for k in range(per):
        at = k * cols
        tile = score[:, at // LANES * LANES : at // LANES * LANES + LANES]
        if at % LANES:
            tile = pltpu.roll(tile, LANES - at % LANES, 1)
        tile = jnp.where(lane < cols, tile, 0.0)
        x_ref[pl.ds(step * per + k + 1, chans, stride=slots), :] = tile
        if k == 0:

            @pl.when(step == 0)
            def _():
                e_ref[0:chans, :] = tile

        if k == per - 1:

            @pl.when(step == steps - 1)
            def _():
                e_ref[chans : 2 * chans, :] = tile

    @pl.when(step == steps - 1)
    def _():
        edges = lax.dot_general(
            sel_ref[...], stack3(x_ref[...], cols), (((1,), (1,)), ((), ())), preferred_element_type=f32
        )
        at = lax.broadcasted_iota(jnp.int32, (SUB, LANES), 1)
        even = lax.rem(lax.axis_index("gx"), 2) == 0
        n = chans * slots // LANES
        for b in range(rows // SUB):
            left = jnp.full((SUB, LANES), -1.0, f32)
            right = left
            for j in range(PATCH):
                pick = pl.ds(b * SUB * PATCH + j, SUB, stride=PATCH)
                here = (at >= j * HALF) & (at < j * HALF + HALF)
                lab = jnp.where(ml_ref[pick, :] != 0, ll_ref[pick, :], -1).astype(f32)
                shift = j * HALF
                left = jnp.where(here, pltpu.roll(lab, shift, 1) if shift else lab, left)
                lab = jnp.where(mr_ref[pick, :] != 0, lr_ref[pick, :], -1).astype(f32)
                right = jnp.where(here, pltpu.roll(lab, (shift + HALF) % LANES, 1), right)
            sa_ref[b * SUB : b * SUB + SUB, :] = jnp.where(even, right, left)
            sb_ref[b * SUB : b * SUB + SUB, :] = jnp.where(even, left, right)
        for r in range(n):
            part = edges[:, r * LANES : r * LANES + LANES]
            sa_ref[rows + r : rows + r + 1, :] = jnp.where(even, part[1:2], part[0:1])
            sb_ref[rows + r : rows + r + 1, :] = jnp.where(even, part[0:1], part[1:2])
        pad = sa_ref.shape[0] - rows - n
        if pad:
            sa_ref[rows + n :, :] = jnp.zeros((pad, LANES), f32)
            sb_ref[rows + n :, :] = jnp.zeros((pad, LANES), f32)


def softmax_fast(groups, chans, slots, up, w_ref, p_ref):
    sums = [None] * (groups * HALF)
    for c in range(chans):
        for b in range(groups):
            row = c * slots + SUB * b
            centre = w_ref[pl.ds(row + 1, SUB), :]
            beyond = w_ref[pl.ds(row + (2 if up else 0), SUB), :]
            slope = (beyond - centre) * (1.0 / STEP)
            p = jnp.exp2(centre + slope)
            ratio = jnp.exp2(slope + slope)
            for m in range(HALF):
                k = b * HALF + m
                if m:
                    p = p * ratio
                p_ref[c * groups * HALF + k] = p
                sums[k] = p if sums[k] is None else sums[k] + p
    return sums


def softmax_slow(groups, chans, slots, up, w_ref, p_ref, labels, weights):
    sums, losses = [], jnp.zeros((SUB, LANES), f32)
    for b in range(groups):
        for m in range(HALF):
            k = b * HALF + m

            def score(c, b=b, m=m):
                row = c * slots + SUB * b
                centre = w_ref[pl.ds(row + 1, SUB), :]
                beyond = w_ref[pl.ds(row + (2 if up else 0), SUB), :]
                return centre + (beyond - centre) * ((2 * m + 1.0) / STEP)

            top = lax.fori_loop(1, chans, lambda c, t: jnp.maximum(t, score(c)), score(0))

            def take(c, carry, k=k, top=top, score=score):
                total, picked = carry
                shifted = score(c) - top
                p = jnp.exp2(shifted)
                p_ref[c * groups * HALF + k] = p
                return total + p, jnp.where(labels[k] == c, shifted, picked)

            zero = jnp.zeros((SUB, LANES), f32)
            total, picked = lax.fori_loop(0, chans, take, (zero, zero))
            sums.append(total)
            losses = losses - weights[k] * picked
    return sums, losses


def pixels(groups, chans, slots, load_labels, fast, w_ref, p_ref, g_ref, s_ref):
    count = groups * HALF
    g_ref[...] = jnp.zeros_like(g_ref)
    loss = jnp.zeros((SUB, LANES), f32)
    for up in (False, True):
        labels = [None] * count
        for m in range(HALF):
            for b in range(groups):
                labels[b * HALF + m] = load_labels(b, HALF + m if up else HALF - 1 - m)
        weights = [jnp.where(lab >= 0, 1.0, 0.0) for lab in labels]
        packed = [
            jnp.concatenate([labels[b * HALF + m] for b in range(groups)], axis=0).astype(jnp.int16)
            for m in range(HALF)
        ]

        @pl.when(fast)
        def _():
            sums = softmax_fast(groups, chans, slots, up, w_ref, p_ref)
            for k in range(count):
                s_ref[k] = sums[k]
            s_ref[count] = jnp.zeros((SUB, LANES), f32)

        @pl.when(jnp.logical_not(fast))
        def _():
            sums, losses = softmax_slow(groups, chans, slots, up, w_ref, p_ref, labels, weights)
            for k in range(count):
                s_ref[k] = sums[k]
            s_ref[count] = losses

        sums = [s_ref[k] for k in range(count)]
        extra = s_ref[count]
        scale = []
        for k in range(count):
            loss = loss + weights[k] * jnp.log(sums[k])
            scale.append(weights[k] / sums[k])
        picked = jnp.zeros((SUB, LANES), f32)
        for c in range(chans):
            tally = None
            for m in range(HALF):
                hit = jnp.where(packed[m] == jnp.int16(c), jnp.int16(1 + SUB * (2 * m + 1)), jnp.int16(0))
                tally = hit if tally is None else tally + hit
            tally = tally.astype(jnp.int32)
            for b in range(groups):
                total = run = None
                for m in reversed(range(HALF)):
                    g = p_ref[c * count + b * HALF + m] * scale[b * HALF + m]
                    total = g if total is None else total + g
                    run = total if run is None else run + total
                part = tally[b * SUB : b * SUB + SUB]
                ones = (part & (SUB - 1)).astype(f32)
                far = lax.shift_right_logical(part, 3).astype(f32) * (1.0 / STEP)
                centre = pl.ds(c * slots + 1 + SUB * b, SUB)
                beyond = pl.ds(c * slots + (2 if up else 0) + SUB * b, SUB)
                picked = picked + (ones - far) * w_ref[centre, :] + far * w_ref[beyond, :]
                out = (run + run - total) * (1.0 / STEP) - far
                g_ref[centre, :] += (total - ones) - out
                g_ref[beyond, :] += out
        loss = loss + LN2 * jnp.where(fast, -picked, extra)
    return loss


def narrow(g_ref, table):
    g = g_ref[...]
    hi = g.astype(bf16)
    low = (g - hi.astype(f32)).astype(bf16)
    return jnp.dot(jnp.concatenate([hi, low], axis=1), table, preferred_element_type=f32)


def inner_kernel(
    cols, chans, slots, groups, x_ref, own_ref, got_ref, table_ref, back_ref, lab_ref, mask_ref,
    acc_ref, loss_ref, stack_ref, floor_ref, w_ref, p_ref, g_ref, s_ref, h_ref,
):
    step = pl.program_id(0)

    @pl.when(step == 0)
    def _():
        h_ref[...] = x_ref[...]
        row = lax.axis_index("gy")
        top = jnp.where(row == 0, own_ref[0:chans, :], got_ref[chans : 2 * chans, :])
        last = row == lax.axis_size("gy") - 1
        bottom = jnp.where(last, own_ref[chans : 2 * chans, :], got_ref[0:chans, :])
        h_ref[pl.ds(0, chans, stride=slots), :] = top
        h_ref[pl.ds(groups * SUB + 1, chans, stride=slots), :] = bottom
        full = h_ref[...]
        floor_ref[0] = jnp.min(full) * STEP
        stack_ref[...] = stack3(full, cols)
        acc_ref[...] = jnp.zeros_like(acc_ref)
        loss_ref[...] = jnp.zeros_like(loss_ref)

    w_ref[...] = jnp.dot(stack_ref[...], table_ref[...], preferred_element_type=f32)
    lane = lax.broadcasted_iota(jnp.int32, (SUB, LANES), 1) + step * LANES
    inside = (lane >= HALF) & (lane < cols * PATCH - HALF)

    def load_labels(b, j):
        pick = pl.ds(b * SUB * PATCH + j, SUB, stride=PATCH)
        return jnp.where((mask_ref[pick, :] != 0) & inside, lab_ref[pick, :], -1)

    fast = floor_ref[0] >= FLOOR
    loss_ref[...] += pixels(groups, chans, slots, load_labels, fast, w_ref, p_ref, g_ref, s_ref)
    acc_ref[...] += narrow(g_ref, back_ref[...])


def edge_kernel(
    rows, cols, chans, slots, groups, floor_ref, stack_ref, acc_ref, loss_in_ref, sa_ref, sb_ref, ra_ref, rb_ref,
    va_ref, vb_ref, table_ref, fold_ref, back_ref, halo_ref, out_ref, v_ref, loss_ref, w_ref, p_ref, g_ref, s_ref,
):
    col = lax.axis_index("gx")
    row = lax.axis_index("gy")
    even = lax.rem(col, 2) == 0
    first, last = col == 0, col == lax.axis_size("gx") - 1
    n = chans * slots // LANES
    width = n * LANES

    def line(ref):
        return jnp.concatenate([ref[rows + r : rows + r + 1, :] for r in range(n)], axis=1)

    slot = lax.rem(lax.broadcasted_iota(jnp.int32, (1, width), 1), slots)

    def with_ends(mine, partner):
        top = jnp.where(row == 0, pltpu.roll(mine, width - 1, 1), pltpu.roll(partner, width - rows, 1))
        bottom = jnp.where(row == lax.axis_size("gy") - 1, pltpu.roll(mine, 1, 1), pltpu.roll(partner, rows, 1))
        return jnp.where(slot == 0, top, jnp.where(slot == rows + 1, bottom, mine))

    a = with_ends(line(ra_ref), line(va_ref))
    b = with_ends(line(rb_ref), line(vb_ref))
    sides = [jnp.where(even, b, a), jnp.where(even, a, b)]
    absent = [first, last]
    lows = jnp.float32(0.0)
    parts = []
    for side, gone in zip(sides, absent):
        side = jnp.where(gone, 0.0, side)
        lows = jnp.minimum(lows, jnp.min(side))
        parts += [part.astype(f32) for part in split3(side)]
    parts.append(jnp.zeros((16 - len(parts), width), f32))
    halo = jnp.concatenate(parts, axis=0).astype(bf16)
    table = table_ref[...]
    back = back_ref[...]
    depth = table.shape[0]
    zero = jnp.zeros_like(table)
    table = table + jnp.where(first, fold_ref[0:depth, :], zero) + jnp.where(last, fold_ref[depth : 2 * depth, :], zero)
    back = back + jnp.where(first, fold_ref[2 * depth : 3 * depth, :], zero)
    back = back + jnp.where(last, fold_ref[3 * depth : 4 * depth, :], zero)
    w_ref[...] = jnp.dot(stack_ref[...], table, preferred_element_type=f32) + lax.dot_general(
        halo, halo_ref[...], (((0,), (0,)), ((), ())), preferred_element_type=f32
    )
    lane = lax.broadcasted_iota(jnp.int32, (SUB, LANES), 1)

    def load_labels(b, j):
        pick = slice(b * SUB, b * SUB + SUB)
        strips = [
            jnp.where(first, -1.0, jnp.where(even, rb_ref[pick, :], ra_ref[pick, :])),
            jnp.where(even, sb_ref[pick, :], sa_ref[pick, :]),
            jnp.where(even, sa_ref[pick, :], sb_ref[pick, :]),
            jnp.where(last, -1.0, jnp.where(even, ra_ref[pick, :], rb_ref[pick, :])),
        ]
        out = jnp.full((SUB, LANES), -1.0, f32)
        for k, strip in enumerate(strips):
            shift = (k * HALF - j * HALF) % LANES
            moved = pltpu.roll(strip, shift, 1) if shift else strip
            out = jnp.where((lane >= k * HALF) & (lane < k * HALF + HALF), moved, out)
        return out.astype(jnp.int32)

    fast = jnp.minimum(lows * STEP, floor_ref[0]) >= FLOOR
    outside = (lane < HALF) | (lane >= 3 * HALF)
    loss = pixels(groups, chans, slots, load_labels, fast, w_ref, p_ref, g_ref, s_ref)
    loss_ref[...] = loss_in_ref[...] + jnp.where(outside, 0.0, loss)
    out_ref[...] = (acc_ref[...] + narrow(g_ref, back)) * (1.0 / STEP)
    v_ref[0:chans, :] = out_ref[pl.ds(0, chans, stride=slots), :]
    v_ref[chans : 2 * chans, :] = out_ref[pl.ds(rows + 1, chans, stride=slots), :]


def grad_kernel(
    rows, cols, chans, slots, per, f_ref, g_ref, own_ref, got_ref, loss_ref, count_ref,
    mine_ref, other_ref, sum_ref, acc_ref,
):
    step = pl.program_id(0)
    row = lax.axis_index("gy")

    @pl.when(step == 0)
    def _():
        sum_ref[...] = g_ref[...]
        last = row == lax.axis_size("gy") - 1
        top = jnp.where(row == 0, own_ref[0:chans, :], got_ref[chans : 2 * chans, :])
        bottom = jnp.where(last, own_ref[chans : 2 * chans, :], got_ref[0:chans, :])
        sum_ref[pl.ds(1, chans, stride=slots), :] += top
        sum_ref[pl.ds(rows, chans, stride=slots), :] += bottom
        acc_ref[...] = jnp.zeros_like(acc_ref)

    lane = lax.broadcasted_iota(jnp.int32, (chans, LANES), 1)
    share = LANES // cols
    tiles = []
    for k in range(0, per, share):
        tile = None
        for r in range(share):
            piece = sum_ref[pl.ds(step * per + k + r + 1, chans, stride=slots), :]
            if r:
                piece = pltpu.roll(piece, r * cols, 1)
            tile = piece if tile is None else jnp.where(lane < r * cols, tile, piece)
        tiles.append(tile.astype(bf16))
    block = f_ref[...].reshape(per * cols, f_ref.shape[2])
    acc_ref[...] += jnp.dot(jnp.concatenate(tiles, axis=1), block, preferred_element_type=f32)

    @pl.when(step == pl.num_programs(0) - 1)
    def _():
        total = sum_ref[pl.ds(1, chans, stride=slots), :]
        for i in range(2, rows + 1):
            total = total + sum_ref[pl.ds(i, chans, stride=slots), :]
        total = jnp.where(lane < cols, total, 0.0)
        square = jnp.concatenate([total, jnp.zeros((LANES - chans, LANES), f32)], axis=0)
        bias = jnp.sum(square.T, axis=0, keepdims=True)
        at = lax.broadcasted_iota(jnp.int32, (SUB, LANES), 0)
        rest = jnp.where(at == 1, jnp.sum(loss_ref[...]), count_ref[0, 0].astype(f32))
        stats = jnp.where(at == 0, bias, jnp.where(at < 3, rest, 0.0))
        half = acc_ref.shape[1] // 2
        low, high = acc_ref[:, 0:half], acc_ref[:, half:]
        mine_ref[:, 0:half] = jnp.where(row == 0, low, high)
        other_ref[:, 0:half] = jnp.where(row == 0, high, low)
        for ref in (mine_ref, other_ref):
            ref[0:SUB, half:] = stats
            ref[SUB:, half:] = jnp.zeros((chans - SUB, LANES), f32)


def final_kernel(y_ref, z_ref, loss_ref, weight_ref, bias_ref):
    chans = y_ref.shape[0]
    half = y_ref.shape[1] - LANES
    lower = lax.axis_index("gy") == 0
    y, z = y_ref[:, 0:half], z_ref[:, 0:half]
    stats = y_ref[0:SUB, half:]
    total = stats[2:3, 0:1]
    weight_ref[:, 0:half] = jnp.where(lower, y, z) / total
    weight_ref[:, half:] = jnp.where(lower, z, y) / total
    loss_ref[...] = stats[1:2, 0:1] / total
    bias_ref[...] = stats[0:1, 0:chans] / total


def body(features, probe_weight, probe_bias, labels, valid_mask, valid_count):
    rows, cols, width = features.shape
    chans = probe_weight.shape[1]
    gx, gy = lax.axis_size("gx"), lax.axis_size("gy")
    if gy != 2 or rows % SUB or cols * PATCH % LANES or gx & (gx - 1):
        raise ValueError("unsupported tile")
    groups = rows // SUB
    slots = rows + SUB
    count = groups * HALF
    tiles = cols * PATCH // LANES
    tall = rows * PATCH
    depth = 2 * LANES
    inner, own, halo = column_tables(cols)

    def forward(table):
        out = np.zeros((depth, table.shape[1]), np.float32)
        for k in range(3):
            out[k * cols : k * cols + cols] = table
        return out

    def backward(table):
        out = np.zeros((table.shape[1] // LANES, 2, LANES, LANES), np.float32)
        out[:, :, :, :cols] = table.T.reshape(-1, 1, LANES, cols)
        return out.reshape(-1, LANES)

    lift, back = forward(inner), backward(inner)
    left, right = np.zeros_like(own), np.zeros_like(own)
    left[0], right[cols - 1] = halo
    fold = np.concatenate([forward(left), forward(right), backward(left), backward(right)])
    sides = np.zeros((16, LANES), np.float32)
    sides[0:3], sides[3:6] = halo[0], halo[1]
    ends = np.zeros((SUB, depth), np.float32)
    for k in range(3):
        ends[0, k * cols] = 1.0
        ends[1, k * cols + cols - 1] = 1.0
    lift, back, own_f, own_b, fold, sides, ends = (
        jnp.asarray(t, bf16) for t in (lift, back, forward(own), backward(own), fold, sides, ends)
    )

    per = 4
    shape = lambda *dims: jax.ShapeDtypeStruct(dims, f32)
    strip = -(-(rows + chans * slots // LANES) // SUB) * SUB
    block = pl.BlockSpec((per, cols, width), lambda i: (i, 0, 0))
    tail = pl.BlockSpec((tall, LANES), lambda i: (0, tiles - 1))
    head = pl.BlockSpec((tall, LANES), lambda i: (0, 0))
    x, edge, send_a, send_b = pl.pallas_call(
        functools.partial(logits_kernel, rows, cols, chans, slots, per),
        grid=(rows // per,),
        in_specs=[block, whole((chans, width)), whole((chans, 1)), head, tail, head, tail, whole((SUB, depth))],
        out_specs=[whole((chans * slots, LANES)), whole((2 * chans, LANES)), whole((strip, LANES)), whole((strip, LANES))],
        out_shape=[shape(chans * slots, LANES), shape(2 * chans, LANES), shape(strip, LANES), shape(strip, LANES)],
        name="logits",
    )(features, probe_weight.T, probe_bias.reshape(chans, 1), labels, labels, valid_mask, valid_mask, ends)

    swap = lambda v: lax.ppermute(v, "gy", [(0, 1), (1, 0)])
    pairs = lambda at: [p for i in range(at, gx - 1, 2) for p in ((i, i + 1), (i + 1, i))]
    got = swap(edge)
    got_a = lax.ppermute(send_a, "gx", pairs(0))
    got_b = lax.ppermute(send_b, "gx", pairs(1))

    scratch = [
        pltpu.VMEM((chans * slots, LANES), f32),
        pltpu.VMEM((chans * count, SUB, LANES), f32),
        pltpu.VMEM((chans * slots, LANES), f32),
        pltpu.VMEM((count + 1, SUB, LANES), f32),
    ]
    column = pl.BlockSpec((tall, LANES), lambda t: (0, t))
    acc, loss, stack, floor = pl.pallas_call(
        functools.partial(inner_kernel, cols, chans, slots, groups),
        grid=(tiles,),
        in_specs=[
            whole((chans * slots, LANES)), whole((2 * chans, LANES)), whole((2 * chans, LANES)),
            pl.BlockSpec((depth, LANES), lambda t: (0, t)), pl.BlockSpec((depth, LANES), lambda t: (t, 0)),
            column, column,
        ],
        out_specs=[whole((chans * slots, LANES)), whole((SUB, LANES)), whole((chans * slots, depth)), SMEM],
        out_shape=[
            shape(chans * slots, LANES), shape(SUB, LANES),
            jax.ShapeDtypeStruct((chans * slots, depth), bf16), shape(1),
        ],
        scratch_shapes=scratch + [pltpu.VMEM((chans * slots, LANES), f32)],
        cost_estimate=pl.CostEstimate(flops=2 * 10**9, bytes_accessed=4 * 10**6, transcendentals=10**6),
        name="inner",
    )(x, edge, got, lift, back, labels, valid_mask)

    far_a, far_b = swap(got_a), swap(got_b)
    grad, spill, loss = pl.pallas_call(
        functools.partial(edge_kernel, rows, cols, chans, slots, groups),
        in_specs=[SMEM] + [VMEM] * 13,
        out_specs=[VMEM] * 3,
        out_shape=[shape(chans * slots, LANES), shape(2 * chans, LANES), shape(SUB, LANES)],
        scratch_shapes=scratch,
        name="edge",
    )(floor, stack, acc, loss, send_a, send_b, got_a, got_b, far_a, far_b, own_f, fold, own_b, sides)

    got = swap(spill)
    half = width // 2
    part = whole((chans, half + LANES))
    mine, other = pl.pallas_call(
        functools.partial(grad_kernel, rows, cols, chans, slots, per),
        grid=(rows // per,),
        in_specs=[
            block, whole((chans * slots, LANES)), whole((2 * chans, LANES)), whole((2 * chans, LANES)),
            whole((SUB, LANES)), SMEM,
        ],
        out_specs=[part, part],
        out_shape=[shape(chans, half + LANES)] * 2,
        scratch_shapes=[pltpu.VMEM((chans * slots, LANES), f32), pltpu.VMEM((chans, width), f32)],
        name="grad",
    )(features, grad, spill, got, loss, valid_count)

    total = mine + swap(other)
    step = 1
    while step < gx:
        total = total + lax.ppermute(total, "gx", [(i, i ^ step) for i in range(gx)])
        step *= 2
    loss, weight, bias = pl.pallas_call(
        final_kernel,
        in_specs=[VMEM] * 2,
        out_specs=[VMEM] * 3,
        out_shape=[shape(1, 1), shape(chans, width), shape(1, chans)],
        name="final",
    )(total, swap(total))
    return loss.reshape(1), weight.T, bias.reshape(chans)


def solution(mesh):
    return jax.shard_map(
        body,
        mesh=mesh,
        in_specs=(
            P(("groups", "gy"), "gx", None),
            P(),
            P(),
            P(("groups", "gy"), "gx"),
            P(("groups", "gy"), "gx"),
            P(("groups", "gy"), "gx"),
        ),
        out_specs=(P("groups"), P("groups", None), P("groups")),
        check_vma=False,
    )
```

```python
import functools
import math

import jax
import jax.numpy as jnp
import numpy as np
from jax import lax
from jax.experimental import pallas as pl
from jax.experimental.pallas import tpu as pltpu
from jax.sharding import PartitionSpec as P

PATCH = 14
HALF = PATCH // 2
STEP = 2 * PATCH
LANES = 128
SUB = 8
LOG2E = 1.0 / math.log(2.0)
LN2 = math.log(2.0)
FLOOR = -100.0
f32 = jnp.float32
bf16 = jnp.bfloat16
VMEM = pl.BlockSpec(memory_space=pltpu.VMEM)
ANY = pl.BlockSpec(memory_space=pl.ANY)
ROOM = pltpu.CompilerParams(vmem_limit_bytes=16 * 2**20)
SMEM = pl.BlockSpec(memory_space=pltpu.SMEM)


def whole(shape):
    return pl.BlockSpec(shape, lambda *ids: (0,) * len(shape))


def column_tables(cols):
    near = np.array([STEP - abs(2 * j + 1 - PATCH) for j in range(PATCH)])
    far = STEP - near
    inner = np.zeros((cols, cols * PATCH), np.float32)
    for q in range(cols * PATCH):
        i, j = divmod(q, PATCH)
        inner[i, q] += near[j]
        k = i - 1 if j < HALF else i + 1
        if 0 <= k < cols:
            inner[k, q] += far[j]
    own = np.zeros((cols, LANES), np.float32)
    halo = np.zeros((2, LANES), np.float32)
    for lane in range(4 * HALF):
        side, k = divmod(lane, HALF)
        j = k + HALF if side in (0, 2) else k
        edge = 0 if side < 2 else cols - 1
        outside = side in (0, 3)
        own[edge, lane] = far[j] if outside else near[j]
        halo[int(side > 1), lane] = near[j] if outside else far[j]
    return inner, own, halo


def split3(x):
    hi = x.astype(bf16)
    rest = x - hi.astype(f32)
    mid = rest.astype(bf16)
    return hi, mid, (rest - mid.astype(f32)).astype(bf16)


def stack3(x, cols):
    lane = lax.broadcasted_iota(jnp.int32, x.shape, 1)
    hi, mid, low = (part.astype(f32) for part in split3(jnp.where(lane < cols, x, 0.0)))
    first = jnp.where(lane < cols, hi, pltpu.roll(mid, cols, 1))
    return jnp.concatenate([first.astype(bf16), low.astype(bf16)], axis=1)


def logits_kernel(
    rows, cols, chans, slots, per, f_ref, w_ref, bias_ref, lab_ref, mask_ref, sel_ref,
    x_ref, e_ref, sa_ref, sb_ref, keep_ref, strip_ref, f_sem, s_sem,
):
    steps = rows // per
    tail = lab_ref.shape[1] - LANES
    loads = [
        pltpu.make_async_copy(f_ref.at[pl.ds(k * per, per)], keep_ref.at[pl.ds(k * per, per)], f_sem.at[k])
        for k in range(steps)
    ]
    strips = [
        pltpu.make_async_copy(ref.at[:, pl.ds(at, LANES)], strip_ref.at[k], s_sem.at[k])
        for k, (ref, at) in enumerate(((lab_ref, 0), (mask_ref, 0), (lab_ref, tail), (mask_ref, tail)))
    ]
    for copy in strips + loads:
        copy.start()
    x_ref[...] = jnp.zeros_like(x_ref)
    bias = jnp.concatenate([bias_ref[...], jnp.zeros((1, LANES - chans), f32)], axis=1)
    bias = jnp.broadcast_to(bias, (LANES, LANES)).T[0:chans, :]
    bias = jnp.concatenate([bias] * (per * cols // LANES), axis=1)
    at = lax.broadcasted_iota(jnp.int32, (SUB, LANES), 1)
    even = lax.rem(lax.axis_index("gx"), 2) == 0
    for copy in strips:
        copy.wait()
    for b in range(rows // SUB):
        left = jnp.full((SUB, LANES), -1.0, f32)
        right = left
        for j in range(PATCH):
            pick = pl.ds(b * SUB * PATCH + j, SUB, stride=PATCH)
            here = (at >= j * HALF) & (at < j * HALF + HALF)
            lab = jnp.where(strip_ref[1, pick, :] != 0, strip_ref[0, pick, :], -1).astype(f32)
            shift = j * HALF
            left = jnp.where(here, pltpu.roll(lab, shift, 1) if shift else lab, left)
            lab = jnp.where(strip_ref[3, pick, :] != 0, strip_ref[2, pick, :], -1).astype(f32)
            right = jnp.where(here, pltpu.roll(lab, (shift + HALF) % LANES, 1), right)
        sa_ref[b * SUB : b * SUB + SUB, :] = jnp.where(even, right, left)
        sb_ref[b * SUB : b * SUB + SUB, :] = jnp.where(even, left, right)
    lane = lax.broadcasted_iota(jnp.int32, (chans, LANES), 1)
    for step in range(steps):
        loads[step].wait()
        block = keep_ref[step * per : step * per + per].reshape(per * cols, f_ref.shape[2])
        score = lax.dot_general(w_ref[...], block, (((1,), (1,)), ((), ())), preferred_element_type=f32)
        score = score + bias
        score = (score - jnp.max(score, axis=0, keepdims=True)) * (LOG2E / STEP)
        for k in range(per):
            off = k * cols
            tile = score[:, off // LANES * LANES : off // LANES * LANES + LANES]
            if off % LANES:
                tile = pltpu.roll(tile, LANES - off % LANES, 1)
            tile = jnp.where(lane < cols, tile, 0.0)
            x_ref[pl.ds(step * per + k + 1, chans, stride=slots), :] = tile
            if step == 0 and k == 0:
                e_ref[0:chans, :] = tile
            if step == steps - 1 and k == per - 1:
                e_ref[chans : 2 * chans, :] = tile
    edges = lax.dot_general(
        sel_ref[...], stack3(x_ref[...], cols), (((1,), (1,)), ((), ())), preferred_element_type=f32
    )
    n = chans * slots // LANES
    for r in range(n):
        part = edges[:, r * LANES : r * LANES + LANES]
        sa_ref[rows + r : rows + r + 1, :] = jnp.where(even, part[1:2], part[0:1])
        sb_ref[rows + r : rows + r + 1, :] = jnp.where(even, part[0:1], part[1:2])
    pad = sa_ref.shape[0] - rows - n
    if pad:
        sa_ref[rows + n :, :] = jnp.zeros((pad, LANES), f32)
        sb_ref[rows + n :, :] = jnp.zeros((pad, LANES), f32)


def softmax_fast(groups, chans, slots, up, w_ref, p_ref):
    sums = [None] * (groups * HALF)
    for c in range(chans):
        for b in range(groups):
            row = c * slots + SUB * b
            centre = w_ref[pl.ds(row + 1, SUB), :]
            beyond = w_ref[pl.ds(row + (2 if up else 0), SUB), :]
            slope = (beyond - centre) * (1.0 / STEP)
            p = jnp.exp2(centre + slope)
            ratio = jnp.exp2(slope + slope)
            for m in range(HALF):
                k = b * HALF + m
                if m:
                    p = p * ratio
                p_ref[c * groups * HALF + k] = p
                sums[k] = p if sums[k] is None else sums[k] + p
    return sums


def softmax_slow(groups, chans, slots, up, w_ref, p_ref, labels, weights):
    sums, losses = [], jnp.zeros((SUB, LANES), f32)
    for b in range(groups):
        for m in range(HALF):
            k = b * HALF + m

            def score(c, b=b, m=m):
                row = c * slots + SUB * b
                centre = w_ref[pl.ds(row + 1, SUB), :]
                beyond = w_ref[pl.ds(row + (2 if up else 0), SUB), :]
                return centre + (beyond - centre) * ((2 * m + 1.0) / STEP)

            top = lax.fori_loop(1, chans, lambda c, t: jnp.maximum(t, score(c)), score(0))

            def take(c, carry, k=k, top=top, score=score):
                total, picked = carry
                shifted = score(c) - top
                p = jnp.exp2(shifted)
                p_ref[c * groups * HALF + k] = p
                return total + p, jnp.where(labels[k] == c, shifted, picked)

            zero = jnp.zeros((SUB, LANES), f32)
            total, picked = lax.fori_loop(0, chans, take, (zero, zero))
            sums.append(total)
            losses = losses - weights[k] * picked
    return sums, losses


def pixels(groups, chans, slots, load_labels, fast, w_ref, p_ref, g_ref, s_ref):
    count = groups * HALF
    g_ref[...] = jnp.zeros_like(g_ref)
    loss = jnp.zeros((SUB, LANES), f32)
    for up in (False, True):
        labels = [None] * count
        for m in range(HALF):
            for b in range(groups):
                labels[b * HALF + m] = load_labels(b, HALF + m if up else HALF - 1 - m)
        weights = [jnp.where(lab >= 0, 1.0, 0.0) for lab in labels]
        packed = [
            jnp.concatenate([labels[b * HALF + m] for b in range(groups)], axis=0).astype(jnp.int16)
            for m in range(HALF)
        ]

        @pl.when(fast)
        def _():
            sums = softmax_fast(groups, chans, slots, up, w_ref, p_ref)
            for k in range(count):
                s_ref[k] = sums[k]
            s_ref[count] = jnp.zeros((SUB, LANES), f32)

        @pl.when(jnp.logical_not(fast))
        def _():
            sums, losses = softmax_slow(groups, chans, slots, up, w_ref, p_ref, labels, weights)
            for k in range(count):
                s_ref[k] = sums[k]
            s_ref[count] = losses

        sums = [s_ref[k] for k in range(count)]
        extra = s_ref[count]
        scale = []
        for k in range(count):
            loss = loss + weights[k] * jnp.log(sums[k])
            scale.append(weights[k] / sums[k])
        picked = jnp.zeros((SUB, LANES), f32)
        for c in range(chans):
            tally = None
            for m in range(HALF):
                hit = jnp.where(packed[m] == jnp.int16(c), jnp.int16(1 + SUB * (2 * m + 1)), jnp.int16(0))
                tally = hit if tally is None else tally + hit
            tally = tally.astype(jnp.int32)
            for b in range(groups):
                total = run = None
                for m in reversed(range(HALF)):
                    g = p_ref[c * count + b * HALF + m] * scale[b * HALF + m]
                    total = g if total is None else total + g
                    run = total if run is None else run + total
                part = tally[b * SUB : b * SUB + SUB]
                ones = (part & (SUB - 1)).astype(f32)
                far = lax.shift_right_logical(part, 3).astype(f32) * (1.0 / STEP)
                centre = pl.ds(c * slots + 1 + SUB * b, SUB)
                beyond = pl.ds(c * slots + (2 if up else 0) + SUB * b, SUB)
                picked = picked + (ones - far) * w_ref[centre, :] + far * w_ref[beyond, :]
                out = (run + run - total) * (1.0 / STEP) - far
                g_ref[centre, :] += (total - ones) - out
                g_ref[beyond, :] += out
        loss = loss + LN2 * jnp.where(fast, -picked, extra)
    return loss


def narrow(g_ref, table):
    g = g_ref[...]
    hi = g.astype(bf16)
    low = (g - hi.astype(f32)).astype(bf16)
    return jnp.dot(jnp.concatenate([hi, low], axis=1), table, preferred_element_type=f32)


def inner_kernel(
    cols, chans, slots, groups, x_ref, own_ref, got_ref, table_ref, back_ref, lab_ref, mask_ref,
    acc_ref, loss_ref, stack_ref, floor_ref, w_ref, p_ref, g_ref, s_ref, h_ref,
):
    step = pl.program_id(0)

    @pl.when(step == 0)
    def _():
        h_ref[...] = x_ref[...]
        row = lax.axis_index("gy")
        top = jnp.where(row == 0, own_ref[0:chans, :], got_ref[chans : 2 * chans, :])
        last = row == lax.axis_size("gy") - 1
        bottom = jnp.where(last, own_ref[chans : 2 * chans, :], got_ref[0:chans, :])
        h_ref[pl.ds(0, chans, stride=slots), :] = top
        h_ref[pl.ds(groups * SUB + 1, chans, stride=slots), :] = bottom
        full = h_ref[...]
        floor_ref[0] = jnp.min(full) * STEP
        stack_ref[...] = stack3(full, cols)
        acc_ref[...] = jnp.zeros_like(acc_ref)
        loss_ref[...] = jnp.zeros_like(loss_ref)

    w_ref[...] = jnp.dot(stack_ref[...], table_ref[...], preferred_element_type=f32)
    lane = lax.broadcasted_iota(jnp.int32, (SUB, LANES), 1) + step * LANES
    inside = (lane >= HALF) & (lane < cols * PATCH - HALF)

    def load_labels(b, j):
        pick = pl.ds(b * SUB * PATCH + j, SUB, stride=PATCH)
        return jnp.where((mask_ref[pick, :] != 0) & inside, lab_ref[pick, :], -1)

    fast = floor_ref[0] >= FLOOR
    loss_ref[...] += pixels(groups, chans, slots, load_labels, fast, w_ref, p_ref, g_ref, s_ref)
    acc_ref[...] += narrow(g_ref, back_ref[...])


def edge_kernel(
    rows, cols, chans, slots, groups, floor_ref, stack_ref, acc_ref, loss_in_ref, sa_ref, sb_ref, ra_ref, rb_ref,
    va_ref, vb_ref, table_ref, fold_ref, back_ref, halo_ref, out_ref, v_ref, loss_ref, w_ref, p_ref, g_ref, s_ref,
):
    col = lax.axis_index("gx")
    row = lax.axis_index("gy")
    even = lax.rem(col, 2) == 0
    first, last = col == 0, col == lax.axis_size("gx") - 1
    n = chans * slots // LANES
    width = n * LANES

    def line(ref):
        return jnp.concatenate([ref[rows + r : rows + r + 1, :] for r in range(n)], axis=1)

    slot = lax.rem(lax.broadcasted_iota(jnp.int32, (1, width), 1), slots)

    def with_ends(mine, partner):
        top = jnp.where(row == 0, pltpu.roll(mine, width - 1, 1), pltpu.roll(partner, width - rows, 1))
        bottom = jnp.where(row == lax.axis_size("gy") - 1, pltpu.roll(mine, 1, 1), pltpu.roll(partner, rows, 1))
        return jnp.where(slot == 0, top, jnp.where(slot == rows + 1, bottom, mine))

    a = with_ends(line(ra_ref), line(va_ref))
    b = with_ends(line(rb_ref), line(vb_ref))
    sides = [jnp.where(even, b, a), jnp.where(even, a, b)]
    absent = [first, last]
    lows = jnp.float32(0.0)
    parts = []
    for side, gone in zip(sides, absent):
        side = jnp.where(gone, 0.0, side)
        lows = jnp.minimum(lows, jnp.min(side))
        parts += [part.astype(f32) for part in split3(side)]
    parts.append(jnp.zeros((16 - len(parts), width), f32))
    halo = jnp.concatenate(parts, axis=0).astype(bf16)
    table = table_ref[...]
    back = back_ref[...]
    depth = table.shape[0]
    zero = jnp.zeros_like(table)
    table = table + jnp.where(first, fold_ref[0:depth, :], zero) + jnp.where(last, fold_ref[depth : 2 * depth, :], zero)
    back = back + jnp.where(first, fold_ref[2 * depth : 3 * depth, :], zero)
    back = back + jnp.where(last, fold_ref[3 * depth : 4 * depth, :], zero)
    w_ref[...] = jnp.dot(stack_ref[...], table, preferred_element_type=f32) + lax.dot_general(
        halo, halo_ref[...], (((0,), (0,)), ((), ())), preferred_element_type=f32
    )
    lane = lax.broadcasted_iota(jnp.int32, (SUB, LANES), 1)

    def load_labels(b, j):
        pick = slice(b * SUB, b * SUB + SUB)
        strips = [
            jnp.where(first, -1.0, jnp.where(even, rb_ref[pick, :], ra_ref[pick, :])),
            jnp.where(even, sb_ref[pick, :], sa_ref[pick, :]),
            jnp.where(even, sa_ref[pick, :], sb_ref[pick, :]),
            jnp.where(last, -1.0, jnp.where(even, ra_ref[pick, :], rb_ref[pick, :])),
        ]
        out = jnp.full((SUB, LANES), -1.0, f32)
        for k, strip in enumerate(strips):
            shift = (k * HALF - j * HALF) % LANES
            moved = pltpu.roll(strip, shift, 1) if shift else strip
            out = jnp.where((lane >= k * HALF) & (lane < k * HALF + HALF), moved, out)
        return out.astype(jnp.int32)

    fast = jnp.minimum(lows * STEP, floor_ref[0]) >= FLOOR
    outside = (lane < HALF) | (lane >= 3 * HALF)
    loss = pixels(groups, chans, slots, load_labels, fast, w_ref, p_ref, g_ref, s_ref)
    loss_ref[...] = loss_in_ref[...] + jnp.where(outside, 0.0, loss)
    out_ref[...] = (acc_ref[...] + narrow(g_ref, back)) * (1.0 / STEP)
    v_ref[0:chans, :] = out_ref[pl.ds(0, chans, stride=slots), :]
    v_ref[chans : 2 * chans, :] = out_ref[pl.ds(rows + 1, chans, stride=slots), :]


def grad_kernel(
    rows, cols, chans, slots, f_ref, g_ref, own_ref, got_ref, loss_ref, count_ref, mine_ref, other_ref, sum_ref,
):
    row = lax.axis_index("gy")
    sum_ref[...] = g_ref[...]
    last = row == lax.axis_size("gy") - 1
    top = jnp.where(row == 0, own_ref[0:chans, :], got_ref[chans : 2 * chans, :])
    bottom = jnp.where(last, own_ref[chans : 2 * chans, :], got_ref[0:chans, :])
    sum_ref[pl.ds(1, chans, stride=slots), :] += top
    sum_ref[pl.ds(rows, chans, stride=slots), :] += bottom
    lane = lax.broadcasted_iota(jnp.int32, (chans, LANES), 1)
    share = LANES // cols
    tiles = []
    total = jnp.zeros((chans, LANES), f32)
    for k in range(0, rows, share):
        tile = None
        for r in range(share):
            piece = sum_ref[pl.ds(k + r + 1, chans, stride=slots), :]
            total = total + piece
            if r:
                piece = pltpu.roll(piece, r * cols, 1)
            tile = piece if tile is None else jnp.where(lane < r * cols, tile, piece)
        tiles.append(tile.astype(bf16))
    block = f_ref[...].reshape(rows * cols, f_ref.shape[2])
    out = jnp.dot(jnp.concatenate(tiles, axis=1), block, preferred_element_type=f32)
    total = jnp.where(lane < cols, total, 0.0)
    square = jnp.concatenate([total, jnp.zeros((LANES - chans, LANES), f32)], axis=0)
    bias = jnp.sum(square.T, axis=0, keepdims=True)
    at = lax.broadcasted_iota(jnp.int32, (SUB, LANES), 0)
    rest = jnp.where(at == 1, jnp.sum(loss_ref[...]), count_ref[0, 0].astype(f32))
    stats = jnp.where(at == 0, bias, jnp.where(at < 3, rest, 0.0))
    pieces = out.shape[1] // LANES // 2
    for k in range(pieces):
        low = out[:, k * LANES : k * LANES + LANES]
        high = out[:, (pieces + k) * LANES : (pieces + k + 1) * LANES]
        mine_ref[k * chans : k * chans + chans, :] = jnp.where(row == 0, low, high)
        other_ref[k * chans : k * chans + chans, :] = jnp.where(row == 0, high, low)
    mine_ref[pieces * chans :, :] = stats
    other_ref[pieces * chans :, :] = stats


def final_kernel(chans, y_ref, z_ref, loss_ref, weight_ref, bias_ref):
    pieces = y_ref.shape[0] // chans
    lower = lax.axis_index("gy") == 0
    stats = y_ref[pieces * chans :, :]
    total = stats[2:3, 0:1]
    for k in range(pieces):
        y = y_ref[k * chans : k * chans + chans, :]
        z = z_ref[k * chans : k * chans + chans, :]
        weight_ref[:, k * LANES : k * LANES + LANES] = jnp.where(lower, y, z) / total
        weight_ref[:, (pieces + k) * LANES : (pieces + k + 1) * LANES] = jnp.where(lower, z, y) / total
    loss_ref[...] = stats[1:2, 0:1] / total
    bias_ref[...] = stats[0:1, 0:chans] / total


def body(features, probe_weight, probe_bias, labels, valid_mask, valid_count):
    rows, cols, width = features.shape
    chans = probe_weight.shape[1]
    gx, gy = lax.axis_size("gx"), lax.axis_size("gy")
    if gy != 2 or rows % SUB or cols * PATCH % LANES or gx & (gx - 1):
        raise ValueError("unsupported tile")
    groups = rows // SUB
    slots = rows + SUB
    count = groups * HALF
    tiles = cols * PATCH // LANES
    tall = rows * PATCH
    depth = 2 * LANES
    inner, own, halo = column_tables(cols)

    def forward(table):
        out = np.zeros((depth, table.shape[1]), np.float32)
        for k in range(3):
            out[k * cols : k * cols + cols] = table
        return out

    def backward(table):
        out = np.zeros((table.shape[1] // LANES, 2, LANES, LANES), np.float32)
        out[:, :, :, :cols] = table.T.reshape(-1, 1, LANES, cols)
        return out.reshape(-1, LANES)

    lift, back = forward(inner), backward(inner)
    left, right = np.zeros_like(own), np.zeros_like(own)
    left[0], right[cols - 1] = halo
    fold = np.concatenate([forward(left), forward(right), backward(left), backward(right)])
    sides = np.zeros((16, LANES), np.float32)
    sides[0:3], sides[3:6] = halo[0], halo[1]
    ends = np.zeros((SUB, depth), np.float32)
    for k in range(3):
        ends[0, k * cols] = 1.0
        ends[1, k * cols + cols - 1] = 1.0
    lift, back, own_f, own_b, fold, sides, ends = (
        jnp.asarray(t, bf16) for t in (lift, back, forward(own), backward(own), fold, sides, ends)
    )

    per = 4
    shape = lambda *dims: jax.ShapeDtypeStruct(dims, f32)
    held = lambda *dims, kind=f32: pltpu.VMEM(dims, kind)
    here = lambda v: pltpu.with_memory_space_constraint(v, pltpu.VMEM)
    strip = -(-(rows + chans * slots // LANES) // SUB) * SUB
    tall_x = chans * slots
    x, edge, send_a, send_b, kept = pl.pallas_call(
        functools.partial(logits_kernel, rows, cols, chans, slots, per),
        in_specs=[ANY, VMEM, VMEM, ANY, ANY, VMEM],
        out_specs=[VMEM] * 5,
        out_shape=[
            held(tall_x, LANES), held(2 * chans, LANES), held(strip, LANES), held(strip, LANES),
            held(rows, cols, width, kind=bf16),
        ],
        scratch_shapes=[
            pltpu.VMEM((4, tall, LANES), jnp.int32),
            pltpu.SemaphoreType.DMA((rows // per,)),
            pltpu.SemaphoreType.DMA((4,)),
        ],
        compiler_params=ROOM,
        name="logits",
    )(features, probe_weight.T, probe_bias.reshape(1, chans), labels, valid_mask, ends)

    swap = lambda v: lax.ppermute(v, "gy", [(0, 1), (1, 0)])
    pairs = lambda at: [p for i in range(at, gx - 1, 2) for p in ((i, i + 1), (i + 1, i))]
    got = swap(edge)
    got_a = lax.ppermute(send_a, "gx", pairs(0))
    got_b = lax.ppermute(send_b, "gx", pairs(1))

    scratch = [
        pltpu.VMEM((tall_x, LANES), f32),
        pltpu.VMEM((chans * count, SUB, LANES), f32),
        pltpu.VMEM((tall_x, LANES), f32),
        pltpu.VMEM((count + 1, SUB, LANES), f32),
    ]
    column = pl.BlockSpec((tall, LANES), lambda t: (0, t))
    acc, loss, stack, floor = pl.pallas_call(
        functools.partial(inner_kernel, cols, chans, slots, groups),
        grid=(tiles,),
        in_specs=[
            VMEM, VMEM, VMEM,
            pl.BlockSpec((depth, LANES), lambda t: (0, t)), pl.BlockSpec((depth, LANES), lambda t: (t, 0)),
            column, column,
        ],
        out_specs=[VMEM, VMEM, VMEM, SMEM],
        out_shape=[held(tall_x, LANES), held(SUB, LANES), held(tall_x, depth, kind=bf16), shape(1)],
        scratch_shapes=scratch + [pltpu.VMEM((tall_x, LANES), f32)],
        cost_estimate=pl.CostEstimate(flops=2 * 10**9, bytes_accessed=4 * 10**6, transcendentals=10**6),
        compiler_params=ROOM,
        name="inner",
    )(here(x), here(edge), here(got), lift, back, labels, valid_mask)

    far_a, far_b = swap(got_a), swap(got_b)
    grad, spill, loss = pl.pallas_call(
        functools.partial(edge_kernel, rows, cols, chans, slots, groups),
        in_specs=[SMEM] + [VMEM] * 13,
        out_specs=[VMEM] * 3,
        out_shape=[held(tall_x, LANES), held(2 * chans, LANES), held(SUB, LANES)],
        scratch_shapes=scratch,
        compiler_params=ROOM,
        name="edge",
    )(
        floor, *(here(v) for v in (stack, acc, loss, send_a, send_b, got_a, got_b, far_a, far_b)),
        own_f, fold, own_b, sides,
    )

    got = swap(spill)
    pack = (chans * width // 2 // LANES + SUB, LANES)
    mine, other = pl.pallas_call(
        functools.partial(grad_kernel, rows, cols, chans, slots),
        in_specs=[VMEM] * 5 + [SMEM],
        out_specs=[VMEM] * 2,
        out_shape=[held(*pack)] * 2,
        scratch_shapes=[pltpu.VMEM((tall_x, LANES), f32)],
        compiler_params=ROOM,
        name="grad",
    )(*(here(v) for v in (kept, grad, spill, got, loss)), valid_count)

    total = mine + swap(other)
    step = 1
    while step < gx:
        total = total + lax.ppermute(total, "gx", [(i, i ^ step) for i in range(gx)])
        step *= 2
    loss, weight, bias = pl.pallas_call(
        functools.partial(final_kernel, chans),
        in_specs=[VMEM] * 2,
        out_specs=[VMEM] * 3,
        out_shape=[shape(1, 1), shape(chans, width), shape(1, chans)],
        compiler_params=ROOM,
        name="final",
    )(here(total), here(swap(total)))
    return loss.reshape(1), weight.T, bias.reshape(chans)


def solution(mesh):
    return jax.shard_map(
        body,
        mesh=mesh,
        in_specs=(
            P(("groups", "gy"), "gx", None),
            P(),
            P(),
            P(("groups", "gy"), "gx"),
            P(("groups", "gy"), "gx"),
            P(("groups", "gy"), "gx"),
        ),
        out_specs=(P("groups"), P("groups", None), P("groups")),
        check_vma=False,
    )
```

```python
import functools
import math

import jax
import jax.numpy as jnp
import numpy as np
from jax import lax
from jax.experimental import pallas as pl
from jax.experimental.pallas import tpu as pltpu
from jax.sharding import PartitionSpec as P

PATCH = 14
HALF = PATCH // 2
STEP = 2 * PATCH
LANES = 128
SUB = 8
LOG2E = 1.0 / math.log(2.0)
LN2 = math.log(2.0)
FLOOR = -100.0
f32 = jnp.float32
bf16 = jnp.bfloat16
VMEM = pl.BlockSpec(memory_space=pltpu.VMEM)
ANY = pl.BlockSpec(memory_space=pl.ANY)
ROOM = pltpu.CompilerParams(vmem_limit_bytes=16 * 2**20)
SMEM = pl.BlockSpec(memory_space=pltpu.SMEM)


def whole(shape):
    return pl.BlockSpec(shape, lambda *ids: (0,) * len(shape))


def column_tables(cols):
    near = np.array([STEP - abs(2 * j + 1 - PATCH) for j in range(PATCH)])
    far = STEP - near
    inner = np.zeros((cols, cols * PATCH), np.float32)
    for q in range(cols * PATCH):
        i, j = divmod(q, PATCH)
        inner[i, q] += near[j]
        k = i - 1 if j < HALF else i + 1
        if 0 <= k < cols:
            inner[k, q] += far[j]
    own = np.zeros((cols, LANES), np.float32)
    halo = np.zeros((2, LANES), np.float32)
    for lane in range(4 * HALF):
        side, k = divmod(lane, HALF)
        j = k + HALF if side in (0, 2) else k
        edge = 0 if side < 2 else cols - 1
        outside = side in (0, 3)
        own[edge, lane] = far[j] if outside else near[j]
        halo[int(side > 1), lane] = near[j] if outside else far[j]
    return inner, own, halo


def split3(x):
    hi = x.astype(bf16)
    rest = x - hi.astype(f32)
    mid = rest.astype(bf16)
    return hi, mid, (rest - mid.astype(f32)).astype(bf16)


def stack3(x, cols):
    lane = lax.broadcasted_iota(jnp.int32, x.shape, 1)
    hi, mid, low = (part.astype(f32) for part in split3(jnp.where(lane < cols, x, 0.0)))
    first = jnp.where(lane < cols, hi, pltpu.roll(mid, cols, 1))
    return jnp.concatenate([first.astype(bf16), low.astype(bf16)], axis=1)


def logits_kernel(
    rows, cols, chans, slots, per, f_ref, w_ref, bias_ref, lab_ref, mask_ref, sel_ref,
    x_ref, e_ref, sa_ref, sb_ref, keep_ref, strip_ref, wv_ref, bv_ref, selv_ref, f_sem, s_sem,
):
    steps = rows // per
    tail = lab_ref.shape[1] - LANES
    loads = [
        pltpu.make_async_copy(f_ref.at[pl.ds(k * per, per)], keep_ref.at[pl.ds(k * per, per)], f_sem.at[k])
        for k in range(steps)
    ]
    strips = [
        pltpu.make_async_copy(ref.at[:, pl.ds(at, LANES)], strip_ref.at[k], s_sem.at[k])
        for k, (ref, at) in enumerate(((lab_ref, 0), (mask_ref, 0), (lab_ref, tail), (mask_ref, tail)))
    ]
    small = [
        pltpu.make_async_copy(a, b, s_sem.at[len(strips) + k])
        for k, (a, b) in enumerate(((w_ref, wv_ref), (bias_ref, bv_ref), (sel_ref, selv_ref)))
    ]
    for copy in strips + small + loads:
        copy.start()
    x_ref[...] = jnp.zeros_like(x_ref)
    for copy in small:
        copy.wait()
    bias = jnp.concatenate([bv_ref[...], jnp.zeros((1, LANES - chans), f32)], axis=1)
    bias = jnp.broadcast_to(bias, (LANES, LANES)).T[0:chans, :]
    bias = jnp.concatenate([bias] * (per * cols // LANES), axis=1)
    at = lax.broadcasted_iota(jnp.int32, (SUB, LANES), 1)
    even = lax.rem(lax.axis_index("gx"), 2) == 0
    for copy in strips:
        copy.wait()
    for b in range(rows // SUB):
        left = jnp.full((SUB, LANES), -1.0, f32)
        right = left
        for j in range(PATCH):
            pick = pl.ds(b * SUB * PATCH + j, SUB, stride=PATCH)
            here = (at >= j * HALF) & (at < j * HALF + HALF)
            lab = jnp.where(strip_ref[1, pick, :] != 0, strip_ref[0, pick, :], -1).astype(f32)
            shift = j * HALF
            left = jnp.where(here, pltpu.roll(lab, shift, 1) if shift else lab, left)
            lab = jnp.where(strip_ref[3, pick, :] != 0, strip_ref[2, pick, :], -1).astype(f32)
            right = jnp.where(here, pltpu.roll(lab, (shift + HALF) % LANES, 1), right)
        sa_ref[b * SUB : b * SUB + SUB, :] = jnp.where(even, right, left)
        sb_ref[b * SUB : b * SUB + SUB, :] = jnp.where(even, left, right)
    lane = lax.broadcasted_iota(jnp.int32, (chans, LANES), 1)
    for step in range(steps):
        loads[step].wait()
        block = keep_ref[step * per : step * per + per].reshape(per * cols, f_ref.shape[2])
        score = lax.dot_general(wv_ref[...], block, (((1,), (1,)), ((), ())), preferred_element_type=f32)
        score = score + bias
        score = (score - jnp.max(score, axis=0, keepdims=True)) * (LOG2E / STEP)
        for k in range(per):
            off = k * cols
            tile = score[:, off // LANES * LANES : off // LANES * LANES + LANES]
            if off % LANES:
                tile = pltpu.roll(tile, LANES - off % LANES, 1)
            tile = jnp.where(lane < cols, tile, 0.0)
            x_ref[pl.ds(step * per + k + 1, chans, stride=slots), :] = tile
            if step == 0 and k == 0:
                e_ref[0:chans, :] = tile
            if step == steps - 1 and k == per - 1:
                e_ref[chans : 2 * chans, :] = tile
    edges = lax.dot_general(
        selv_ref[...], stack3(x_ref[...], cols), (((1,), (1,)), ((), ())), preferred_element_type=f32
    )
    n = chans * slots // LANES
    for r in range(n):
        part = edges[:, r * LANES : r * LANES + LANES]
        sa_ref[rows + r : rows + r + 1, :] = jnp.where(even, part[1:2], part[0:1])
        sb_ref[rows + r : rows + r + 1, :] = jnp.where(even, part[0:1], part[1:2])
    pad = sa_ref.shape[0] - rows - n
    if pad:
        sa_ref[rows + n :, :] = jnp.zeros((pad, LANES), f32)
        sb_ref[rows + n :, :] = jnp.zeros((pad, LANES), f32)


def softmax_fast(groups, chans, slots, w_ref, p_ref):
    sums = [None] * (2 * groups * HALF)
    for c in range(chans):
        for b in range(groups):
            row = c * slots + SUB * b
            centre = w_ref[row + 1 : row + 1 + SUB, :]
            for up in range(2):
                beyond = w_ref[row + 2 * up : row + 2 * up + SUB, :]
                slope = (beyond - centre) * (1.0 / STEP)
                p = jnp.exp2(centre + slope)
                ratio = jnp.exp2(slope + slope)
                for m in range(HALF):
                    k = (up * groups + b) * HALF + m
                    if m:
                        p = p * ratio
                    p_ref[c * len(sums) + k] = p
                    sums[k] = p if sums[k] is None else sums[k] + p
    return sums


def softmax_slow(groups, chans, slots, w_ref, p_ref, labels, weights):
    count = len(labels)
    sums, losses = [], jnp.zeros((SUB, LANES), f32)
    for k in range(count):
        up, b, m = k // (groups * HALF), k // HALF % groups, k % HALF

        def score(c, up=up, b=b, m=m):
            row = c * slots + SUB * b
            centre = w_ref[pl.ds(row + 1, SUB), :]
            beyond = w_ref[pl.ds(row + 2 * up, SUB), :]
            return centre + (beyond - centre) * ((2 * m + 1.0) / STEP)

        top = lax.fori_loop(1, chans, lambda c, t, score=score: jnp.maximum(t, score(c)), score(0))

        def take(c, carry, k=k, top=top, score=score):
            total, picked = carry
            shifted = score(c) - top
            p = jnp.exp2(shifted)
            p_ref[c * count + k] = p
            return total + p, jnp.where(labels[k] == c, shifted, picked)

        zero = jnp.zeros((SUB, LANES), f32)
        total, picked = lax.fori_loop(0, chans, take, (zero, zero))
        sums.append(total)
        losses = losses - weights[k] * picked
    return sums, losses


def pixels(groups, chans, slots, load_labels, fast, w_ref, p_ref, s_ref, lhs_ref):
    count = 2 * groups * HALF
    labels = []
    for up in range(2):
        for b in range(groups):
            labels += [load_labels(b, HALF + m if up else HALF - 1 - m) for m in range(HALF)]
    weights = [jnp.where(lab >= 0, 1.0, 0.0) for lab in labels]

    @pl.when(fast)
    def _():
        sums = softmax_fast(groups, chans, slots, w_ref, p_ref)
        for k in range(count):
            s_ref[k] = sums[k]
        s_ref[count] = jnp.zeros((SUB, LANES), f32)

    @pl.when(jnp.logical_not(fast))
    def _():
        sums, losses = softmax_slow(groups, chans, slots, w_ref, p_ref, labels, weights)
        for k in range(count):
            s_ref[k] = sums[k]
        s_ref[count] = losses

    loss = jnp.zeros((SUB, LANES), f32)
    scale = []
    for k in range(count):
        total = s_ref[k]
        loss = loss + weights[k] * jnp.log(total)
        scale.append(weights[k] / total)
    packed = [
        jnp.concatenate([labels[(up * groups + b) * HALF + m] for b in range(groups)], axis=0).astype(f32).astype(bf16)
        for up in range(2)
        for m in range(HALF)
    ]
    half = jnp.asarray(0.5, bf16)
    near = jnp.zeros((SUB, LANES), f32)
    away = jnp.zeros((SUB, LANES), f32)
    tall = groups * SUB
    for c in range(chans):
        tally, hits = None, []
        for up in range(2):
            total = run = None
            for m in reversed(range(HALF)):
                hit = jnp.where(packed[up * HALF + m] == jnp.asarray(c, bf16), jnp.asarray(1, bf16), jnp.asarray(0, bf16))
                total = hit if total is None else total + hit
                if m:
                    run = total if run is None else run + total
            hits.append(run + total * half)
            tally = total if tally is None else tally + total
        hits = [v.astype(f32) for v in [tally] + hits]
        parts = [[], [], []]
        for b in range(groups):
            whole_sum = None
            for up in range(2):
                total = run = None
                for m in reversed(range(HALF)):
                    k = (up * groups + b) * HALF + m
                    g = p_ref[c * count + k] * scale[k]
                    total = g if total is None else total + g
                    if m:
                        run = total if run is None else run + total
                parts[up + 1].append(run + total * 0.5)
                whole_sum = total if whole_sum is None else whole_sum + total
            parts[0].append(whole_sum)
            row = c * slots + SUB * b
            centre = w_ref[row + 1 : row + 1 + SUB, :]
            mine = [v[b * SUB : b * SUB + SUB] for v in hits]
            near = near + mine[0] * centre
            away = away + mine[1] * (w_ref[row : row + SUB, :] - centre)
            away = away + mine[2] * (w_ref[row + 2 : row + 2 + SUB, :] - centre)
        for kind in range(3):
            g = jnp.concatenate(parts[kind], axis=0) - hits[kind]
            hi = g.astype(bf16)
            at = (kind * chans + c) * tall
            lhs_ref[at : at + tall, 0:LANES] = hi
            lhs_ref[at : at + tall, LANES:] = (g - hi.astype(f32)).astype(bf16)
    picked = near + away * (1.0 / PATCH)
    return loss + LN2 * jnp.where(fast, -picked, s_ref[count])


def to_slots(groups, chans, slots, sums_ref, out_ref):
    out_ref[...] = jnp.zeros_like(out_ref)
    for c in range(chans):
        for b in range(groups):
            total, low, high = (
                sums_ref[((kind * chans + c) * groups + b) * SUB : ((kind * chans + c) * groups + b + 1) * SUB, :]
                for kind in range(3)
            )
            low = low * (1.0 / PATCH)
            high = high * (1.0 / PATCH)
            row = c * slots + SUB * b
            out_ref[row : row + SUB, :] += low
            out_ref[row + 1 : row + 1 + SUB, :] += total - low - high
            out_ref[row + 2 : row + 2 + SUB, :] += high


def inner_kernel(
    cols, chans, slots, groups, first, tiles, x_ref, own_ref, got_ref, table_ref, next_ref, back_ref, lab_ref, mask_ref,
    *rest,
):
    if first:
        acc_ref, loss_ref, stack_ref, floor_ref, w_ref, p_ref, s_ref, lhs_ref = rest
        begin = 0
    else:
        acc_in_ref, loss_in_ref, stack_ref, floor_ref, acc_ref, loss_ref, w_ref, p_ref, s_ref, lhs_ref, sum_ref = rest
        begin = tiles - pl.num_programs(0)
    step = pl.program_id(0)
    now = lax.rem(step, 2)

    @pl.when(step == 0)
    def _():
        if first:
            w_ref[0] = x_ref[...]
            row = lax.axis_index("gy")
            top = jnp.where(row == 0, own_ref[0:chans, :], got_ref[chans : 2 * chans, :])
            last = row == lax.axis_size("gy") - 1
            bottom = jnp.where(last, own_ref[chans : 2 * chans, :], got_ref[0:chans, :])
            w_ref[0, pl.ds(0, chans, stride=slots), :] = top
            w_ref[0, pl.ds(groups * SUB + 1, chans, stride=slots), :] = bottom
            full = w_ref[0]
            floor_ref[0] = jnp.min(full) * STEP
            stack_ref[...] = stack3(full, cols)
            acc_ref[...] = jnp.zeros_like(acc_ref)
            loss_ref[...] = jnp.zeros_like(loss_ref)
        else:
            sum_ref[...] = acc_in_ref[...]
            loss_ref[...] = loss_in_ref[...]
        w_ref[0] = jnp.dot(stack_ref[...], table_ref[...], preferred_element_type=f32)

    sums = acc_ref if first else sum_ref
    lane = lax.broadcasted_iota(jnp.int32, (SUB, LANES), 1) + (step + begin) * LANES
    inside = (lane >= HALF) & (lane < cols * PATCH - HALF)

    def load_labels(b, j):
        pick = pl.ds(b * SUB * PATCH + j, SUB, stride=PATCH)
        return jnp.where((mask_ref[pick, :] != 0) & inside, lab_ref[pick, :], -1)

    fast = floor_ref[0] >= FLOOR
    loss_ref[...] += pixels(groups, chans, slots, load_labels, fast, w_ref.at[now], p_ref, s_ref, lhs_ref)
    w_ref[1 - now] = jnp.dot(stack_ref[...], next_ref[...], preferred_element_type=f32)
    sums[...] += jnp.dot(lhs_ref[...], back_ref[...], preferred_element_type=f32)
    if not first:

        @pl.when(step == pl.num_programs(0) - 1)
        def _():
            to_slots(groups, chans, slots, sum_ref, acc_ref)


def edge_kernel(
    rows, cols, chans, slots, groups, floor_ref, stack_ref, acc_ref, loss_in_ref, sa_ref, sb_ref, ra_ref, rb_ref,
    v_in_ref, table_ref, fold_ref, back_ref, halo_ref, out_ref, v_ref, loss_ref, w_ref, p_ref, s_ref, lhs_ref, sum_ref, more_ref,
):
    col = lax.axis_index("gx")
    row = lax.axis_index("gy")
    even = lax.rem(col, 2) == 0
    first, last = col == 0, col == lax.axis_size("gx") - 1
    n = chans * slots // LANES
    width = n * LANES

    def line(ref, at=0):
        return jnp.concatenate([ref[at + rows + r : at + rows + r + 1, :] for r in range(n)], axis=1)

    slot = lax.rem(lax.broadcasted_iota(jnp.int32, (1, width), 1), slots)

    def with_ends(mine, partner):
        top = jnp.where(row == 0, pltpu.roll(mine, width - 1, 1), pltpu.roll(partner, width - rows, 1))
        bottom = jnp.where(row == lax.axis_size("gy") - 1, pltpu.roll(mine, 1, 1), pltpu.roll(partner, rows, 1))
        return jnp.where(slot == 0, top, jnp.where(slot == rows + 1, bottom, mine))

    a = with_ends(line(ra_ref), line(v_in_ref))
    b = with_ends(line(rb_ref), line(v_in_ref, ra_ref.shape[0]))
    sides = [jnp.where(even, b, a), jnp.where(even, a, b)]
    absent = [first, last]
    lows = jnp.float32(0.0)
    parts = []
    for side, gone in zip(sides, absent):
        side = jnp.where(gone, 0.0, side)
        lows = jnp.minimum(lows, jnp.min(side))
        parts += [part.astype(f32) for part in split3(side)]
    parts.append(jnp.zeros((16 - len(parts), width), f32))
    halo = jnp.concatenate(parts, axis=0).astype(bf16)
    table = table_ref[...]
    back = back_ref[...]
    depth = table.shape[0]
    zero = jnp.zeros_like(table)
    table = table + jnp.where(first, fold_ref[0:depth, :], zero) + jnp.where(last, fold_ref[depth : 2 * depth, :], zero)
    back = back + jnp.where(first, fold_ref[2 * depth : 3 * depth, :], zero)
    back = back + jnp.where(last, fold_ref[3 * depth : 4 * depth, :], zero)
    w_ref[...] = jnp.dot(stack_ref[...], table, preferred_element_type=f32) + lax.dot_general(
        halo, halo_ref[...], (((0,), (0,)), ((), ())), preferred_element_type=f32
    )
    lane = lax.broadcasted_iota(jnp.int32, (SUB, LANES), 1)

    def load_labels(b, j):
        pick = slice(b * SUB, b * SUB + SUB)
        strips = [
            jnp.where(first, -1.0, jnp.where(even, rb_ref[pick, :], ra_ref[pick, :])),
            jnp.where(even, sb_ref[pick, :], sa_ref[pick, :]),
            jnp.where(even, sa_ref[pick, :], sb_ref[pick, :]),
            jnp.where(last, -1.0, jnp.where(even, ra_ref[pick, :], rb_ref[pick, :])),
        ]
        out = jnp.full((SUB, LANES), -1.0, f32)
        for k, strip in enumerate(strips):
            shift = (k * HALF - j * HALF) % LANES
            moved = pltpu.roll(strip, shift, 1) if shift else strip
            out = jnp.where((lane >= k * HALF) & (lane < k * HALF + HALF), moved, out)
        return out.astype(jnp.int32)

    fast = jnp.minimum(lows * STEP, floor_ref[0]) >= FLOOR
    outside = (lane < HALF) | (lane >= 3 * HALF)
    loss = pixels(groups, chans, slots, load_labels, fast, w_ref, p_ref, s_ref, lhs_ref)
    loss_ref[...] = loss_in_ref[...] + jnp.where(outside, 0.0, loss)
    sum_ref[...] = jnp.dot(lhs_ref[...], back, preferred_element_type=f32)
    to_slots(groups, chans, slots, sum_ref, more_ref)
    out_ref[...] = (acc_ref[...] + more_ref[...]) * (1.0 / STEP)
    v_ref[0:chans, :] = out_ref[pl.ds(0, chans, stride=slots), :]
    v_ref[chans : 2 * chans, :] = out_ref[pl.ds(rows + 1, chans, stride=slots), :]


def grad_kernel(
    rows, cols, chans, slots, f_ref, g_ref, own_ref, got_ref, loss_ref, count_ref, mine_ref, other_ref, sum_ref,
):
    row = lax.axis_index("gy")
    sum_ref[...] = g_ref[...]
    last = row == lax.axis_size("gy") - 1
    top = jnp.where(row == 0, own_ref[0:chans, :], got_ref[chans : 2 * chans, :])
    bottom = jnp.where(last, own_ref[chans : 2 * chans, :], got_ref[0:chans, :])
    sum_ref[pl.ds(1, chans, stride=slots), :] += top
    sum_ref[pl.ds(rows, chans, stride=slots), :] += bottom
    lane = lax.broadcasted_iota(jnp.int32, (chans, LANES), 1)
    share = LANES // cols
    tiles = []
    total = jnp.zeros((chans, LANES), f32)
    for k in range(0, rows, share):
        tile = None
        for r in range(share):
            piece = sum_ref[pl.ds(k + r + 1, chans, stride=slots), :]
            total = total + piece
            if r:
                piece = pltpu.roll(piece, r * cols, 1)
            tile = piece if tile is None else jnp.where(lane < r * cols, tile, piece)
        tiles.append(tile.astype(bf16))
    block = f_ref[...].reshape(rows * cols, f_ref.shape[2])
    out = jnp.dot(jnp.concatenate(tiles, axis=1), block, preferred_element_type=f32)
    total = jnp.where(lane < cols, total, 0.0)
    square = jnp.concatenate([total, jnp.zeros((LANES - chans, LANES), f32)], axis=0)
    bias = jnp.sum(square.T, axis=0, keepdims=True)
    at = lax.broadcasted_iota(jnp.int32, (SUB, LANES), 0)
    rest = jnp.where(at == 1, jnp.sum(loss_ref[...]), count_ref[0, 0].astype(f32))
    stats = jnp.where(at == 0, bias, jnp.where(at < 3, rest, 0.0))
    pieces = out.shape[1] // LANES // 2
    for k in range(pieces):
        low = out[:, k * LANES : k * LANES + LANES]
        high = out[:, (pieces + k) * LANES : (pieces + k + 1) * LANES]
        mine_ref[k * chans : k * chans + chans, :] = jnp.where(row == 0, low, high)
        other_ref[k * chans : k * chans + chans, :] = jnp.where(row == 0, high, low)
    mine_ref[pieces * chans :, :] = stats
    other_ref[pieces * chans :, :] = stats


def final_kernel(chans, y_ref, z_ref, loss_ref, weight_ref, bias_ref):
    pieces = y_ref.shape[0] // chans
    lower = lax.axis_index("gy") == 0
    stats = y_ref[pieces * chans :, :]
    total = stats[2:3, 0:1]
    for k in range(pieces):
        y = y_ref[k * chans : k * chans + chans, :]
        z = z_ref[k * chans : k * chans + chans, :]
        weight_ref[:, k * LANES : k * LANES + LANES] = jnp.where(lower, y, z) / total
        weight_ref[:, (pieces + k) * LANES : (pieces + k + 1) * LANES] = jnp.where(lower, z, y) / total
    loss_ref[...] = stats[1:2, 0:1] / total
    bias_ref[...] = stats[0:1, 0:chans] / total


def body(features, probe_weight, probe_bias, labels, valid_mask, valid_count):
    rows, cols, width = features.shape
    chans = probe_weight.shape[1]
    gx, gy = lax.axis_size("gx"), lax.axis_size("gy")
    if gy != 2 or rows % SUB or cols * PATCH % LANES or gx & (gx - 1):
        raise ValueError("unsupported tile")
    groups = rows // SUB
    slots = rows + SUB
    count = groups * HALF
    tiles = cols * PATCH // LANES
    tall = rows * PATCH
    depth = 2 * LANES
    inner, own, halo = column_tables(cols)

    def forward(table):
        out = np.zeros((depth, table.shape[1]), np.float32)
        for k in range(3):
            out[k * cols : k * cols + cols] = table
        return out

    def backward(table):
        out = np.zeros((table.shape[1] // LANES, 2, LANES, LANES), np.float32)
        out[:, :, :, :cols] = table.T.reshape(-1, 1, LANES, cols)
        return out.reshape(-1, LANES)

    lift, back = forward(inner), backward(inner)
    left, right = np.zeros_like(own), np.zeros_like(own)
    left[0], right[cols - 1] = halo
    fold = np.concatenate([forward(left), forward(right), backward(left), backward(right)])
    sides = np.zeros((16, LANES), np.float32)
    sides[0:3], sides[3:6] = halo[0], halo[1]
    ends = np.zeros((SUB, depth), np.float32)
    for k in range(3):
        ends[0, k * cols] = 1.0
        ends[1, k * cols + cols - 1] = 1.0
    lift, back, own_f, own_b, fold, sides, ends = (
        jnp.asarray(t, bf16) for t in (lift, back, forward(own), backward(own), fold, sides, ends)
    )

    per = 4
    shape = lambda *dims: jax.ShapeDtypeStruct(dims, f32)
    held = lambda *dims, kind=f32: pltpu.VMEM(dims, kind)
    far = lambda v: pltpu.with_memory_space_constraint(v, pltpu.HBM)
    here = lambda v: pltpu.with_memory_space_constraint(v, pltpu.VMEM)
    strip = -(-(rows + chans * slots // LANES) // SUB) * SUB
    tall_x = chans * slots
    x, edge, send_a, send_b, kept = pl.pallas_call(
        functools.partial(logits_kernel, rows, cols, chans, slots, per),
        in_specs=[ANY] * 6,
        out_specs=[VMEM] * 5,
        out_shape=[
            held(tall_x, LANES), held(2 * chans, LANES), held(strip, LANES), held(strip, LANES),
            held(rows, cols, width, kind=bf16),
        ],
        scratch_shapes=[
            pltpu.VMEM((4, tall, LANES), jnp.int32),
            pltpu.VMEM((chans, width), bf16),
            pltpu.VMEM((1, chans), f32),
            pltpu.VMEM((SUB, depth), bf16),
            pltpu.SemaphoreType.DMA((rows // per,)),
            pltpu.SemaphoreType.DMA((7,)),
        ],
        compiler_params=ROOM,
        name="logits",
    )(*(far(v) for v in (features, probe_weight.T, probe_bias.reshape(1, chans), labels, valid_mask, ends)))

    swap = lambda v: lax.ppermute(v, "gy", [(0, 1), (1, 0)])
    pairs = lambda at: [p for i in range(at, gx - 1, 2) for p in ((i, i + 1), (i + 1, i))]
    got = swap(edge)
    got_a = lax.ppermute(send_a, "gx", pairs(0))
    got_b = lax.ppermute(send_b, "gx", pairs(1))

    scratch = [
        pltpu.VMEM((2 * chans * count, SUB, LANES), f32),
        pltpu.VMEM((2 * count + 1, SUB, LANES), f32),
        pltpu.VMEM((3 * chans * rows, 2 * LANES), bf16),
    ]
    sums = (3 * chans * rows, LANES)

    def inner_call(first, *args):
        begin, steps = (0, tiles // 2 + 1) if first else (tiles // 2 + 1, tiles - tiles // 2 - 1)
        column = pl.BlockSpec((tall, LANES), lambda t: (0, t + begin))
        outs = [held(*sums), held(SUB, LANES)]
        if first:
            outs += [held(tall_x, depth, kind=bf16), shape(1)]
        else:
            outs[0] = held(tall_x, LANES)
        return pl.pallas_call(
            functools.partial(inner_kernel, cols, chans, slots, groups, first, tiles),
            grid=(steps,),
            in_specs=[
                VMEM, VMEM, VMEM,
                pl.BlockSpec((depth, LANES), lambda t: (0, t + begin)),
                pl.BlockSpec((depth, LANES), lambda t: (0, jnp.minimum(t + begin + 1, tiles - 1))),
                pl.BlockSpec((depth, LANES), lambda t: (t + begin, 0)),
                column, column,
            ] + ([] if first else [VMEM, VMEM, VMEM, SMEM]),
            out_specs=[VMEM, VMEM, VMEM, SMEM] if first else [VMEM, VMEM],
            out_shape=outs,
            scratch_shapes=[pltpu.VMEM((2, tall_x, LANES), f32)] + scratch + ([] if first else [pltpu.VMEM(sums, f32)]),
            cost_estimate=pl.CostEstimate(flops=2 * 10**9, bytes_accessed=4 * 10**6, transcendentals=10**6),
            compiler_params=ROOM,
            name="inner_head" if first else "inner_tail",
        )(*args)

    base = (here(x), here(edge), here(got), lift, lift, back, labels, valid_mask)
    acc, loss, stack, floor = inner_call(True, *base)
    got_a, got_b, acc = lax.optimization_barrier((got_a, got_b, acc))
    corners = swap(jnp.concatenate([got_a, got_b]))
    acc, loss = inner_call(False, *base, here(acc), here(loss), here(stack), floor)
    grad, spill, loss = pl.pallas_call(
        functools.partial(edge_kernel, rows, cols, chans, slots, groups),
        in_specs=[SMEM] + [VMEM] * 12,
        out_specs=[VMEM] * 3,
        out_shape=[held(tall_x, LANES), held(2 * chans, LANES), held(SUB, LANES)],
        scratch_shapes=[pltpu.VMEM((tall_x, LANES), f32)] + scratch + [pltpu.VMEM(sums, f32), pltpu.VMEM((tall_x, LANES), f32)],
        compiler_params=ROOM,
        name="edge",
    )(
        floor, *(here(v) for v in (stack, acc, loss, send_a, send_b, got_a, got_b, corners)),
        own_f, fold, own_b, sides,
    )

    got = swap(spill)
    pack = (chans * width // 2 // LANES + SUB, LANES)
    mine, other = pl.pallas_call(
        functools.partial(grad_kernel, rows, cols, chans, slots),
        in_specs=[VMEM] * 5 + [SMEM],
        out_specs=[VMEM] * 2,
        out_shape=[held(*pack)] * 2,
        scratch_shapes=[pltpu.VMEM((tall_x, LANES), f32)],
        compiler_params=ROOM,
        name="grad",
    )(*(here(v) for v in (kept, grad, spill, got, loss)), valid_count)

    total = mine + swap(other)
    step = 1
    while step < gx:
        total = total + lax.ppermute(total, "gx", [(i, i ^ step) for i in range(gx)])
        step *= 2
    loss, weight, bias = pl.pallas_call(
        functools.partial(final_kernel, chans),
        in_specs=[VMEM] * 2,
        out_specs=[VMEM] * 3,
        out_shape=[shape(1, 1), shape(chans, width), shape(1, chans)],
        compiler_params=ROOM,
        name="final",
    )(here(total), here(swap(total)))
    return loss.reshape(1), weight.T, bias.reshape(chans)


def solution(mesh):
    return jax.shard_map(
        body,
        mesh=mesh,
        in_specs=(
            P(("groups", "gy"), "gx", None),
            P(),
            P(),
            P(("groups", "gy"), "gx"),
            P(("groups", "gy"), "gx"),
            P(("groups", "gy"), "gx"),
        ),
        out_specs=(P("groups"), P("groups", None), P("groups")),
        check_vma=False,
    )
```

```python
import functools
import math

import jax
import jax.numpy as jnp
import numpy as np
from jax import lax
from jax.experimental import pallas as pl
from jax.experimental.pallas import tpu as pltpu
from jax.sharding import PartitionSpec as P

PATCH = 14
HALF = PATCH // 2
STEP = 2 * PATCH
LANES = 128
SUB = 8
LOG2E = 1.0 / math.log(2.0)
LN2 = math.log(2.0)
FLOOR = -100.0
f32 = jnp.float32
bf16 = jnp.bfloat16
VMEM = pl.BlockSpec(memory_space=pltpu.VMEM)
ANY = pl.BlockSpec(memory_space=pl.ANY)
ROOM = pltpu.CompilerParams(vmem_limit_bytes=16 * 2**20)
SMEM = pl.BlockSpec(memory_space=pltpu.SMEM)


def whole(shape):
    return pl.BlockSpec(shape, lambda *ids: (0,) * len(shape))


def column_tables(cols):
    tables = np.zeros((2, cols + 1, cols * PATCH), np.float32)
    for q in range(cols * PATCH):
        i, k = divmod((q if q >= HALF else q + cols * PATCH) - HALF, PATCH)
        far = 2 * k + 1
        for end in range(2):
            if end and i == cols - 1:
                tables[end, i + (k >= HALF), q] = STEP
            else:
                tables[end, i, q] = STEP - far
                tables[end, i + 1, q] = far
    return tables


def split3(x):
    hi = x.astype(bf16)
    rest = x - hi.astype(f32)
    mid = rest.astype(bf16)
    return hi, mid, (rest - mid.astype(f32)).astype(bf16)


def stack3(x):
    cols = LANES // 2
    lane = lax.broadcasted_iota(jnp.int32, x.shape, 1)
    hi, mid, low = (part.astype(f32) for part in split3(x))
    first = jnp.where(lane < cols, hi, pltpu.roll(mid, cols, 1))
    second = jnp.where(lane == cols + 1, pltpu.roll(mid, 1, 1), pltpu.roll(low, 2, 1))
    second = jnp.where(lane == cols, hi, jnp.where(lane < cols + 3, second, 0.0))
    second = jnp.where(lane < cols, low, second)
    return jnp.concatenate([first.astype(bf16), second.astype(bf16)], axis=1)


def pack_kernel(rows, f_ref, lab_ref, mask_ref, out_ref, head_ref, f_vmem, l_vmem, h_vmem, sem):
    width = f_vmem.shape[2]
    tiles = head_ref.shape[0] // SUB
    copies = [
        pltpu.make_async_copy(lab_ref.at[:, pl.ds(0, LANES)], l_vmem.at[0], sem.at[0]),
        pltpu.make_async_copy(mask_ref.at[:, pl.ds(0, LANES)], l_vmem.at[1], sem.at[1]),
        pltpu.make_async_copy(f_ref.at[:, pl.ds(0, SUB)], f_vmem, sem.at[2]),
        pltpu.make_async_copy(lab_ref.at[pl.ds(0, SUB)], h_vmem.at[0], sem.at[3]),
        pltpu.make_async_copy(mask_ref.at[pl.ds(0, SUB)], h_vmem.at[1], sem.at[4]),
    ]
    for copy in copies:
        copy.start()
    at = lax.broadcasted_iota(jnp.int32, (SUB, LANES), 1)
    for copy in copies:
        copy.wait()
    for b in range(rows // SUB):
        strip = jnp.full((SUB, LANES), -1.0, f32)
        for j in range(PATCH):
            pick = pl.ds(b * SUB * PATCH + j, SUB, stride=PATCH)
            lab = jnp.where(l_vmem[1, pick, :] != 0, l_vmem[0, pick, :], -1).astype(f32)
            here = (at >= j * HALF) & (at < j * HALF + HALF)
            strip = jnp.where(here, pltpu.roll(lab, j * HALF, 1) if j else lab, strip)
        out_ref[b * SUB : b * SUB + SUB, :] = strip
    for i in range(rows):
        line = f_vmem[i].astype(f32)
        for k in range(width // LANES):
            out_ref[rows + k * rows + i : rows + k * rows + i + 1, :] = line[0:1, k * LANES : k * LANES + LANES]
    for t in range(tiles):
        lanes = slice(t * LANES, t * LANES + LANES)
        head_ref[t * SUB : t * SUB + SUB, :] = jnp.where(h_vmem[1, :, lanes] != 0, h_vmem[0, :, lanes], -1).astype(f32)


def logits_kernel(
    rows, cols, chans, slots, per, f_ref, w_ref, bias_ref, side_ref, head_ref, x_ref, e_ref, beside_ref,
):
    x_ref[...] = jnp.zeros_like(x_ref)
    bias = jnp.concatenate([bias_ref[...], jnp.zeros((1, LANES - chans), f32)], axis=1)
    bias = jnp.broadcast_to(bias, (LANES, LANES)).T[0:chans, :]
    width = f_ref.shape[2]

    def score_of(block):
        score = lax.dot_general(w_ref[...], block, (((1,), (1,)), ((), ())), preferred_element_type=f32)
        score = score + jnp.concatenate([bias] * (block.shape[0] // LANES), axis=1)
        return (score - jnp.max(score, axis=0, keepdims=True)) * (LOG2E / STEP)

    side = jnp.concatenate(
        [side_ref[rows + k * rows : rows + k * rows + rows, :] for k in range(width // LANES)], axis=1
    ).astype(bf16)
    beside_ref[...] = side
    beyond = score_of(jnp.concatenate([side, jnp.zeros((LANES - rows, width), bf16)], axis=0))
    lane = lax.broadcasted_iota(jnp.int32, (chans, LANES), 1)
    for step in range(rows // per):
        block = f_ref[step * per : step * per + per].reshape(per * cols, width)
        score = score_of(block)
        for k in range(per):
            i, off = step * per + k, k * cols
            tile = score[:, off // LANES * LANES : off // LANES * LANES + LANES]
            if off % LANES:
                tile = pltpu.roll(tile, LANES - off % LANES, 1)
            tile = jnp.where(lane < cols, tile, jnp.where(lane == cols, pltpu.roll(beyond, cols - i, 1), 0.0))
            x_ref[pl.ds(i, chans, stride=slots), :] = tile
            if i == 0:
                e_ref[0:chans, :] = tile
    e_ref[chans : chans + head_ref.shape[0], :] = head_ref[...]
    e_ref[chans + head_ref.shape[0] :, :] = side_ref[0:SUB, :]


def softmax_fast(groups, chans, slots, fold, w_ref, p_ref):
    sums = [None] * (2 * groups * HALF)
    for c in range(chans):
        for b in range(groups):
            row = c * slots + SUB * b
            upper = w_ref[row : row + SUB, :]
            lower = w_ref[row + 1 : row + 1 + SUB, :]
            slope = (lower - upper) * fold[b]
            twice = slope + slope
            for half, (p, ratio) in enumerate(((upper + slope, twice), (lower - slope, -twice))):
                p, ratio = jnp.exp2(p), jnp.exp2(ratio)
                for m in range(HALF):
                    k = (half * groups + b) * HALF + m
                    if m:
                        p = p * ratio
                    p_ref[c * len(sums) + k] = p
                    sums[k] = p if sums[k] is None else sums[k] + p
    return sums


def softmax_slow(groups, chans, slots, fold, w_ref, p_ref, labels, weights):
    count = len(labels)
    sums, losses = [], jnp.zeros((SUB, LANES), f32)
    for k in range(count):
        half, b, m = k // (groups * HALF), k // HALF % groups, k % HALF

        def score(c, half=half, b=b, m=m):
            row = c * slots + SUB * b
            near = w_ref[pl.ds(row + half, SUB), :]
            away = w_ref[pl.ds(row + 1 - half, SUB), :]
            return near + (away - near) * fold[b] * (2 * m + 1.0)

        top = lax.fori_loop(1, chans, lambda c, t, score=score: jnp.maximum(t, score(c)), score(0))

        def take(c, carry, k=k, top=top, score=score):
            total, picked = carry
            shifted = score(c) - top
            p = jnp.exp2(shifted)
            p_ref[c * count + k] = p
            return total + p, jnp.where(labels[k] == c, shifted, picked)

        zero = jnp.zeros((SUB, LANES), f32)
        total, picked = lax.fori_loop(0, chans, take, (zero, zero))
        sums.append(total)
        losses = losses - weights[k] * picked
    return sums, losses


def pixels(groups, chans, slots, fold, lab_ref, fast, w_ref, p_ref, s_ref, lhs_ref):
    count = 2 * groups * HALF
    labels = []
    for half in range(2):
        for b in range(groups):
            for m in range(HALF):
                k = PATCH - 1 - m if half else m
                labels.append(lab_ref[pl.ds(b * SUB * PATCH + HALF + k, SUB, stride=PATCH), :])
    weights = [jnp.where(lab >= 0, 1.0, 0.0) for lab in labels]

    @pl.when(fast)
    def _():
        sums = softmax_fast(groups, chans, slots, fold, w_ref, p_ref)
        for k in range(count):
            s_ref[k] = sums[k]
        s_ref[count] = jnp.zeros((SUB, LANES), f32)

    @pl.when(jnp.logical_not(fast))
    def _():
        sums, losses = softmax_slow(groups, chans, slots, fold, w_ref, p_ref, labels, weights)
        for k in range(count):
            s_ref[k] = sums[k]
        s_ref[count] = losses

    loss = jnp.zeros((SUB, LANES), f32)
    scale = []
    for k in range(count):
        total = s_ref[k]
        loss = loss + weights[k] * jnp.log(total)
        scale.append(weights[k] / total)
    packed = [
        jnp.concatenate([labels[(half * groups + b) * HALF + m] for b in range(groups)], axis=0).astype(f32).astype(bf16)
        for half in range(2)
        for m in range(HALF)
    ]
    one, none, mid = (jnp.asarray(v, bf16) for v in (1, 0, 0.5))
    picked = jnp.zeros((SUB, LANES), f32)
    tall = groups * SUB

    def two_sums(item):
        totals, runs = [], []
        for half in range(2):
            total = run = None
            for m in reversed(range(HALF)):
                v = item(half, m)
                total = v if total is None else total + v
                if m:
                    run = total if run is None else run + total
            totals.append(total)
            runs.append(run)
        return totals[0], totals[1], runs[0] - runs[1], totals[0] - totals[1]

    for c in range(chans):
        mark = jnp.asarray(c, bf16)
        up, down, run, lean = two_sums(lambda half, m: jnp.where(packed[half * HALF + m] == mark, one, none))
        hits = [v.astype(f32) for v in (up, down, run + lean * mid)]
        parts = [[], []]
        for b in range(groups):
            row = c * slots + SUB * b
            up, down, lean = (v[b * SUB : b * SUB + SUB] for v in hits)
            lean = lean * (fold[b] * 2.0)
            up, down = up - lean, down + lean
            picked = picked + up * w_ref[row : row + SUB, :] + down * w_ref[row + 1 : row + 1 + SUB, :]
            above, below, run, lean = two_sums(
                lambda half, m: p_ref[c * count + (half * groups + b) * HALF + m] * scale[(half * groups + b) * HALF + m]
            )
            lean = (run + lean * 0.5) * (fold[b] * 2.0)
            parts[0].append((above - up) - lean)
            parts[1].append((below - down) + lean)
        for kind in range(2):
            g = jnp.concatenate(parts[kind], axis=0)
            hi = g.astype(bf16)
            at = (kind * chans + c) * tall
            lhs_ref[at : at + tall, 0:LANES] = hi
            lhs_ref[at : at + tall, LANES:] = (g - hi.astype(f32)).astype(bf16)
    return loss + LN2 * jnp.where(fast, -picked, s_ref[count])


def inner_kernel(
    rows, cols, chans, slots, groups, x_ref, got_ref, strip_ref, lift_ref, lift_end_ref, next_ref, next_end_ref,
    back_ref, back_end_ref, lab_ref, mask_ref, out_ref, spill_ref, loss_ref,
    w_ref, p_ref, s_ref, lhs_ref, sum_ref, stack_ref, tile_ref, floor_ref,
):
    step = pl.program_id(0)
    steps = pl.num_programs(0)
    now = lax.rem(step, 2)
    last_col = lax.axis_index("gx") == lax.axis_size("gx") - 1
    last_row = lax.axis_index("gy") == lax.axis_size("gy") - 1
    tall = rows * PATCH
    lane = lax.broadcasted_iota(jnp.int32, (SUB, LANES), 1)

    @pl.when(step == 0)
    def _():
        w_ref[0] = x_ref[...]
        w_ref[0, pl.ds(rows, chans, stride=slots), :] = got_ref[0:chans, :]
        full = w_ref[0]
        floor_ref[0] = jnp.min(full) * STEP
        stack_ref[...] = stack3(full)
        sum_ref[...] = jnp.zeros_like(sum_ref)
        loss_ref[...] = jnp.zeros_like(loss_ref)
        table = jnp.where(last_col, lift_end_ref[...], lift_ref[...])
        w_ref[0] = jnp.dot(stack_ref[...], table, preferred_element_type=f32)

    tile_ref[0:tall, :] = jnp.where(mask_ref[...] != 0, lab_ref[...], -1)
    tile_ref[tall : tall + SUB, :] = got_ref[pl.ds(pl.multiple_of(chans + step * SUB, SUB), SUB), :].astype(jnp.int32)

    @pl.when(step == 0)
    def _():
        for j in range(PATCH):
            for b in range(groups):
                pick = pl.ds(b * SUB * PATCH + j, SUB, stride=PATCH)
                strip = strip_ref[b * SUB : b * SUB + SUB, :]
                strip = pltpu.roll(strip, LANES - j * HALF, 1) if j else strip
                tile_ref[pick, :] = jnp.where(lane < HALF, strip.astype(jnp.int32), tile_ref[pick, :])
        at = chans + steps * SUB
        for j in range(HALF):
            strip = got_ref[at : at + 1, :]
            strip = pltpu.roll(strip, LANES - j * HALF, 1) if j else strip
            row = tile_ref[tall + j : tall + j + 1, :]
            tile_ref[tall + j : tall + j + 1, :] = jnp.where(lane[0:1] < HALF, strip.astype(jnp.int32), row)

    flat = jnp.full((SUB, LANES), 1.0 / STEP, f32)
    sub = lax.broadcasted_iota(jnp.int32, (SUB, LANES), 0)
    fold = [flat] * (groups - 1) + [jnp.where(last_row & (sub == SUB - 1), 0.0, flat)]
    fast = floor_ref[0] >= FLOOR
    loss_ref[...] += pixels(groups, chans, slots, fold, tile_ref, fast, w_ref.at[now], p_ref, s_ref, lhs_ref)
    table = jnp.where(last_col, next_end_ref[...], next_ref[...])
    w_ref[1 - now] = jnp.dot(stack_ref[...], table, preferred_element_type=f32)
    table = jnp.where(last_col, back_end_ref[...], back_ref[...])
    sum_ref[...] += jnp.dot(lhs_ref[...], table, preferred_element_type=f32)

    @pl.when(step == steps - 1)
    def _():
        w_ref[0] = jnp.zeros_like(w_ref[0])
        high = groups * SUB
        for c in range(chans):
            for kind in range(2):
                at = (kind * chans + c) * high
                row = c * slots + kind
                w_ref[0, row : row + high, :] += sum_ref[at : at + high, :]
        out_ref[...] = w_ref[0] * (1.0 / STEP)
        spill_ref[...] = out_ref[pl.ds(rows, chans, stride=slots), :]


def grad_kernel(
    rows, cols, chans, slots, f_ref, beside_ref, g_ref, got_ref, loss_ref, count_ref, mine_ref, other_ref, sum_ref,
):
    row = lax.axis_index("gy")
    sum_ref[...] = g_ref[...]
    sum_ref[pl.ds(0, chans, stride=slots), :] += got_ref[...]
    lane = lax.broadcasted_iota(jnp.int32, (chans, LANES), 1)
    share = LANES // cols
    edge = jnp.zeros((chans, LANES), f32)
    tiles = []
    total = jnp.zeros((chans, LANES), f32)
    for k in range(0, rows, share):
        tile = None
        for r in range(share):
            piece = sum_ref[pl.ds(k + r, chans, stride=slots), :]
            total = total + piece
            edge = jnp.where(lane == k + r, pltpu.roll(piece, (k + r - cols) % LANES, 1), edge)
            if r:
                piece = pltpu.roll(piece, r * cols, 1)
            tile = piece if tile is None else jnp.where(lane < r * cols, tile, piece)
        tiles.append(tile.astype(bf16))
    block = f_ref[...].reshape(rows * cols, f_ref.shape[2])
    out = jnp.dot(jnp.concatenate(tiles, axis=1), block, preferred_element_type=f32)
    beside = jnp.concatenate([beside_ref[...], jnp.zeros((LANES - rows, f_ref.shape[2]), bf16)], axis=0)
    out = out + jnp.dot(edge.astype(bf16), beside, preferred_element_type=f32)
    total = jnp.where(lane <= cols, total, 0.0)
    square = jnp.concatenate([total, jnp.zeros((LANES - chans, LANES), f32)], axis=0)
    bias = jnp.sum(square.T, axis=0, keepdims=True)
    at = lax.broadcasted_iota(jnp.int32, (SUB, LANES), 0)
    rest = jnp.where(at == 1, jnp.sum(loss_ref[...]), count_ref[0, 0].astype(f32))
    stats = jnp.where(at == 0, bias, jnp.where(at < 3, rest, 0.0))
    pieces = out.shape[1] // LANES // 2
    for k in range(pieces):
        low = out[:, k * LANES : k * LANES + LANES]
        high = out[:, (pieces + k) * LANES : (pieces + k + 1) * LANES]
        mine_ref[k * chans : k * chans + chans, :] = jnp.where(row == 0, low, high)
        other_ref[k * chans : k * chans + chans, :] = jnp.where(row == 0, high, low)
    mine_ref[pieces * chans :, :] = stats
    other_ref[pieces * chans :, :] = stats


def final_kernel(chans, y_ref, z_ref, loss_ref, weight_ref, bias_ref):
    pieces = y_ref.shape[0] // chans
    lower = lax.axis_index("gy") == 0
    stats = y_ref[pieces * chans :, :]
    total = stats[2:3, 0:1]
    for k in range(pieces):
        y = y_ref[k * chans : k * chans + chans, :]
        z = z_ref[k * chans : k * chans + chans, :]
        weight_ref[:, k * LANES : k * LANES + LANES] = jnp.where(lower, y, z) / total
        weight_ref[:, (pieces + k) * LANES : (pieces + k + 1) * LANES] = jnp.where(lower, z, y) / total
    loss_ref[...] = stats[1:2, 0:1] / total
    bias_ref[...] = stats[0:1, 0:chans] / total


def body(features, probe_weight, probe_bias, labels, valid_mask, valid_count):
    rows, cols, width = features.shape
    chans = probe_weight.shape[1]
    gx, gy = lax.axis_size("gx"), lax.axis_size("gy")
    if gy != 2 or rows % SUB or 2 * cols != LANES or cols * PATCH % LANES or width % (2 * LANES) or gx & (gx - 1):
        raise ValueError("unsupported tile")
    groups = rows // SUB
    slots = rows + SUB
    count = groups * HALF
    tiles = cols * PATCH // LANES
    tall = rows * PATCH
    depth = 2 * LANES

    def forward(table):
        out = np.zeros((depth, table.shape[1]), np.float32)
        for k in range(3):
            out[k * cols : k * cols + cols] = table[:cols]
            out[3 * cols + k] = table[cols]
        return out

    def backward(table):
        out = np.zeros((table.shape[1] // LANES, 2, LANES, LANES), np.float32)
        out[:, :, :, : cols + 1] = table.T.reshape(-1, 1, LANES, cols + 1)
        return out.reshape(-1, LANES)

    inside, ending = column_tables(cols)
    lift, lift_end, back, back_end = (
        jnp.asarray(t, bf16) for t in (forward(inside), forward(ending), backward(inside), backward(ending))
    )

    shape = lambda *dims: jax.ShapeDtypeStruct(dims, f32)
    held = lambda *dims, kind=f32: pltpu.VMEM(dims, kind)
    far = lambda v: pltpu.with_memory_space_constraint(v, pltpu.HBM)
    here = lambda v: pltpu.with_memory_space_constraint(v, pltpu.VMEM)
    ring = lambda v, axis: lax.ppermute(v, axis, [(i, (i - 1) % lax.axis_size(axis)) for i in range(lax.axis_size(axis))])
    swap = lambda v: lax.ppermute(v, "gy", [(0, 1), (1, 0)])
    tall_x = chans * slots

    side, head = pl.pallas_call(
        functools.partial(pack_kernel, rows),
        in_specs=[ANY] * 3,
        out_specs=[VMEM] * 2,
        out_shape=[held(rows + rows * width // LANES, LANES), held(tiles * SUB, LANES)],
        scratch_shapes=[
            pltpu.VMEM((rows, SUB, width), bf16),
            pltpu.VMEM((2, tall, LANES), jnp.int32),
            pltpu.VMEM((2, SUB, tiles * LANES), jnp.int32),
            pltpu.SemaphoreType.DMA((5,)),
        ],
        compiler_params=ROOM,
        name="pack",
    )(far(features), far(labels), far(valid_mask))
    side = ring(side, "gx")
    x, edge, beside = pl.pallas_call(
        functools.partial(logits_kernel, rows, cols, chans, slots, 4),
        in_specs=[VMEM] * 5,
        out_specs=[VMEM] * 3,
        out_shape=[
            held(tall_x, LANES), held(chans + tiles * SUB + SUB, LANES), held(rows, width, kind=bf16),
        ],
        compiler_params=ROOM,
        name="logits",
    )(*(here(v) for v in (features, probe_weight.T, probe_bias.reshape(1, chans), side, head)))
    got = ring(edge, "gy")
    column = pl.BlockSpec((tall, LANES), lambda t: (0, t))
    block = pl.BlockSpec((depth, LANES), lambda t: (0, t))
    ahead = pl.BlockSpec((depth, LANES), lambda t: (0, jnp.minimum(t + 1, tiles - 1)))
    rear = pl.BlockSpec((depth, LANES), lambda t: (t, 0))
    grad, spill, loss = pl.pallas_call(
        functools.partial(inner_kernel, rows, cols, chans, slots, groups),
        grid=(tiles,),
        in_specs=[VMEM] * 3 + [block, block, ahead, ahead, rear, rear, column, column],
        out_specs=[VMEM] * 3,
        out_shape=[held(tall_x, LANES), held(chans, LANES), held(SUB, LANES)],
        scratch_shapes=[
            pltpu.VMEM((2, tall_x, LANES), f32),
            pltpu.VMEM((2 * chans * count, SUB, LANES), f32),
            pltpu.VMEM((2 * count + 1, SUB, LANES), f32),
            pltpu.VMEM((2 * chans * rows, depth), bf16),
            pltpu.VMEM((2 * chans * rows, LANES), f32),
            pltpu.VMEM((tall_x, depth), bf16),
            pltpu.VMEM((tall + SUB, LANES), jnp.int32),
            pltpu.SMEM((1,), f32),
        ],
        compiler_params=ROOM,
        name="inner",
    )(here(x), here(got), here(side), lift, lift_end, lift, lift_end, back, back_end, labels, valid_mask)
    got = lax.ppermute(spill, "gy", [(i, (i + 1) % gy) for i in range(gy)])
    pack = (chans * width // 2 // LANES + SUB, LANES)
    mine, other = pl.pallas_call(
        functools.partial(grad_kernel, rows, cols, chans, slots),
        in_specs=[VMEM] * 5 + [SMEM],
        out_specs=[VMEM] * 2,
        out_shape=[held(*pack)] * 2,
        scratch_shapes=[pltpu.VMEM((tall_x, LANES), f32)],
        compiler_params=ROOM,
        name="grad",
    )(*(here(v) for v in (features, beside, grad, got, loss)), valid_count)

    total = mine + swap(other)
    step = 1
    while step < gx:
        total = total + lax.ppermute(total, "gx", [(i, i ^ step) for i in range(gx)])
        step *= 2
    loss, weight, bias = pl.pallas_call(
        functools.partial(final_kernel, chans),
        in_specs=[VMEM] * 2,
        out_specs=[VMEM] * 3,
        out_shape=[shape(1, 1), shape(chans, width), shape(1, chans)],
        compiler_params=ROOM,
        name="final",
    )(here(total), here(swap(total)))
    return loss.reshape(1), weight.T, bias.reshape(chans)


def solution(mesh):
    return jax.shard_map(
        body,
        mesh=mesh,
        in_specs=(
            P(("groups", "gy"), "gx", None),
            P(),
            P(),
            P(("groups", "gy"), "gx"),
            P(("groups", "gy"), "gx"),
            P(("groups", "gy"), "gx"),
        ),
        out_specs=(P("groups"), P("groups", None), P("groups")),
        check_vma=False,
    )
```

```python
import functools
import math

import jax
import jax.numpy as jnp
import numpy as np
from jax import lax
from jax.experimental import pallas as pl
from jax.experimental.pallas import tpu as pltpu
from jax.sharding import PartitionSpec as P

PATCH = 14
HALF = PATCH // 2
STEP = 2 * PATCH
LANES = 128
SUB = 8
LOG2E = 1.0 / math.log(2.0)
LN2 = math.log(2.0)
FLOOR = -100.0
f32 = jnp.float32
bf16 = jnp.bfloat16
VMEM = pl.BlockSpec(memory_space=pltpu.VMEM)
ANY = pl.BlockSpec(memory_space=pl.ANY)
ROOM = pltpu.CompilerParams(vmem_limit_bytes=16 * 2**20)
SMEM = pl.BlockSpec(memory_space=pltpu.SMEM)


def whole(shape):
    return pl.BlockSpec(shape, lambda *ids: (0,) * len(shape))


def column_tables(cols):
    tables = np.zeros((2, cols + 1, cols * PATCH), np.float32)
    for q in range(cols * PATCH):
        i, k = divmod((q if q >= HALF else q + cols * PATCH) - HALF, PATCH)
        far = 2 * k + 1
        for end in range(2):
            if end and i == cols - 1:
                tables[end, i + (k >= HALF), q] = STEP
            else:
                tables[end, i, q] = STEP - far
                tables[end, i + 1, q] = far
    return tables


def split3(x):
    hi = x.astype(bf16)
    rest = x - hi.astype(f32)
    mid = rest.astype(bf16)
    return hi, mid, (rest - mid.astype(f32)).astype(bf16)


def stack3(x):
    cols = LANES // 2
    lane = lax.broadcasted_iota(jnp.int32, x.shape, 1)
    hi, mid, low = (part.astype(f32) for part in split3(x))
    first = jnp.where(lane < cols, hi, pltpu.roll(mid, cols, 1))
    second = jnp.where(lane == cols + 1, pltpu.roll(mid, 1, 1), pltpu.roll(low, 2, 1))
    second = jnp.where(lane == cols, hi, jnp.where(lane < cols + 3, second, 0.0))
    second = jnp.where(lane < cols, low, second)
    return jnp.concatenate([first.astype(bf16), second.astype(bf16)], axis=1)


def pack_kernel(
    rows, f_ref, lab_ref, mask_ref, w_ref, bias_ref, out_ref, head_ref, weight_ref, shift_ref, f_vmem, l_vmem, h_vmem, b_vmem, sem,
):
    width = f_vmem.shape[2]
    tiles = head_ref.shape[0] // SUB
    copies = [
        pltpu.make_async_copy(lab_ref.at[:, pl.ds(0, LANES)], l_vmem.at[0], sem.at[0]),
        pltpu.make_async_copy(mask_ref.at[:, pl.ds(0, LANES)], l_vmem.at[1], sem.at[1]),
        pltpu.make_async_copy(f_ref.at[:, pl.ds(0, SUB)], f_vmem, sem.at[2]),
        pltpu.make_async_copy(lab_ref.at[pl.ds(0, SUB)], h_vmem.at[0], sem.at[3]),
        pltpu.make_async_copy(mask_ref.at[pl.ds(0, SUB)], h_vmem.at[1], sem.at[4]),
        pltpu.make_async_copy(w_ref, weight_ref, sem.at[5]),
        pltpu.make_async_copy(bias_ref, b_vmem, sem.at[6]),
    ]
    for copy in copies:
        copy.start()
    at = lax.broadcasted_iota(jnp.int32, (SUB, LANES), 1)
    for copy in copies:
        copy.wait()
    for b in range(rows // SUB):
        strip = jnp.full((SUB, LANES), -1.0, f32)
        for j in range(PATCH):
            pick = pl.ds(b * SUB * PATCH + j, SUB, stride=PATCH)
            lab = jnp.where(l_vmem[1, pick, :] != 0, l_vmem[0, pick, :], -1).astype(f32)
            here = (at >= j * HALF) & (at < j * HALF + HALF)
            strip = jnp.where(here, pltpu.roll(lab, j * HALF, 1) if j else lab, strip)
        out_ref[b * SUB : b * SUB + SUB, :] = strip
    for i in range(rows):
        line = f_vmem[i].astype(f32)
        for k in range(width // LANES):
            out_ref[rows + k * rows + i : rows + k * rows + i + 1, :] = line[0:1, k * LANES : k * LANES + LANES]
    for t in range(tiles):
        lanes = slice(t * LANES, t * LANES + LANES)
        head_ref[t * SUB : t * SUB + SUB, :] = jnp.where(h_vmem[1, :, lanes] != 0, h_vmem[0, :, lanes], -1).astype(f32)
    chans = shift_ref.shape[0]
    bias = jnp.concatenate([b_vmem[...], jnp.zeros((1, LANES - chans), f32)], axis=1)
    shift_ref[...] = jnp.broadcast_to(bias, (LANES, LANES)).T[0:chans, :]


def score_of(w_ref, shift_ref, block):
    score = lax.dot_general(w_ref[...], block, (((1,), (1,)), ((), ())), preferred_element_type=f32)
    score = score + jnp.concatenate([shift_ref[...]] * (block.shape[0] // LANES), axis=1)
    return (score - jnp.max(score, axis=0, keepdims=True)) * (LOG2E / STEP)


def logits_kernel(rows, cols, chans, slots, per, f_ref, w_ref, shift_ref, head_ref, x_ref, e_ref):
    x_ref[...] = jnp.zeros_like(x_ref)
    lane = lax.broadcasted_iota(jnp.int32, (chans, LANES), 1)
    for step in range(rows // per):
        score = score_of(w_ref, shift_ref, f_ref[step * per : step * per + per].reshape(per * cols, f_ref.shape[2]))
        for k in range(per):
            i, off = step * per + k, k * cols
            tile = score[:, off // LANES * LANES : off // LANES * LANES + LANES]
            if off % LANES:
                tile = pltpu.roll(tile, LANES - off % LANES, 1)
            tile = jnp.where(lane < cols, tile, 0.0)
            x_ref[pl.ds(i, chans, stride=slots), :] = tile
            if i == 0:
                e_ref[0:chans, :] = tile
    e_ref[chans:, :] = head_ref[...]


def beside_kernel(rows, chans, side_ref, w_ref, shift_ref, beside_ref, out_ref):
    width = w_ref.shape[1]
    side = jnp.concatenate(
        [side_ref[rows + k * rows : rows + k * rows + rows, :] for k in range(width // LANES)], axis=1
    ).astype(bf16)
    beside_ref[...] = side
    side = jnp.concatenate([side, jnp.zeros((LANES - rows, width), bf16)], axis=0)
    out_ref[0:chans, :] = score_of(w_ref, shift_ref, side)
    out_ref[chans:, :] = side_ref[0:SUB, :]


def softmax_fast(groups, chans, slots, fold, w_ref, p_ref):
    sums = [None] * (2 * groups * HALF)
    for c in range(chans):
        for b in range(groups):
            row = c * slots + SUB * b
            upper = w_ref[row : row + SUB, :]
            lower = w_ref[row + 1 : row + 1 + SUB, :]
            slope = (lower - upper) * fold[b]
            twice = slope + slope
            for half, (p, ratio) in enumerate(((upper + slope, twice), (lower - slope, -twice))):
                p, ratio = jnp.exp2(p), jnp.exp2(ratio)
                for m in range(HALF):
                    k = (half * groups + b) * HALF + m
                    if m:
                        p = p * ratio
                    p_ref[c * len(sums) + k] = p
                    sums[k] = p if sums[k] is None else sums[k] + p
    return sums


def softmax_slow(groups, chans, slots, fold, w_ref, p_ref, labels, weights):
    count = len(labels)
    sums, losses = [], jnp.zeros((SUB, LANES), f32)
    for k in range(count):
        half, b, m = k // (groups * HALF), k // HALF % groups, k % HALF

        def score(c, half=half, b=b, m=m):
            row = c * slots + SUB * b
            near = w_ref[pl.ds(row + half, SUB), :]
            away = w_ref[pl.ds(row + 1 - half, SUB), :]
            return near + (away - near) * fold[b] * (2 * m + 1.0)

        top = lax.fori_loop(1, chans, lambda c, t, score=score: jnp.maximum(t, score(c)), score(0))

        def take(c, carry, k=k, top=top, score=score):
            total, picked = carry
            shifted = score(c) - top
            p = jnp.exp2(shifted)
            p_ref[c * count + k] = p
            return total + p, jnp.where(labels[k] == c, shifted, picked)

        zero = jnp.zeros((SUB, LANES), f32)
        total, picked = lax.fori_loop(0, chans, take, (zero, zero))
        sums.append(total)
        losses = losses - weights[k] * picked
    return sums, losses


def pixels(groups, chans, slots, fold, lab_ref, fast, prepare, w_ref, p_ref, s_ref, lhs_ref):
    count = 2 * groups * HALF
    labels = []
    for half in range(2):
        for b in range(groups):
            for m in range(HALF):
                k = PATCH - 1 - m if half else m
                labels.append(lab_ref[pl.ds(b * SUB * PATCH + HALF + k, SUB, stride=PATCH), :])
    weights = [jnp.where(lab >= 0, 1.0, 0.0) for lab in labels]

    @pl.when(fast)
    def _():
        sums = softmax_fast(groups, chans, slots, fold, w_ref, p_ref)
        for k in range(count):
            s_ref[k] = sums[k]
        s_ref[count] = jnp.zeros((SUB, LANES), f32)
        prepare()

    @pl.when(jnp.logical_not(fast))
    def _():
        sums, losses = softmax_slow(groups, chans, slots, fold, w_ref, p_ref, labels, weights)
        for k in range(count):
            s_ref[k] = sums[k]
        s_ref[count] = losses
        prepare()

    loss = jnp.zeros((SUB, LANES), f32)
    scale = []
    for k in range(count):
        total = s_ref[k]
        loss = loss + weights[k] * jnp.log(total)
        scale.append(weights[k] / total)
    packed = [
        jnp.concatenate([labels[(half * groups + b) * HALF + m] for b in range(groups)], axis=0).astype(f32).astype(bf16)
        for half in range(2)
        for m in range(HALF)
    ]
    one, none, mid = (jnp.asarray(v, bf16) for v in (1, 0, 0.5))
    picked = jnp.zeros((SUB, LANES), f32)
    tall = groups * SUB

    def two_sums(item):
        totals, runs = [], []
        for half in range(2):
            total = run = None
            for m in reversed(range(HALF)):
                v = item(half, m)
                total = v if total is None else total + v
                if m:
                    run = total if run is None else run + total
            totals.append(total)
            runs.append(run)
        return totals[0], totals[1], runs[0] - runs[1], totals[0] - totals[1]

    for c in range(chans):
        mark = jnp.asarray(c, bf16)
        up, down, run, lean = two_sums(lambda half, m: jnp.where(packed[half * HALF + m] == mark, one, none))
        hits = [v.astype(f32) for v in (up, down, run + lean * mid)]
        parts = [[], []]
        for b in range(groups):
            row = c * slots + SUB * b
            up, down, lean = (v[b * SUB : b * SUB + SUB] for v in hits)
            lean = lean * (fold[b] * 2.0)
            up, down = up - lean, down + lean
            picked = picked + up * w_ref[row : row + SUB, :] + down * w_ref[row + 1 : row + 1 + SUB, :]
            above, below, run, lean = two_sums(
                lambda half, m: p_ref[c * count + (half * groups + b) * HALF + m] * scale[(half * groups + b) * HALF + m]
            )
            lean = (run + lean * 0.5) * (fold[b] * 2.0)
            parts[0].append((above - up) - lean)
            parts[1].append((below - down) + lean)
        for kind in range(2):
            g = jnp.concatenate(parts[kind], axis=0)
            hi = g.astype(bf16)
            at = (kind * chans + c) * tall
            lhs_ref[at : at + tall, 0:LANES] = hi
            lhs_ref[at : at + tall, LANES:] = (g - hi.astype(f32)).astype(bf16)
    return loss + LN2 * jnp.where(fast, -picked, s_ref[count])


def inner_kernel(rows, cols, chans, slots, groups, part, begin, tiles, *refs):
    (got_ref, lift_ref, lift_end_ref, next_ref, next_end_ref, back_ref, back_end_ref, lab_ref, mask_ref), refs = (
        refs[:9], refs[9:],
    )
    if part == 0:
        (x_ref, sum_ref, loss_ref, stack_ref, floor_ref), refs = refs[:5], refs[5:]
    elif part == 1:
        (sum_in_ref, loss_in_ref, stack_ref, floor_ref, sum_ref, loss_ref), refs = refs[:6], refs[6:]
    else:
        (x_ref, beyond_ref, corner_ref, strip_ref, sum_in_ref, loss_in_ref), refs = refs[:6], refs[6:]
        (out_ref, spill_ref, loss_ref), refs = refs[:3], refs[3:]
    (w_ref, p_ref, s_ref, lhs_ref, tile_ref), refs = refs[:5], refs[5:]
    if part == 2:
        sum_ref, stack_ref, floor_ref = refs
    step = pl.program_id(0)
    steps = pl.num_programs(0)
    now = lax.rem(step, 2)
    which = lax.rem(step + begin, tiles)
    last_col = lax.axis_index("gx") == lax.axis_size("gx") - 1
    last_row = lax.axis_index("gy") == lax.axis_size("gy") - 1
    tall = rows * PATCH
    lane = lax.broadcasted_iota(jnp.int32, (SUB, LANES), 1)

    @pl.when(step == 0)
    def _():
        if part == 0:
            sum_ref[...] = jnp.zeros_like(sum_ref)
            loss_ref[...] = jnp.zeros_like(loss_ref)
        else:
            sum_ref[...] = sum_in_ref[...]
            loss_ref[...] = loss_in_ref[...]
        if part != 1:
            w_ref[0] = x_ref[...]
            w_ref[0, pl.ds(rows, chans, stride=slots), :] = got_ref[0:chans, :]
            if part == 2:
                wide = lax.broadcasted_iota(jnp.int32, (chans, LANES), 1)
                for i in range(rows + 1):
                    column = beyond_ref[0:chans, :] if i < rows else corner_ref[0:chans, :]
                    column = pltpu.roll(column, cols - i if i < rows else cols, 1)
                    pick = pl.ds(i, chans, stride=slots)
                    w_ref[0, pick, :] = jnp.where(wide == cols, column, w_ref[0, pick, :])
            full = w_ref[0]
            floor_ref[0] = jnp.min(full) * STEP
            stack_ref[...] = stack3(full)
        table = jnp.where(last_col, lift_end_ref[...], lift_ref[...])
        w_ref[0] = jnp.dot(stack_ref[...], table, preferred_element_type=f32)

    tile_ref[0:tall, :] = jnp.where(mask_ref[...] != 0, lab_ref[...], -1)
    tile_ref[tall : tall + SUB, :] = got_ref[pl.ds(pl.multiple_of(chans + which * SUB, SUB), SUB), :].astype(jnp.int32)

    if part == 2:

        @pl.when(which == 0)
        def _():
            for j in range(PATCH):
                for b in range(groups):
                    pick = pl.ds(b * SUB * PATCH + j, SUB, stride=PATCH)
                    strip = strip_ref[b * SUB : b * SUB + SUB, :]
                    strip = pltpu.roll(strip, LANES - j * HALF, 1) if j else strip
                    tile_ref[pick, :] = jnp.where(lane < HALF, strip.astype(jnp.int32), tile_ref[pick, :])
            for j in range(HALF):
                strip = corner_ref[chans : chans + 1, :]
                strip = pltpu.roll(strip, LANES - j * HALF, 1) if j else strip
                row = tile_ref[tall + j : tall + j + 1, :]
                tile_ref[tall + j : tall + j + 1, :] = jnp.where(lane[0:1] < HALF, strip.astype(jnp.int32), row)

    flat = jnp.full((SUB, LANES), 1.0 / STEP, f32)
    sub = lax.broadcasted_iota(jnp.int32, (SUB, LANES), 0)
    fold = [flat] * (groups - 1) + [jnp.where(last_row & (sub == SUB - 1), 0.0, flat)]
    fast = floor_ref[0] >= FLOOR

    def prepare():
        table = jnp.where(last_col, next_end_ref[...], next_ref[...])
        w_ref[1 - now] = jnp.dot(stack_ref[...], table, preferred_element_type=f32)

    loss_ref[...] += pixels(groups, chans, slots, fold, tile_ref, fast, prepare, w_ref.at[now], p_ref, s_ref, lhs_ref)
    table = jnp.where(last_col, back_end_ref[...], back_ref[...])
    sum_ref[...] += jnp.dot(lhs_ref[...], table, preferred_element_type=f32)

    if part == 2:

        @pl.when(step == steps - 1)
        def _():
            w_ref[0] = jnp.zeros_like(w_ref[0])
            high = groups * SUB
            for c in range(chans):
                for kind in range(2):
                    at = (kind * chans + c) * high
                    row = c * slots + kind
                    w_ref[0, row : row + high, :] += sum_ref[at : at + high, :]
            out_ref[...] = w_ref[0] * (1.0 / STEP)
            spill_ref[...] = out_ref[pl.ds(rows, chans, stride=slots), :]


def grad_kernel(
    rows, cols, chans, slots, f_ref, beside_ref, g_ref, got_ref, loss_ref, count_ref, mine_ref, other_ref, sum_ref,
):
    row = lax.axis_index("gy")
    sum_ref[...] = g_ref[...]
    sum_ref[pl.ds(0, chans, stride=slots), :] += got_ref[...]
    lane = lax.broadcasted_iota(jnp.int32, (chans, LANES), 1)
    share = LANES // cols
    edge = jnp.zeros((chans, LANES), f32)
    tiles = []
    total = jnp.zeros((chans, LANES), f32)
    for k in range(0, rows, share):
        tile = None
        for r in range(share):
            piece = sum_ref[pl.ds(k + r, chans, stride=slots), :]
            total = total + piece
            edge = jnp.where(lane == k + r, pltpu.roll(piece, (k + r - cols) % LANES, 1), edge)
            if r:
                piece = pltpu.roll(piece, r * cols, 1)
            tile = piece if tile is None else jnp.where(lane < r * cols, tile, piece)
        tiles.append(tile.astype(bf16))
    block = f_ref[...].reshape(rows * cols, f_ref.shape[2])
    out = jnp.dot(jnp.concatenate(tiles, axis=1), block, preferred_element_type=f32)
    beside = jnp.concatenate([beside_ref[...], jnp.zeros((LANES - rows, f_ref.shape[2]), bf16)], axis=0)
    out = out + jnp.dot(edge.astype(bf16), beside, preferred_element_type=f32)
    total = jnp.where(lane <= cols, total, 0.0)
    square = jnp.concatenate([total, jnp.zeros((LANES - chans, LANES), f32)], axis=0)
    bias = jnp.sum(square.T, axis=0, keepdims=True)
    at = lax.broadcasted_iota(jnp.int32, (SUB, LANES), 0)
    rest = jnp.where(at == 1, jnp.sum(loss_ref[...]), count_ref[0, 0].astype(f32))
    stats = jnp.where(at == 0, bias, jnp.where(at < 3, rest, 0.0))
    pieces = out.shape[1] // LANES // 2
    for k in range(pieces):
        low = out[:, k * LANES : k * LANES + LANES]
        high = out[:, (pieces + k) * LANES : (pieces + k + 1) * LANES]
        mine_ref[k * chans : k * chans + chans, :] = jnp.where(row == 0, low, high)
        other_ref[k * chans : k * chans + chans, :] = jnp.where(row == 0, high, low)
    mine_ref[pieces * chans :, :] = stats
    other_ref[pieces * chans :, :] = stats


def final_kernel(chans, y_ref, z_ref, loss_ref, weight_ref, bias_ref):
    pieces = y_ref.shape[0] // chans
    lower = lax.axis_index("gy") == 0
    stats = y_ref[pieces * chans :, :]
    total = stats[2:3, 0:1]
    for k in range(pieces):
        y = y_ref[k * chans : k * chans + chans, :]
        z = z_ref[k * chans : k * chans + chans, :]
        weight_ref[:, k * LANES : k * LANES + LANES] = jnp.where(lower, y, z) / total
        weight_ref[:, (pieces + k) * LANES : (pieces + k + 1) * LANES] = jnp.where(lower, z, y) / total
    loss_ref[...] = stats[1:2, 0:1] / total
    bias_ref[...] = stats[0:1, 0:chans] / total


def body(features, probe_weight, probe_bias, labels, valid_mask, valid_count):
    rows, cols, width = features.shape
    chans = probe_weight.shape[1]
    gx, gy = lax.axis_size("gx"), lax.axis_size("gy")
    if gy != 2 or rows % SUB or 2 * cols != LANES or cols * PATCH % LANES or width % (2 * LANES) or gx & (gx - 1):
        raise ValueError("unsupported tile")
    groups = rows // SUB
    slots = rows + SUB
    count = groups * HALF
    tiles = cols * PATCH // LANES
    tall = rows * PATCH
    depth = 2 * LANES

    def forward(table):
        out = np.zeros((depth, table.shape[1]), np.float32)
        for k in range(3):
            out[k * cols : k * cols + cols] = table[:cols]
            out[3 * cols + k] = table[cols]
        return out

    def backward(table):
        out = np.zeros((table.shape[1] // LANES, 2, LANES, LANES), np.float32)
        out[:, :, :, : cols + 1] = table.T.reshape(-1, 1, LANES, cols + 1)
        return out.reshape(-1, LANES)

    inside, ending = column_tables(cols)
    lift, lift_end, back, back_end = (
        jnp.asarray(t, bf16) for t in (forward(inside), forward(ending), backward(inside), backward(ending))
    )

    shape = lambda *dims: jax.ShapeDtypeStruct(dims, f32)
    held = lambda *dims, kind=f32: pltpu.VMEM(dims, kind)
    far = lambda v: pltpu.with_memory_space_constraint(v, pltpu.HBM)
    here = lambda v: pltpu.with_memory_space_constraint(v, pltpu.VMEM)
    ring = lambda v, axis: lax.ppermute(v, axis, [(i, (i - 1) % lax.axis_size(axis)) for i in range(lax.axis_size(axis))])
    swap = lambda v: lax.ppermute(v, "gy", [(0, 1), (1, 0)])
    tall_x = chans * slots

    side, head, weight, shift = pl.pallas_call(
        functools.partial(pack_kernel, rows),
        in_specs=[ANY] * 5,
        out_specs=[VMEM] * 4,
        out_shape=[
            held(rows + rows * width // LANES, LANES), held(tiles * SUB, LANES), held(chans, width, kind=bf16),
            held(chans, LANES),
        ],
        scratch_shapes=[
            pltpu.VMEM((rows, SUB, width), bf16),
            pltpu.VMEM((2, tall, LANES), jnp.int32),
            pltpu.VMEM((2, SUB, tiles * LANES), jnp.int32),
            pltpu.VMEM((1, chans), f32),
            pltpu.SemaphoreType.DMA((7,)),
        ],
        compiler_params=ROOM,
        name="pack",
    )(*(far(v) for v in (features, labels, valid_mask, probe_weight.T, probe_bias.reshape(1, chans))))
    side = ring(side, "gx")
    x, edge = pl.pallas_call(
        functools.partial(logits_kernel, rows, cols, chans, slots, 4),
        in_specs=[VMEM] * 4,
        out_specs=[VMEM] * 2,
        out_shape=[held(tall_x, LANES), held(chans + tiles * SUB, LANES)],
        compiler_params=ROOM,
        name="logits",
    )(*(here(v) for v in (features, weight, shift, head)))
    got = ring(edge, "gy")

    sums = (2 * chans * rows, LANES)
    stacked = held(tall_x, depth, kind=bf16)

    def inner(part, begin, steps, *args):
        at = lambda t: (t + begin) % tiles
        column = pl.BlockSpec((tall, LANES), lambda t: (0, at(t)))
        block = pl.BlockSpec((depth, LANES), lambda t: (0, at(t)))
        ahead = pl.BlockSpec((depth, LANES), lambda t: (0, at(t + 1)))
        rear = pl.BlockSpec((depth, LANES), lambda t: (at(t), 0))
        outs = [
            ([held(*sums), held(SUB, LANES), stacked, shape(1)], [VMEM] * 3 + [SMEM], [VMEM]),
            ([held(*sums), held(SUB, LANES)], [VMEM] * 2, [VMEM] * 3 + [SMEM]),
            ([held(tall_x, LANES), held(chans, LANES), held(SUB, LANES)], [VMEM] * 3, [VMEM] * 6),
        ][part]
        return pl.pallas_call(
            functools.partial(inner_kernel, rows, cols, chans, slots, groups, part, begin, tiles),
            grid=(steps,),
            in_specs=[VMEM, block, block, ahead, ahead, rear, rear, column, column] + outs[2],
            out_specs=outs[1],
            out_shape=outs[0],
            scratch_shapes=[
                pltpu.VMEM((2, tall_x, LANES), f32),
                pltpu.VMEM((2 * chans * count, SUB, LANES), f32),
                pltpu.VMEM((2 * count + 1, SUB, LANES), f32),
                pltpu.VMEM((2 * chans * rows, depth), bf16),
                pltpu.VMEM((tall + SUB, LANES), jnp.int32),
            ] + ([pltpu.VMEM(sums, f32), stacked, pltpu.SMEM((1,), f32)] if part == 2 else []),
            cost_estimate=pl.CostEstimate(flops=10**9, bytes_accessed=2 * 10**6, transcendentals=10**6),
            compiler_params=ROOM,
            name=("inner_head", "inner_middle", "inner_tail")[part],
        )(here(got), lift, lift_end, lift, lift_end, back, back_end, labels, valid_mask, *args)

    middle = tiles // 2 + 1
    total, loss, stack, floor = inner(0, 1, middle - 1, here(x))
    side, total = lax.optimization_barrier((side, total))
    beside, beyond = pl.pallas_call(
        functools.partial(beside_kernel, rows, chans),
        in_specs=[VMEM] * 3,
        out_specs=[VMEM] * 2,
        out_shape=[held(rows, width, kind=bf16), held(chans + SUB, LANES)],
        compiler_params=ROOM,
        name="beside",
    )(here(side), here(weight), here(shift))
    corner = ring(beyond, "gy")
    total, loss = inner(1, middle, tiles - 1 - middle, *(here(v) for v in (total, loss, stack)), floor)
    grad, spill, loss = inner(2, tiles - 1, 2, *(here(v) for v in (x, beyond, corner, side, total, loss)))
    got = lax.ppermute(spill, "gy", [(i, (i + 1) % gy) for i in range(gy)])
    pack = (chans * width // 2 // LANES + SUB, LANES)
    mine, other = pl.pallas_call(
        functools.partial(grad_kernel, rows, cols, chans, slots),
        in_specs=[VMEM] * 5 + [SMEM],
        out_specs=[VMEM] * 2,
        out_shape=[held(*pack)] * 2,
        scratch_shapes=[pltpu.VMEM((tall_x, LANES), f32)],
        compiler_params=ROOM,
        name="grad",
    )(*(here(v) for v in (features, beside, grad, got, loss)), valid_count)

    total = mine + swap(other)
    step = 1
    while step < gx:
        total = total + lax.ppermute(total, "gx", [(i, i ^ step) for i in range(gx)])
        step *= 2
    loss, weight, bias = pl.pallas_call(
        functools.partial(final_kernel, chans),
        in_specs=[VMEM] * 2,
        out_specs=[VMEM] * 3,
        out_shape=[shape(1, 1), shape(chans, width), shape(1, chans)],
        compiler_params=ROOM,
        name="final",
    )(here(total), here(swap(total)))
    return loss.reshape(1), weight.T, bias.reshape(chans)


def solution(mesh):
    return jax.shard_map(
        body,
        mesh=mesh,
        in_specs=(
            P(("groups", "gy"), "gx", None),
            P(),
            P(),
            P(("groups", "gy"), "gx"),
            P(("groups", "gy"), "gx"),
            P(("groups", "gy"), "gx"),
        ),
        out_specs=(P("groups"), P("groups", None), P("groups")),
        check_vma=False,
    )
```

```python
import functools
import math

import jax
import jax.numpy as jnp
import numpy as np
from jax import lax
from jax.experimental import pallas as pl
from jax.experimental.pallas import tpu as pltpu
from jax.sharding import PartitionSpec as P

PATCH = 14
HALF = PATCH // 2
STEP = 2 * PATCH
LANES = 128
SUB = 8
LOG2E = 1.0 / math.log(2.0)
LN2 = math.log(2.0)
FLOOR = -100.0
f32 = jnp.float32
bf16 = jnp.bfloat16
VMEM = pl.BlockSpec(memory_space=pltpu.VMEM)
ANY = pl.BlockSpec(memory_space=pl.ANY)
ROOM = pltpu.CompilerParams(vmem_limit_bytes=16 * 2**20)
SMEM = pl.BlockSpec(memory_space=pltpu.SMEM)


def whole(shape):
    return pl.BlockSpec(shape, lambda *ids: (0,) * len(shape))


def column_tables(cols):
    tables = np.zeros((2, cols + 1, cols * PATCH), np.float32)
    for q in range(cols * PATCH):
        i, k = divmod((q if q >= HALF else q + cols * PATCH) - HALF, PATCH)
        far = 2 * k + 1
        for end in range(2):
            if end and i == cols - 1:
                tables[end, i + (k >= HALF), q] = STEP
            else:
                tables[end, i, q] = STEP - far
                tables[end, i + 1, q] = far
    return tables


def split3(x):
    hi = x.astype(bf16)
    rest = x - hi.astype(f32)
    mid = rest.astype(bf16)
    return hi, mid, (rest - mid.astype(f32)).astype(bf16)


def stack3(x):
    cols = LANES // 2
    lane = lax.broadcasted_iota(jnp.int32, x.shape, 1)
    hi, mid, low = (part.astype(f32) for part in split3(x))
    first = jnp.where(lane < cols, hi, pltpu.roll(mid, cols, 1))
    second = jnp.where(lane == cols + 1, pltpu.roll(mid, 1, 1), pltpu.roll(low, 2, 1))
    second = jnp.where(lane == cols, hi, jnp.where(lane < cols + 3, second, 0.0))
    second = jnp.where(lane < cols, low, second)
    return jnp.concatenate([first.astype(bf16), second.astype(bf16)], axis=1)


def pack_kernel(
    rows, f_ref, lab_ref, mask_ref, w_ref, bias_ref, out_ref, head_ref, weight_ref, shift_ref, f_vmem, l_vmem, h_vmem, b_vmem, sem,
):
    width = f_vmem.shape[2]
    tiles = head_ref.shape[0] // SUB
    copies = [
        pltpu.make_async_copy(lab_ref.at[:, pl.ds(0, LANES)], l_vmem.at[0], sem.at[0]),
        pltpu.make_async_copy(mask_ref.at[:, pl.ds(0, LANES)], l_vmem.at[1], sem.at[1]),
        pltpu.make_async_copy(f_ref.at[:, pl.ds(0, SUB)], f_vmem, sem.at[2]),
        pltpu.make_async_copy(lab_ref.at[pl.ds(0, SUB)], h_vmem.at[0], sem.at[3]),
        pltpu.make_async_copy(mask_ref.at[pl.ds(0, SUB)], h_vmem.at[1], sem.at[4]),
        pltpu.make_async_copy(w_ref, weight_ref, sem.at[5]),
        pltpu.make_async_copy(bias_ref, b_vmem, sem.at[6]),
    ]
    for copy in copies:
        copy.start()
    at = lax.broadcasted_iota(jnp.int32, (SUB, LANES), 1)
    for copy in copies:
        copy.wait()
    for b in range(rows // SUB):
        strip = jnp.full((SUB, LANES), -1.0, f32)
        for j in range(PATCH):
            pick = pl.ds(b * SUB * PATCH + j, SUB, stride=PATCH)
            lab = jnp.where(l_vmem[1, pick, :] != 0, l_vmem[0, pick, :], -1).astype(f32)
            here = (at >= j * HALF) & (at < j * HALF + HALF)
            strip = jnp.where(here, pltpu.roll(lab, j * HALF, 1) if j else lab, strip)
        out_ref[b * SUB : b * SUB + SUB, :] = strip
    for i in range(rows):
        line = f_vmem[i].astype(f32)
        for k in range(width // LANES):
            out_ref[rows + k * rows + i : rows + k * rows + i + 1, :] = line[0:1, k * LANES : k * LANES + LANES]
    for t in range(tiles):
        lanes = slice(t * LANES, t * LANES + LANES)
        head_ref[t * SUB : t * SUB + SUB, :] = jnp.where(h_vmem[1, :, lanes] != 0, h_vmem[0, :, lanes], -1).astype(f32)
    chans = shift_ref.shape[0]
    bias = jnp.concatenate([b_vmem[...], jnp.zeros((1, LANES - chans), f32)], axis=1)
    shift_ref[...] = jnp.broadcast_to(bias, (LANES, LANES)).T[0:chans, :]


def score_of(w_ref, shift_ref, block):
    score = lax.dot_general(w_ref[...], block, (((1,), (1,)), ((), ())), preferred_element_type=f32)
    score = score + jnp.concatenate([shift_ref[...]] * (block.shape[0] // LANES), axis=1)
    return (score - jnp.max(score, axis=0, keepdims=True)) * (LOG2E / STEP)


def logits_kernel(rows, cols, chans, slots, per, f_ref, w_ref, shift_ref, head_ref, side_ref, x_ref, e_ref):
    x_ref[...] = jnp.zeros_like(x_ref)
    lane = lax.broadcasted_iota(jnp.int32, (chans, LANES), 1)
    for step in range(rows // per):
        score = score_of(w_ref, shift_ref, f_ref[step * per : step * per + per].reshape(per * cols, f_ref.shape[2]))
        for k in range(per):
            i, off = step * per + k, k * cols
            tile = score[:, off // LANES * LANES : off // LANES * LANES + LANES]
            if off % LANES:
                tile = pltpu.roll(tile, LANES - off % LANES, 1)
            tile = jnp.where(lane < cols, tile, 0.0)
            x_ref[pl.ds(i, chans, stride=slots), :] = tile
            if i == 0:
                e_ref[0:chans, :] = tile
    e_ref[chans : chans + head_ref.shape[0], :] = head_ref[...]
    e_ref[chans + head_ref.shape[0] :, :] = side_ref[0:SUB, :]


def beside_kernel(rows, chans, side_ref, w_ref, shift_ref, beside_ref, out_ref):
    width = w_ref.shape[1]
    side = jnp.concatenate(
        [side_ref[rows + k * rows : rows + k * rows + rows, :] for k in range(width // LANES)], axis=1
    ).astype(bf16)
    beside_ref[...] = side
    side = jnp.concatenate([side, jnp.zeros((LANES - rows, width), bf16)], axis=0)
    out_ref[0:chans, :] = score_of(w_ref, shift_ref, side)
    out_ref[chans:, :] = side_ref[0:SUB, :]


def softmax_fast(groups, chans, slots, fold, w_ref, p_ref):
    sums = [None] * (2 * groups * HALF)
    for c in range(chans):
        for b in range(groups):
            row = c * slots + SUB * b
            upper = w_ref[row : row + SUB, :]
            lower = w_ref[row + 1 : row + 1 + SUB, :]
            slope = (lower - upper) * fold[b]
            twice = slope + slope
            for half, (p, ratio) in enumerate(((upper + slope, twice), (lower - slope, -twice))):
                p, ratio = jnp.exp2(p), jnp.exp2(ratio)
                for m in range(HALF):
                    k = (half * groups + b) * HALF + m
                    if m:
                        p = p * ratio
                    p_ref[c * len(sums) + k] = p
                    sums[k] = p if sums[k] is None else sums[k] + p
    return sums


def softmax_slow(groups, chans, slots, fold, w_ref, p_ref, labels, weights):
    count = len(labels)
    sums, losses = [], jnp.zeros((SUB, LANES), f32)
    for k in range(count):
        half, b, m = k // (groups * HALF), k // HALF % groups, k % HALF

        def score(c, half=half, b=b, m=m):
            row = c * slots + SUB * b
            near = w_ref[pl.ds(row + half, SUB), :]
            away = w_ref[pl.ds(row + 1 - half, SUB), :]
            return near + (away - near) * fold[b] * (2 * m + 1.0)

        top = lax.fori_loop(1, chans, lambda c, t, score=score: jnp.maximum(t, score(c)), score(0))

        def take(c, carry, k=k, top=top, score=score):
            total, picked = carry
            shifted = score(c) - top
            p = jnp.exp2(shifted)
            p_ref[c * count + k] = p
            return total + p, jnp.where(labels[k] == c, shifted, picked)

        zero = jnp.zeros((SUB, LANES), f32)
        total, picked = lax.fori_loop(0, chans, take, (zero, zero))
        sums.append(total)
        losses = losses - weights[k] * picked
    return sums, losses


def pixels(groups, chans, slots, fold, lab_ref, fast, prepare, w_ref, p_ref, s_ref, lhs_ref):
    count = 2 * groups * HALF
    labels = []
    for half in range(2):
        for b in range(groups):
            for m in range(HALF):
                k = PATCH - 1 - m if half else m
                labels.append(lab_ref[pl.ds(b * SUB * PATCH + HALF + k, SUB, stride=PATCH), :])
    weights = [jnp.where(lab >= 0, 1.0, 0.0) for lab in labels]

    @pl.when(fast)
    def _():
        sums = softmax_fast(groups, chans, slots, fold, w_ref, p_ref)
        for k in range(count):
            s_ref[k] = sums[k]
        s_ref[count] = jnp.zeros((SUB, LANES), f32)
        prepare()

    @pl.when(jnp.logical_not(fast))
    def _():
        sums, losses = softmax_slow(groups, chans, slots, fold, w_ref, p_ref, labels, weights)
        for k in range(count):
            s_ref[k] = sums[k]
        s_ref[count] = losses
        prepare()

    loss = jnp.zeros((SUB, LANES), f32)
    scale = []
    for k in range(count):
        total = s_ref[k]
        loss = loss + weights[k] * jnp.log(total)
        scale.append(weights[k] / total)
    packed = [
        jnp.concatenate([labels[(half * groups + b) * HALF + m] for b in range(groups)], axis=0).astype(f32).astype(bf16)
        for half in range(2)
        for m in range(HALF)
    ]
    one, none, mid = (jnp.asarray(v, bf16) for v in (1, 0, 0.5))
    picked = jnp.zeros((SUB, LANES), f32)
    tall = groups * SUB

    def two_sums(item):
        totals, runs = [], []
        for half in range(2):
            total = run = None
            for m in reversed(range(HALF)):
                v = item(half, m)
                total = v if total is None else total + v
                if m:
                    run = total if run is None else run + total
            totals.append(total)
            runs.append(run)
        return totals[0], totals[1], runs[0] - runs[1], totals[0] - totals[1]

    for c in range(chans):
        mark = jnp.asarray(c, bf16)
        up, down, run, lean = two_sums(lambda half, m: jnp.where(packed[half * HALF + m] == mark, one, none))
        hits = [v.astype(f32) for v in (up, down, run + lean * mid)]
        parts = [[], []]
        for b in range(groups):
            row = c * slots + SUB * b
            up, down, lean = (v[b * SUB : b * SUB + SUB] for v in hits)
            lean = lean * (fold[b] * 2.0)
            up, down = up - lean, down + lean
            picked = picked + up * w_ref[row : row + SUB, :] + down * w_ref[row + 1 : row + 1 + SUB, :]
            above, below, run, lean = two_sums(
                lambda half, m: p_ref[c * count + (half * groups + b) * HALF + m] * scale[(half * groups + b) * HALF + m]
            )
            lean = (run + lean * 0.5) * (fold[b] * 2.0)
            parts[0].append((above - up) - lean)
            parts[1].append((below - down) + lean)
        for kind in range(2):
            g = jnp.concatenate(parts[kind], axis=0)
            hi = g.astype(bf16)
            at = (kind * chans + c) * tall
            lhs_ref[at : at + tall, 0:LANES] = hi
            lhs_ref[at : at + tall, LANES:] = (g - hi.astype(f32)).astype(bf16)
    return loss + LN2 * jnp.where(fast, -picked, s_ref[count])


def first_columns(rows, groups, chans, slots, last_row, own_ref, got_ref, w_ref, p_ref, lhs_ref):
    lane = lax.broadcasted_iota(jnp.int32, (SUB, LANES), 1)
    sub = lax.broadcasted_iota(jnp.int32, (SUB, LANES), 0)
    turn = HALF * HALF
    share = jnp.zeros((SUB, LANES), f32)
    for k in range(PATCH):
        share = jnp.where(lane >= k * HALF, (2 * k + 1.0) / STEP, share)
    end = jnp.where(last_row & (sub == SUB - 1), jnp.where(lane < turn, 0.0, 1.0), share)
    shares = [share] * (groups - 1) + [end]
    tall = groups * SUB
    loss = jnp.zeros((SUB, LANES), f32)
    scale, labels = [], []
    for b in range(groups):
        upper = own_ref[b * SUB : b * SUB + SUB, :]
        at = (b + 1) * SUB
        lower = got_ref[got_ref.shape[0] - SUB :, :] if at == rows else own_ref[at : at + SUB, :]
        lower = jnp.where(sub == SUB - 1, pltpu.roll(lower, SUB - 1, 0), pltpu.roll(upper, SUB - 1, 0))
        label = jnp.where(lane < turn, pltpu.roll(upper, LANES - turn, 1), pltpu.roll(lower, turn, 1))
        label = jnp.where(lane < PATCH * HALF, label, -1.0).astype(jnp.int32)
        top = None
        for c in range(chans):
            row = c * slots + SUB * b
            v = w_ref[row : row + SUB, :]
            v = v + (w_ref[row + 1 : row + 1 + SUB, :] - v) * shares[b]
            p_ref[c * groups + b] = v
            top = v if top is None else jnp.maximum(top, v)
        total = picked = jnp.zeros((SUB, LANES), f32)
        for c in range(chans):
            v = p_ref[c * groups + b] - top
            picked = jnp.where(label == c, v, picked)
            v = jnp.exp2(v)
            p_ref[c * groups + b] = v
            total = total + v
        weight = jnp.where(label >= 0, 1.0, 0.0)
        loss = loss + weight * (jnp.log(total) - LN2 * picked)
        scale.append(weight / total)
        labels.append(label)
    for c in range(chans):
        parts = [[], []]
        for b in range(groups):
            g = p_ref[c * groups + b] * scale[b] - jnp.where(labels[b] == c, 1.0, 0.0)
            below = g * shares[b]
            parts[0].append(g - below)
            parts[1].append(below)
        for kind in range(2):
            g = jnp.concatenate(parts[kind], axis=0)
            hi = g.astype(bf16)
            at = (kind * chans + c) * tall
            lhs_ref[at : at + tall, 0:LANES] = hi
            lhs_ref[at : at + tall, LANES:] = (g - hi.astype(f32)).astype(bf16)
    return loss


def inner_kernel(rows, cols, chans, slots, groups, part, begin, tiles, *refs):
    (got_ref, lift_ref, lift_end_ref, next_ref, next_end_ref, back_ref, back_end_ref, lab_ref, mask_ref), refs = (
        refs[:9], refs[9:],
    )
    if part == 0:
        (x_ref, own_ref, fill_ref, sum_ref, loss_ref, stack_ref, floor_ref), refs = refs[:7], refs[7:]
    elif part == 1:
        (sum_in_ref, loss_in_ref, stack_ref, floor_ref, sum_ref, loss_ref), refs = refs[:6], refs[6:]
    else:
        (x_ref, beyond_ref, corner_ref, strip_ref, sum_in_ref, loss_in_ref), refs = refs[:6], refs[6:]
        (out_ref, spill_ref, loss_ref), refs = refs[:3], refs[3:]
    (w_ref, p_ref, s_ref, lhs_ref, tile_ref), refs = refs[:5], refs[5:]
    if part == 2:
        sum_ref, stack_ref, floor_ref = refs
    step = pl.program_id(0)
    steps = pl.num_programs(0)
    now = lax.rem(step, 2)
    which = lax.rem(step + begin, tiles)
    last_col = lax.axis_index("gx") == lax.axis_size("gx") - 1
    last_row = lax.axis_index("gy") == lax.axis_size("gy") - 1
    tall = rows * PATCH
    lane = lax.broadcasted_iota(jnp.int32, (SUB, LANES), 1)

    @pl.when(step == 0)
    def _():
        if part == 0:
            sum_ref[...] = jnp.zeros_like(sum_ref)
            loss_ref[...] = jnp.zeros_like(loss_ref)
        else:
            sum_ref[...] = sum_in_ref[...]
            loss_ref[...] = loss_in_ref[...]
        if part != 1:
            w_ref[0] = x_ref[...]
            w_ref[0, pl.ds(rows, chans, stride=slots), :] = got_ref[0:chans, :]
            if part == 2:
                wide = lax.broadcasted_iota(jnp.int32, (chans, LANES), 1)
                for i in range(rows + 1):
                    column = beyond_ref[0:chans, :] if i < rows else corner_ref[0:chans, :]
                    column = pltpu.roll(column, cols - i if i < rows else cols, 1)
                    pick = pl.ds(i, chans, stride=slots)
                    w_ref[0, pick, :] = jnp.where(wide == cols, column, w_ref[0, pick, :])
            full = w_ref[0]
            floor_ref[0] = jnp.min(full) * STEP
            stack_ref[...] = stack3(full)
        table = jnp.where(last_col, lift_end_ref[...], lift_ref[...])
        w_ref[0] = jnp.dot(stack_ref[...], table, preferred_element_type=f32)

    tile_ref[0:tall, :] = jnp.where(mask_ref[...] != 0, lab_ref[...], -1)
    tile_ref[tall : tall + SUB, :] = got_ref[pl.ds(pl.multiple_of(chans + which * SUB, SUB), SUB), :].astype(jnp.int32)

    if part == 2:

        @pl.when(which == 0)
        def _():
            for j in range(PATCH):
                for b in range(groups):
                    pick = pl.ds(b * SUB * PATCH + j, SUB, stride=PATCH)
                    strip = strip_ref[b * SUB : b * SUB + SUB, :]
                    strip = pltpu.roll(strip, LANES - j * HALF, 1) if j else strip
                    strip = jnp.where(last_col, -1.0, strip)
                    tile_ref[pick, :] = jnp.where(lane < HALF, strip.astype(jnp.int32), tile_ref[pick, :])
            for j in range(HALF):
                strip = corner_ref[chans : chans + 1, :]
                strip = pltpu.roll(strip, LANES - j * HALF, 1) if j else strip
                strip = jnp.where(last_col, -1.0, strip)
                row = tile_ref[tall + j : tall + j + 1, :]
                tile_ref[tall + j : tall + j + 1, :] = jnp.where(lane[0:1] < HALF, strip.astype(jnp.int32), row)

    flat = jnp.full((SUB, LANES), 1.0 / STEP, f32)
    sub = lax.broadcasted_iota(jnp.int32, (SUB, LANES), 0)
    fold = [flat] * (groups - 1) + [jnp.where(last_row & (sub == SUB - 1), 0.0, flat)]
    fast = floor_ref[0] >= FLOOR

    def prepare():
        table = jnp.where(last_col, next_end_ref[...], next_ref[...])
        w_ref[1 - now] = jnp.dot(stack_ref[...], table, preferred_element_type=f32)

    loss_ref[...] += pixels(groups, chans, slots, fold, tile_ref, fast, prepare, w_ref.at[now], p_ref, s_ref, lhs_ref)
    table = jnp.where(last_col, back_end_ref[...], back_ref[...])
    sum_ref[...] += jnp.dot(lhs_ref[...], table, preferred_element_type=f32)

    if part == 0:

        @pl.when((step == steps - 1) & (lax.axis_index("gx") == 0))
        def _():
            depth = stack_ref.shape[1]
            w_ref[1 - now] = jnp.dot(stack_ref[...], fill_ref[0:depth, :], preferred_element_type=f32)
            loss_ref[...] += first_columns(rows, groups, chans, slots, last_row, own_ref, got_ref, w_ref.at[1 - now], p_ref, lhs_ref)
            sum_ref[...] += jnp.dot(lhs_ref[...], fill_ref[depth:, :], preferred_element_type=f32)

    if part == 2:

        @pl.when(step == steps - 1)
        def _():
            w_ref[0] = jnp.zeros_like(w_ref[0])
            high = groups * SUB
            for c in range(chans):
                for kind in range(2):
                    at = (kind * chans + c) * high
                    row = c * slots + kind
                    w_ref[0, row : row + high, :] += sum_ref[at : at + high, :]
            out_ref[...] = w_ref[0] * (1.0 / STEP)
            spill_ref[...] = out_ref[pl.ds(rows, chans, stride=slots), :]


def grad_kernel(
    rows, cols, chans, slots, f_ref, beside_ref, g_ref, got_ref, loss_ref, count_ref, mine_ref, other_ref, sum_ref,
):
    row = lax.axis_index("gy")
    sum_ref[...] = g_ref[...]
    sum_ref[pl.ds(0, chans, stride=slots), :] += got_ref[...]
    lane = lax.broadcasted_iota(jnp.int32, (chans, LANES), 1)
    share = LANES // cols
    edge = jnp.zeros((chans, LANES), f32)
    tiles = []
    total = jnp.zeros((chans, LANES), f32)
    for k in range(0, rows, share):
        tile = None
        for r in range(share):
            piece = sum_ref[pl.ds(k + r, chans, stride=slots), :]
            total = total + piece
            edge = jnp.where(lane == k + r, pltpu.roll(piece, (k + r - cols) % LANES, 1), edge)
            if r:
                piece = pltpu.roll(piece, r * cols, 1)
            tile = piece if tile is None else jnp.where(lane < r * cols, tile, piece)
        tiles.append(tile.astype(bf16))
    block = f_ref[...].reshape(rows * cols, f_ref.shape[2])
    out = jnp.dot(jnp.concatenate(tiles, axis=1), block, preferred_element_type=f32)
    beside = jnp.concatenate([beside_ref[...], jnp.zeros((LANES - rows, f_ref.shape[2]), bf16)], axis=0)
    out = out + jnp.dot(edge.astype(bf16), beside, preferred_element_type=f32)
    total = jnp.where(lane <= cols, total, 0.0)
    square = jnp.concatenate([total, jnp.zeros((LANES - chans, LANES), f32)], axis=0)
    bias = jnp.sum(square.T, axis=0, keepdims=True)
    at = lax.broadcasted_iota(jnp.int32, (SUB, LANES), 0)
    rest = jnp.where(at == 1, jnp.sum(loss_ref[...]), count_ref[0, 0].astype(f32))
    stats = jnp.where(at == 0, bias, jnp.where(at < 3, rest, 0.0))
    pieces = out.shape[1] // LANES // 2
    for k in range(pieces):
        low = out[:, k * LANES : k * LANES + LANES]
        high = out[:, (pieces + k) * LANES : (pieces + k + 1) * LANES]
        mine_ref[k * chans : k * chans + chans, :] = jnp.where(row == 0, low, high)
        other_ref[k * chans : k * chans + chans, :] = jnp.where(row == 0, high, low)
    mine_ref[pieces * chans :, :] = stats
    other_ref[pieces * chans :, :] = stats


def final_kernel(chans, y_ref, z_ref, loss_ref, weight_ref, bias_ref):
    pieces = y_ref.shape[0] // chans
    lower = lax.axis_index("gy") == 0
    stats = y_ref[pieces * chans :, :]
    total = stats[2:3, 0:1]
    for k in range(pieces):
        y = y_ref[k * chans : k * chans + chans, :]
        z = z_ref[k * chans : k * chans + chans, :]
        weight_ref[:, k * LANES : k * LANES + LANES] = jnp.where(lower, y, z) / total
        weight_ref[:, (pieces + k) * LANES : (pieces + k + 1) * LANES] = jnp.where(lower, z, y) / total
    loss_ref[...] = stats[1:2, 0:1] / total
    bias_ref[...] = stats[0:1, 0:chans] / total


def body(features, probe_weight, probe_bias, labels, valid_mask, valid_count):
    rows, cols, width = features.shape
    chans = probe_weight.shape[1]
    gx, gy = lax.axis_size("gx"), lax.axis_size("gy")
    if gy != 2 or rows % SUB or 2 * cols != LANES or cols * PATCH % LANES or width % (2 * LANES) or gx & (gx - 1):
        raise ValueError("unsupported tile")
    groups = rows // SUB
    slots = rows + SUB
    count = groups * HALF
    tiles = cols * PATCH // LANES
    tall = rows * PATCH
    depth = 2 * LANES

    def forward(table):
        out = np.zeros((depth, table.shape[1]), np.float32)
        for k in range(3):
            out[k * cols : k * cols + cols] = table[:cols]
            out[3 * cols + k] = table[cols]
        return out

    def backward(table):
        out = np.zeros((table.shape[1] // LANES, 2, LANES, LANES), np.float32)
        out[:, :, :, : cols + 1] = table.T.reshape(-1, 1, LANES, cols + 1)
        return out.reshape(-1, LANES)

    inside, ending = column_tables(cols)
    lift, lift_end, back, back_end = (
        jnp.asarray(t, bf16) for t in (forward(inside), forward(ending), backward(inside), backward(ending))
    )

    fill = np.zeros((2 * depth, LANES), np.float32)
    fill[[0, cols, 2 * cols]] = STEP
    for part in (depth, depth + LANES):
        fill[part : part + PATCH * HALF, 0] = STEP
    fill = jnp.asarray(fill, bf16)

    shape = lambda *dims: jax.ShapeDtypeStruct(dims, f32)
    held = lambda *dims, kind=f32: pltpu.VMEM(dims, kind)
    far = lambda v: pltpu.with_memory_space_constraint(v, pltpu.HBM)
    here = lambda v: pltpu.with_memory_space_constraint(v, pltpu.VMEM)
    ring = lambda v, axis: lax.ppermute(v, axis, [(i, (i - 1) % lax.axis_size(axis)) for i in range(lax.axis_size(axis))])
    swap = lambda v: lax.ppermute(v, "gy", [(0, 1), (1, 0)])
    tall_x = chans * slots

    own, head, weight, shift = pl.pallas_call(
        functools.partial(pack_kernel, rows),
        in_specs=[ANY] * 5,
        out_specs=[VMEM] * 4,
        out_shape=[
            held(rows + rows * width // LANES, LANES), held(tiles * SUB, LANES), held(chans, width, kind=bf16),
            held(chans, LANES),
        ],
        scratch_shapes=[
            pltpu.VMEM((rows, SUB, width), bf16),
            pltpu.VMEM((2, tall, LANES), jnp.int32),
            pltpu.VMEM((2, SUB, tiles * LANES), jnp.int32),
            pltpu.VMEM((1, chans), f32),
            pltpu.SemaphoreType.DMA((7,)),
        ],
        compiler_params=ROOM,
        name="pack",
    )(*(far(v) for v in (features, labels, valid_mask, probe_weight.T, probe_bias.reshape(1, chans))))
    side = lax.ppermute(own, "gx", [(i, i - 1) for i in range(1, gx)])
    x, edge = pl.pallas_call(
        functools.partial(logits_kernel, rows, cols, chans, slots, 4),
        in_specs=[VMEM] * 5,
        out_specs=[VMEM] * 2,
        out_shape=[held(tall_x, LANES), held(chans + tiles * SUB + SUB, LANES)],
        compiler_params=ROOM,
        name="logits",
    )(*(here(v) for v in (features, weight, shift, head, own)))
    got = ring(edge, "gy")

    sums = (2 * chans * rows, LANES)
    stacked = held(tall_x, depth, kind=bf16)

    def inner(part, begin, steps, *args):
        at = lambda t: (t + begin) % tiles
        column = pl.BlockSpec((tall, LANES), lambda t: (0, at(t)))
        block = pl.BlockSpec((depth, LANES), lambda t: (0, at(t)))
        ahead = pl.BlockSpec((depth, LANES), lambda t: (0, at(t + 1)))
        rear = pl.BlockSpec((depth, LANES), lambda t: (at(t), 0))
        outs = [
            ([held(*sums), held(SUB, LANES), stacked, shape(1)], [VMEM] * 3 + [SMEM], [VMEM] * 3),
            ([held(*sums), held(SUB, LANES)], [VMEM] * 2, [VMEM] * 3 + [SMEM]),
            ([held(tall_x, LANES), held(chans, LANES), held(SUB, LANES)], [VMEM] * 3, [VMEM] * 6),
        ][part]
        return pl.pallas_call(
            functools.partial(inner_kernel, rows, cols, chans, slots, groups, part, begin, tiles),
            grid=(steps,),
            in_specs=[VMEM, block, block, ahead, ahead, rear, rear, column, column] + outs[2],
            out_specs=outs[1],
            out_shape=outs[0],
            scratch_shapes=[
                pltpu.VMEM((2, tall_x, LANES), f32),
                pltpu.VMEM((2 * chans * count, SUB, LANES), f32),
                pltpu.VMEM((2 * count + 1, SUB, LANES), f32),
                pltpu.VMEM((2 * chans * rows, depth), bf16),
                pltpu.VMEM((tall + SUB, LANES), jnp.int32),
            ] + ([pltpu.VMEM(sums, f32), stacked, pltpu.SMEM((1,), f32)] if part == 2 else []),
            cost_estimate=pl.CostEstimate(flops=10**9, bytes_accessed=2 * 10**6, transcendentals=10**6),
            compiler_params=ROOM,
            name=("inner_head", "inner_middle", "inner_tail")[part],
        )(here(got), lift, lift_end, lift, lift_end, back, back_end, labels, valid_mask, *args)

    middle = tiles // 2 + 1
    total, loss, stack, floor = inner(0, 1, middle - 1, here(x), here(own), fill)
    side, total = lax.optimization_barrier((side, total))
    beside, beyond = pl.pallas_call(
        functools.partial(beside_kernel, rows, chans),
        in_specs=[VMEM] * 3,
        out_specs=[VMEM] * 2,
        out_shape=[held(rows, width, kind=bf16), held(chans + SUB, LANES)],
        compiler_params=ROOM,
        name="beside",
    )(here(side), here(weight), here(shift))
    corner = ring(beyond, "gy")
    total, loss = inner(1, middle, tiles - 1 - middle, *(here(v) for v in (total, loss, stack)), floor)
    grad, spill, loss = inner(2, tiles - 1, 2, *(here(v) for v in (x, beyond, corner, side, total, loss)))
    got = lax.ppermute(spill, "gy", [(i, (i + 1) % gy) for i in range(gy)])
    pack = (chans * width // 2 // LANES + SUB, LANES)
    mine, other = pl.pallas_call(
        functools.partial(grad_kernel, rows, cols, chans, slots),
        in_specs=[VMEM] * 5 + [SMEM],
        out_specs=[VMEM] * 2,
        out_shape=[held(*pack)] * 2,
        scratch_shapes=[pltpu.VMEM((tall_x, LANES), f32)],
        compiler_params=ROOM,
        name="grad",
    )(*(here(v) for v in (features, beside, grad, got, loss)), valid_count)

    total = mine + swap(other)
    step = 1
    while step < gx:
        total = total + lax.ppermute(total, "gx", [(i, i ^ step) for i in range(gx)])
        step *= 2
    loss, weight, bias = pl.pallas_call(
        functools.partial(final_kernel, chans),
        in_specs=[VMEM] * 2,
        out_specs=[VMEM] * 3,
        out_shape=[shape(1, 1), shape(chans, width), shape(1, chans)],
        compiler_params=ROOM,
        name="final",
    )(here(total), here(swap(total)))
    return loss.reshape(1), weight.T, bias.reshape(chans)


def solution(mesh):
    return jax.shard_map(
        body,
        mesh=mesh,
        in_specs=(
            P(("groups", "gy"), "gx", None),
            P(),
            P(),
            P(("groups", "gy"), "gx"),
            P(("groups", "gy"), "gx"),
            P(("groups", "gy"), "gx"),
        ),
        out_specs=(P("groups"), P("groups", None), P("groups")),
        check_vma=False,
    )
```

```python
import functools
import math

import jax
import jax.numpy as jnp
import numpy as np
from jax import lax
from jax.experimental import pallas as pl
from jax.experimental.pallas import tpu as pltpu
from jax.sharding import PartitionSpec as P

PATCH = 14
HALF = PATCH // 2
STEP = 2 * PATCH
LANES = 128
SUB = 8
LOG2E = 1.0 / math.log(2.0)
LN2 = math.log(2.0)
FLOOR = -100.0
f32 = jnp.float32
bf16 = jnp.bfloat16
VMEM = pl.BlockSpec(memory_space=pltpu.VMEM)
ANY = pl.BlockSpec(memory_space=pl.ANY)
ROOM = pltpu.CompilerParams(vmem_limit_bytes=16 * 2**20)
SMEM = pl.BlockSpec(memory_space=pltpu.SMEM)


def whole(shape):
    return pl.BlockSpec(shape, lambda *ids: (0,) * len(shape))


def column_tables(cols):
    tables = np.zeros((2, cols + 1, cols * PATCH), np.float32)
    for q in range(cols * PATCH):
        i, k = divmod((q if q >= HALF else q + cols * PATCH) - HALF, PATCH)
        far = 2 * k + 1
        for end in range(2):
            if end and i == cols - 1:
                tables[end, i + (k >= HALF), q] = STEP
            else:
                tables[end, i, q] = STEP - far
                tables[end, i + 1, q] = far
    return tables


def split3(x):
    hi = x.astype(bf16)
    rest = x - hi.astype(f32)
    mid = rest.astype(bf16)
    return hi, mid, (rest - mid.astype(f32)).astype(bf16)


def stack3(x):
    cols = LANES // 2
    lane = lax.broadcasted_iota(jnp.int32, x.shape, 1)
    hi, mid, low = (part.astype(f32) for part in split3(x))
    first = jnp.where(lane < cols, hi, pltpu.roll(mid, cols, 1))
    second = jnp.where(lane == cols + 1, pltpu.roll(mid, 1, 1), pltpu.roll(low, 2, 1))
    second = jnp.where(lane == cols, hi, jnp.where(lane < cols + 3, second, 0.0))
    second = jnp.where(lane < cols, low, second)
    return jnp.concatenate([first.astype(bf16), second.astype(bf16)], axis=1)


def pack_kernel(
    rows, f_ref, lab_ref, mask_ref, w_ref, bias_ref, out_ref, head_ref, weight_ref, shift_ref, f_vmem, l_vmem, h_vmem, b_vmem, sem,
):
    width = f_vmem.shape[2]
    tiles = head_ref.shape[0] // SUB
    copies = [
        pltpu.make_async_copy(lab_ref.at[:, pl.ds(0, LANES)], l_vmem.at[0], sem.at[0]),
        pltpu.make_async_copy(mask_ref.at[:, pl.ds(0, LANES)], l_vmem.at[1], sem.at[1]),
        pltpu.make_async_copy(f_ref.at[:, pl.ds(0, SUB)], f_vmem, sem.at[2]),
        pltpu.make_async_copy(lab_ref.at[pl.ds(0, SUB)], h_vmem.at[0], sem.at[3]),
        pltpu.make_async_copy(mask_ref.at[pl.ds(0, SUB)], h_vmem.at[1], sem.at[4]),
        pltpu.make_async_copy(w_ref, weight_ref, sem.at[5]),
        pltpu.make_async_copy(bias_ref, b_vmem, sem.at[6]),
    ]
    for copy in copies:
        copy.start()
    at = lax.broadcasted_iota(jnp.int32, (SUB, LANES), 1)
    for copy in copies:
        copy.wait()
    for b in range(rows // SUB):
        strip = jnp.full((SUB, LANES), -1.0, f32)
        for j in range(PATCH):
            pick = pl.ds(b * SUB * PATCH + j, SUB, stride=PATCH)
            lab = jnp.where(l_vmem[1, pick, :] != 0, l_vmem[0, pick, :], -1).astype(f32)
            here = (at >= j * HALF) & (at < j * HALF + HALF)
            strip = jnp.where(here, pltpu.roll(lab, j * HALF, 1) if j else lab, strip)
        out_ref[b * SUB : b * SUB + SUB, :] = strip
    for i in range(rows):
        line = f_vmem[i].astype(f32)
        for k in range(width // LANES):
            out_ref[rows + k * rows + i : rows + k * rows + i + 1, :] = line[0:1, k * LANES : k * LANES + LANES]
    for t in range(tiles):
        lanes = slice(t * LANES, t * LANES + LANES)
        head_ref[t * SUB : t * SUB + SUB, :] = jnp.where(h_vmem[1, :, lanes] != 0, h_vmem[0, :, lanes], -1).astype(f32)
    chans = shift_ref.shape[0]
    bias = jnp.concatenate([b_vmem[...], jnp.zeros((1, LANES - chans), f32)], axis=1)
    shift_ref[...] = jnp.broadcast_to(bias, (LANES, LANES)).T[0:chans, :]


def score_of(w_ref, shift_ref, block):
    score = lax.dot_general(w_ref[...], block, (((1,), (1,)), ((), ())), preferred_element_type=f32)
    score = score + jnp.concatenate([shift_ref[...]] * (block.shape[0] // LANES), axis=1)
    return (score - jnp.max(score, axis=0, keepdims=True)) * (LOG2E / STEP)


def logits_kernel(rows, cols, chans, slots, per, f_ref, w_ref, shift_ref, head_ref, side_ref, x_ref, e_ref):
    x_ref[...] = jnp.zeros_like(x_ref)
    lane = lax.broadcasted_iota(jnp.int32, (chans, LANES), 1)
    for step in range(rows // per):
        score = score_of(w_ref, shift_ref, f_ref[step * per : step * per + per].reshape(per * cols, f_ref.shape[2]))
        for k in range(per):
            i, off = step * per + k, k * cols
            tile = score[:, off // LANES * LANES : off // LANES * LANES + LANES]
            if off % LANES:
                tile = pltpu.roll(tile, LANES - off % LANES, 1)
            tile = jnp.where(lane < cols, tile, 0.0)
            x_ref[pl.ds(i, chans, stride=slots), :] = tile
            if i == 0:
                e_ref[0:chans, :] = tile
    e_ref[chans : chans + head_ref.shape[0], :] = head_ref[...]
    e_ref[chans + head_ref.shape[0] :, :] = side_ref[0:SUB, :]


def beside_kernel(rows, chans, side_ref, w_ref, shift_ref, beside_ref, out_ref):
    width = w_ref.shape[1]
    side = jnp.concatenate(
        [side_ref[rows + k * rows : rows + k * rows + rows, :] for k in range(width // LANES)], axis=1
    ).astype(bf16)
    beside_ref[...] = side
    side = jnp.concatenate([side, jnp.zeros((LANES - rows, width), bf16)], axis=0)
    out_ref[0:chans, :] = score_of(w_ref, shift_ref, side)
    out_ref[chans:, :] = side_ref[0:SUB, :]


def softmax_fast(groups, chans, slots, fold, w_ref, p_ref):
    sums = [None] * (2 * groups * HALF)
    for c in range(chans):
        for b in range(groups):
            row = c * slots + SUB * b
            upper = w_ref[row : row + SUB, :]
            lower = w_ref[row + 1 : row + 1 + SUB, :]
            slope = (lower - upper) * fold[b]
            twice = slope + slope
            for half, (p, ratio) in enumerate(((upper + slope, twice), (lower - slope, -twice))):
                p, ratio = jnp.exp2(p), jnp.exp2(ratio)
                for m in range(HALF):
                    k = (half * groups + b) * HALF + m
                    if m:
                        p = p * ratio
                    p_ref[c * len(sums) + k] = p
                    sums[k] = p if sums[k] is None else sums[k] + p
    return sums


def softmax_slow(groups, chans, slots, fold, w_ref, p_ref, labels, weights):
    count = len(labels)
    sums, losses = [], jnp.zeros((SUB, LANES), f32)
    for k in range(count):
        half, b, m = k // (groups * HALF), k // HALF % groups, k % HALF

        def score(c, half=half, b=b, m=m):
            row = c * slots + SUB * b
            near = w_ref[pl.ds(row + half, SUB), :]
            away = w_ref[pl.ds(row + 1 - half, SUB), :]
            return near + (away - near) * fold[b] * (2 * m + 1.0)

        top = lax.fori_loop(1, chans, lambda c, t, score=score: jnp.maximum(t, score(c)), score(0))

        def take(c, carry, k=k, top=top, score=score):
            total, picked = carry
            shifted = score(c) - top
            p = jnp.exp2(shifted)
            p_ref[c * count + k] = p
            return total + p, jnp.where(labels[k] == c, shifted, picked)

        zero = jnp.zeros((SUB, LANES), f32)
        total, picked = lax.fori_loop(0, chans, take, (zero, zero))
        sums.append(total)
        losses = losses - weights[k] * picked
    return sums, losses


def pixels(groups, chans, slots, fold, lab_ref, fast, prepare, w_ref, p_ref, s_ref, lhs_ref):
    count = 2 * groups * HALF
    labels = []
    for half in range(2):
        for b in range(groups):
            for m in range(HALF):
                k = PATCH - 1 - m if half else m
                labels.append(lab_ref[pl.ds(b * SUB * PATCH + HALF + k, SUB, stride=PATCH), :])
    weights = [jnp.where(lab >= 0, 1.0, 0.0) for lab in labels]

    @pl.when(fast)
    def _():
        sums = softmax_fast(groups, chans, slots, fold, w_ref, p_ref)
        for k in range(count):
            s_ref[k] = sums[k]
        s_ref[count] = jnp.zeros((SUB, LANES), f32)
        prepare()

    @pl.when(jnp.logical_not(fast))
    def _():
        sums, losses = softmax_slow(groups, chans, slots, fold, w_ref, p_ref, labels, weights)
        for k in range(count):
            s_ref[k] = sums[k]
        s_ref[count] = losses
        prepare()

    loss = jnp.zeros((SUB, LANES), f32)
    scale = []
    for k in range(count):
        total = s_ref[k]
        loss = loss + weights[k] * jnp.log(total)
        scale.append(weights[k] / total)
    packed = [
        jnp.concatenate([labels[(half * groups + b) * HALF + m] for b in range(groups)], axis=0).astype(f32).astype(bf16)
        for half in range(2)
        for m in range(HALF)
    ]
    one, none, mid = (jnp.asarray(v, bf16) for v in (1, 0, 0.5))
    picked = jnp.zeros((SUB, LANES), f32)
    tall = groups * SUB

    def two_sums(item):
        totals, runs = [], []
        for half in range(2):
            total = run = None
            for m in reversed(range(HALF)):
                v = item(half, m)
                total = v if total is None else total + v
                if m:
                    run = total if run is None else run + total
            totals.append(total)
            runs.append(run)
        return totals[0], totals[1], runs[0] - runs[1], totals[0] - totals[1]

    for c in range(chans):
        mark = jnp.asarray(c, bf16)
        up, down, run, lean = two_sums(lambda half, m: jnp.where(packed[half * HALF + m] == mark, one, none))
        hits = [v.astype(f32) for v in (up, down, run + lean * mid)]
        parts = [[], []]
        for b in range(groups):
            row = c * slots + SUB * b
            up, down, lean = (v[b * SUB : b * SUB + SUB] for v in hits)
            lean = lean * (fold[b] * 2.0)
            up, down = up - lean, down + lean
            picked = picked + up * w_ref[row : row + SUB, :] + down * w_ref[row + 1 : row + 1 + SUB, :]
            above, below, run, lean = two_sums(
                lambda half, m: p_ref[c * count + (half * groups + b) * HALF + m] * scale[(half * groups + b) * HALF + m]
            )
            lean = (run + lean * 0.5) * (fold[b] * 2.0)
            parts[0].append((above - up) - lean)
            parts[1].append((below - down) + lean)
        for kind in range(2):
            g = jnp.concatenate(parts[kind], axis=0)
            hi = g.astype(bf16)
            at = (kind * chans + c) * tall
            lhs_ref[at : at + tall, 0:LANES] = hi
            lhs_ref[at : at + tall, LANES:] = (g - hi.astype(f32)).astype(bf16)
    return loss + LN2 * jnp.where(fast, -picked, s_ref[count])


def first_columns(rows, groups, chans, slots, last_row, own_ref, got_ref, w_ref, p_ref, lhs_ref):
    lane = lax.broadcasted_iota(jnp.int32, (SUB, LANES), 1)
    sub = lax.broadcasted_iota(jnp.int32, (SUB, LANES), 0)
    turn = HALF * HALF
    share = jnp.zeros((SUB, LANES), f32)
    for k in range(PATCH):
        share = jnp.where(lane >= k * HALF, (2 * k + 1.0) / STEP, share)
    end = jnp.where(last_row & (sub == SUB - 1), jnp.where(lane < turn, 0.0, 1.0), share)
    shares = [share] * (groups - 1) + [end]
    tall = groups * SUB
    loss = jnp.zeros((SUB, LANES), f32)
    scale, labels = [], []
    for b in range(groups):
        upper = own_ref[b * SUB : b * SUB + SUB, :]
        at = (b + 1) * SUB
        lower = got_ref[got_ref.shape[0] - SUB :, :] if at == rows else own_ref[at : at + SUB, :]
        lower = jnp.where(sub == SUB - 1, pltpu.roll(lower, SUB - 1, 0), pltpu.roll(upper, SUB - 1, 0))
        label = jnp.where(lane < turn, pltpu.roll(upper, LANES - turn, 1), pltpu.roll(lower, turn, 1))
        label = jnp.where(lane < PATCH * HALF, label, -1.0).astype(jnp.int32)
        top = None
        for c in range(chans):
            row = c * slots + SUB * b
            v = w_ref[row : row + SUB, :]
            v = v + (w_ref[row + 1 : row + 1 + SUB, :] - v) * shares[b]
            p_ref[c * groups + b] = v
            top = v if top is None else jnp.maximum(top, v)
        total = picked = jnp.zeros((SUB, LANES), f32)
        for c in range(chans):
            v = p_ref[c * groups + b] - top
            picked = jnp.where(label == c, v, picked)
            v = jnp.exp2(v)
            p_ref[c * groups + b] = v
            total = total + v
        weight = jnp.where(label >= 0, 1.0, 0.0)
        loss = loss + weight * (jnp.log(total) - LN2 * picked)
        scale.append(weight / total)
        labels.append(label)
    for c in range(chans):
        parts = [[], []]
        for b in range(groups):
            g = p_ref[c * groups + b] * scale[b] - jnp.where(labels[b] == c, 1.0, 0.0)
            below = g * shares[b]
            parts[0].append(g - below)
            parts[1].append(below)
        for kind in range(2):
            g = jnp.concatenate(parts[kind], axis=0)
            hi = g.astype(bf16)
            at = (kind * chans + c) * tall
            lhs_ref[at : at + tall, 0:LANES] = hi
            lhs_ref[at : at + tall, LANES:] = (g - hi.astype(f32)).astype(bf16)
    return loss


def inner_kernel(rows, cols, chans, slots, groups, part, begin, tiles, *refs):
    (got_ref, lift_ref, lift_end_ref, back_ref, back_end_ref, lab_ref, mask_ref), refs = refs[:7], refs[7:]
    if part == 0:
        (x_ref, own_ref, fill_ref, sum_ref, loss_ref, stack_ref, floor_ref), refs = refs[:7], refs[7:]
    elif part == 1:
        (sum_in_ref, loss_in_ref, stack_ref, floor_ref, sum_ref, loss_ref), refs = refs[:6], refs[6:]
    else:
        (x_ref, beyond_ref, corner_ref, strip_ref, sum_in_ref, loss_in_ref), refs = refs[:6], refs[6:]
        (out_ref, spill_ref, loss_ref), refs = refs[:3], refs[3:]
    (w_ref, p_ref, s_ref, lhs_ref, tile_ref), refs = refs[:5], refs[5:]
    if part == 2:
        sum_ref, stack_ref, floor_ref = refs
    step = pl.program_id(0)
    steps = pl.num_programs(0)
    now = lax.rem(step, 2)
    which = lax.rem(step + begin, tiles)
    last_col = lax.axis_index("gx") == lax.axis_size("gx") - 1
    last_row = lax.axis_index("gy") == lax.axis_size("gy") - 1
    tall = rows * PATCH
    lane = lax.broadcasted_iota(jnp.int32, (SUB, LANES), 1)
    lanes = pl.ds(pl.multiple_of(which * LANES, LANES), LANES)

    def lift(at):
        lanes = pl.ds(pl.multiple_of(at * LANES, LANES), LANES)
        table = jnp.where(last_col, lift_end_ref[:, lanes], lift_ref[:, lanes])
        return jnp.dot(stack_ref[...], table, preferred_element_type=f32)

    @pl.when(step == 0)
    def _():
        if part == 0:
            sum_ref[...] = jnp.zeros_like(sum_ref)
            loss_ref[...] = jnp.zeros_like(loss_ref)
        else:
            sum_ref[...] = sum_in_ref[...]
            loss_ref[...] = loss_in_ref[...]
        if part != 1:
            w_ref[0] = x_ref[...]
            w_ref[0, pl.ds(rows, chans, stride=slots), :] = got_ref[0:chans, :]
            if part == 2:
                wide = lax.broadcasted_iota(jnp.int32, (chans, LANES), 1)
                for i in range(rows + 1):
                    column = beyond_ref[0:chans, :] if i < rows else corner_ref[0:chans, :]
                    column = pltpu.roll(column, cols - i if i < rows else cols, 1)
                    pick = pl.ds(i, chans, stride=slots)
                    w_ref[0, pick, :] = jnp.where(wide == cols, column, w_ref[0, pick, :])
            full = w_ref[0]
            floor_ref[0] = jnp.min(full) * STEP
            stack_ref[...] = stack3(full)
        w_ref[0] = lift(which)

    tile_ref[0:tall, :] = jnp.where(mask_ref[:, lanes] != 0, lab_ref[:, lanes], -1)
    tile_ref[tall : tall + SUB, :] = got_ref[pl.ds(pl.multiple_of(chans + which * SUB, SUB), SUB), :].astype(jnp.int32)

    if part == 2:

        @pl.when(which == 0)
        def _():
            for j in range(PATCH):
                for b in range(groups):
                    pick = pl.ds(b * SUB * PATCH + j, SUB, stride=PATCH)
                    strip = strip_ref[b * SUB : b * SUB + SUB, :]
                    strip = pltpu.roll(strip, LANES - j * HALF, 1) if j else strip
                    strip = jnp.where(last_col, -1.0, strip)
                    tile_ref[pick, :] = jnp.where(lane < HALF, strip.astype(jnp.int32), tile_ref[pick, :])
            for j in range(HALF):
                strip = corner_ref[chans : chans + 1, :]
                strip = pltpu.roll(strip, LANES - j * HALF, 1) if j else strip
                strip = jnp.where(last_col, -1.0, strip)
                row = tile_ref[tall + j : tall + j + 1, :]
                tile_ref[tall + j : tall + j + 1, :] = jnp.where(lane[0:1] < HALF, strip.astype(jnp.int32), row)

    flat = jnp.full((SUB, LANES), 1.0 / STEP, f32)
    sub = lax.broadcasted_iota(jnp.int32, (SUB, LANES), 0)
    fold = [flat] * (groups - 1) + [jnp.where(last_row & (sub == SUB - 1), 0.0, flat)]
    fast = floor_ref[0] >= FLOOR

    def prepare():
        w_ref[1 - now] = lift(lax.rem(which + 1, tiles))

    loss_ref[...] += pixels(groups, chans, slots, fold, tile_ref, fast, prepare, w_ref.at[now], p_ref, s_ref, lhs_ref)
    depth = 2 * LANES
    deep = pl.ds(pl.multiple_of(which * depth, depth), depth)
    table = jnp.where(last_col, back_end_ref[deep, :], back_ref[deep, :])
    sum_ref[...] += jnp.dot(lhs_ref[...], table, preferred_element_type=f32)

    if part == 0:

        @pl.when((step == steps - 1) & (lax.axis_index("gx") == 0))
        def _():
            depth = stack_ref.shape[1]
            w_ref[1 - now] = jnp.dot(stack_ref[...], fill_ref[0:depth, :], preferred_element_type=f32)
            loss_ref[...] += first_columns(rows, groups, chans, slots, last_row, own_ref, got_ref, w_ref.at[1 - now], p_ref, lhs_ref)
            sum_ref[...] += jnp.dot(lhs_ref[...], fill_ref[depth:, :], preferred_element_type=f32)

    if part == 2:

        @pl.when(step == steps - 1)
        def _():
            w_ref[0] = jnp.zeros_like(w_ref[0])
            high = groups * SUB
            for c in range(chans):
                for kind in range(2):
                    at = (kind * chans + c) * high
                    row = c * slots + kind
                    w_ref[0, row : row + high, :] += sum_ref[at : at + high, :]
            out_ref[...] = w_ref[0] * (1.0 / STEP)
            spill_ref[...] = out_ref[pl.ds(rows, chans, stride=slots), :]


def grad_kernel(
    rows, cols, chans, slots, f_ref, beside_ref, g_ref, got_ref, loss_ref, count_ref, mine_ref, other_ref, sum_ref,
):
    row = lax.axis_index("gy")
    sum_ref[...] = g_ref[...]
    sum_ref[pl.ds(0, chans, stride=slots), :] += got_ref[...]
    lane = lax.broadcasted_iota(jnp.int32, (chans, LANES), 1)
    share = LANES // cols
    edge = jnp.zeros((chans, LANES), f32)
    tiles = []
    total = jnp.zeros((chans, LANES), f32)
    for k in range(0, rows, share):
        tile = None
        for r in range(share):
            piece = sum_ref[pl.ds(k + r, chans, stride=slots), :]
            total = total + piece
            edge = jnp.where(lane == k + r, pltpu.roll(piece, (k + r - cols) % LANES, 1), edge)
            if r:
                piece = pltpu.roll(piece, r * cols, 1)
            tile = piece if tile is None else jnp.where(lane < r * cols, tile, piece)
        tiles.append(tile.astype(bf16))
    block = f_ref[...].reshape(rows * cols, f_ref.shape[2])
    out = jnp.dot(jnp.concatenate(tiles, axis=1), block, preferred_element_type=f32)
    beside = jnp.concatenate([beside_ref[...], jnp.zeros((LANES - rows, f_ref.shape[2]), bf16)], axis=0)
    out = out + jnp.dot(edge.astype(bf16), beside, preferred_element_type=f32)
    total = jnp.where(lane <= cols, total, 0.0)
    square = jnp.concatenate([total, jnp.zeros((LANES - chans, LANES), f32)], axis=0)
    bias = jnp.sum(square.T, axis=0, keepdims=True)
    at = lax.broadcasted_iota(jnp.int32, (SUB, LANES), 0)
    rest = jnp.where(at == 1, jnp.sum(loss_ref[...]), count_ref[0, 0].astype(f32))
    stats = jnp.where(at == 0, bias, jnp.where(at < 3, rest, 0.0))
    pieces = out.shape[1] // LANES // 2
    for k in range(pieces):
        low = out[:, k * LANES : k * LANES + LANES]
        high = out[:, (pieces + k) * LANES : (pieces + k + 1) * LANES]
        mine_ref[k * chans : k * chans + chans, :] = jnp.where(row == 0, low, high)
        other_ref[k * chans : k * chans + chans, :] = jnp.where(row == 0, high, low)
    mine_ref[pieces * chans :, :] = stats
    other_ref[pieces * chans :, :] = stats


def final_kernel(chans, y_ref, z_ref, loss_ref, weight_ref, bias_ref):
    pieces = y_ref.shape[0] // chans
    lower = lax.axis_index("gy") == 0
    stats = y_ref[pieces * chans :, :]
    total = stats[2:3, 0:1]
    for k in range(pieces):
        y = y_ref[k * chans : k * chans + chans, :]
        z = z_ref[k * chans : k * chans + chans, :]
        weight_ref[:, k * LANES : k * LANES + LANES] = jnp.where(lower, y, z) / total
        weight_ref[:, (pieces + k) * LANES : (pieces + k + 1) * LANES] = jnp.where(lower, z, y) / total
    loss_ref[...] = stats[1:2, 0:1] / total
    bias_ref[...] = stats[0:1, 0:chans] / total


def body(features, probe_weight, probe_bias, labels, valid_mask, valid_count):
    rows, cols, width = features.shape
    chans = probe_weight.shape[1]
    gx, gy = lax.axis_size("gx"), lax.axis_size("gy")
    if gy != 2 or rows % SUB or 2 * cols != LANES or cols * PATCH % LANES or width % (2 * LANES) or gx & (gx - 1):
        raise ValueError("unsupported tile")
    groups = rows // SUB
    slots = rows + SUB
    count = groups * HALF
    tiles = cols * PATCH // LANES
    tall = rows * PATCH
    depth = 2 * LANES

    def forward(table):
        out = np.zeros((depth, table.shape[1]), np.float32)
        for k in range(3):
            out[k * cols : k * cols + cols] = table[:cols]
            out[3 * cols + k] = table[cols]
        return out

    def backward(table):
        out = np.zeros((table.shape[1] // LANES, 2, LANES, LANES), np.float32)
        out[:, :, :, : cols + 1] = table.T.reshape(-1, 1, LANES, cols + 1)
        return out.reshape(-1, LANES)

    inside, ending = column_tables(cols)
    lift, lift_end, back, back_end = (
        jnp.asarray(t, bf16) for t in (forward(inside), forward(ending), backward(inside), backward(ending))
    )

    fill = np.zeros((2 * depth, LANES), np.float32)
    fill[[0, cols, 2 * cols]] = STEP
    for part in (depth, depth + LANES):
        fill[part : part + PATCH * HALF, 0] = STEP
    fill = jnp.asarray(fill, bf16)

    shape = lambda *dims: jax.ShapeDtypeStruct(dims, f32)
    held = lambda *dims, kind=f32: pltpu.VMEM(dims, kind)
    far = lambda v: pltpu.with_memory_space_constraint(v, pltpu.HBM)
    here = lambda v: pltpu.with_memory_space_constraint(v, pltpu.VMEM)
    ring = lambda v, axis: lax.ppermute(v, axis, [(i, (i - 1) % lax.axis_size(axis)) for i in range(lax.axis_size(axis))])
    swap = lambda v: lax.ppermute(v, "gy", [(0, 1), (1, 0)])
    tall_x = chans * slots

    own, head, weight, shift = pl.pallas_call(
        functools.partial(pack_kernel, rows),
        in_specs=[ANY] * 5,
        out_specs=[VMEM] * 4,
        out_shape=[
            held(rows + rows * width // LANES, LANES), held(tiles * SUB, LANES), held(chans, width, kind=bf16),
            held(chans, LANES),
        ],
        scratch_shapes=[
            pltpu.VMEM((rows, SUB, width), bf16),
            pltpu.VMEM((2, tall, LANES), jnp.int32),
            pltpu.VMEM((2, SUB, tiles * LANES), jnp.int32),
            pltpu.VMEM((1, chans), f32),
            pltpu.SemaphoreType.DMA((7,)),
        ],
        compiler_params=ROOM,
        name="pack",
    )(*(far(v) for v in (features, labels, valid_mask, probe_weight.T, probe_bias.reshape(1, chans))))
    side = lax.ppermute(own, "gx", [(i, i - 1) for i in range(1, gx)])
    x, edge = pl.pallas_call(
        functools.partial(logits_kernel, rows, cols, chans, slots, 4),
        in_specs=[VMEM] * 5,
        out_specs=[VMEM] * 2,
        out_shape=[held(tall_x, LANES), held(chans + tiles * SUB + SUB, LANES)],
        compiler_params=ROOM,
        name="logits",
    )(*(here(v) for v in (features, weight, shift, head, own)))
    got = ring(edge, "gy")

    sums = (2 * chans * rows, LANES)
    stacked = held(tall_x, depth, kind=bf16)

    def inner(part, begin, steps, *args):
        outs = [
            ([held(*sums), held(SUB, LANES), stacked, shape(1)], [VMEM] * 3 + [SMEM], [VMEM] * 3),
            ([held(*sums), held(SUB, LANES)], [VMEM] * 2, [VMEM] * 3 + [SMEM]),
            ([held(tall_x, LANES), held(chans, LANES), held(SUB, LANES)], [VMEM] * 3, [VMEM] * 6),
        ][part]
        return pl.pallas_call(
            functools.partial(inner_kernel, rows, cols, chans, slots, groups, part, begin, tiles),
            grid=(steps,),
            in_specs=[VMEM] * 7 + outs[2],
            out_specs=outs[1],
            out_shape=outs[0],
            scratch_shapes=[
                pltpu.VMEM((2, tall_x, LANES), f32),
                pltpu.VMEM((2 * chans * count, SUB, LANES), f32),
                pltpu.VMEM((2 * count + 1, SUB, LANES), f32),
                pltpu.VMEM((2 * chans * rows, depth), bf16),
                pltpu.VMEM((tall + SUB, LANES), jnp.int32),
            ] + ([pltpu.VMEM(sums, f32), stacked, pltpu.SMEM((1,), f32)] if part == 2 else []),
            cost_estimate=pl.CostEstimate(flops=10**9, bytes_accessed=2 * 10**6, transcendentals=10**6),
            compiler_params=ROOM,
            name=("inner_head", "inner_middle", "inner_tail")[part],
        )(*(here(v) for v in (got, lift, lift_end, back, back_end, labels, valid_mask)), *args)

    middle = tiles // 2 + 1
    total, loss, stack, floor = inner(0, 1, middle - 1, here(x), here(own), here(fill))
    side, total = lax.optimization_barrier((side, total))
    beside, beyond = pl.pallas_call(
        functools.partial(beside_kernel, rows, chans),
        in_specs=[VMEM] * 3,
        out_specs=[VMEM] * 2,
        out_shape=[held(rows, width, kind=bf16), held(chans + SUB, LANES)],
        compiler_params=ROOM,
        name="beside",
    )(here(side), here(weight), here(shift))
    corner = ring(beyond, "gy")
    total, loss = inner(1, middle, tiles - 1 - middle, *(here(v) for v in (total, loss, stack)), floor)
    grad, spill, loss = inner(2, tiles - 1, 2, *(here(v) for v in (x, beyond, corner, side, total, loss)))
    got = lax.ppermute(spill, "gy", [(i, (i + 1) % gy) for i in range(gy)])
    pack = (chans * width // 2 // LANES + SUB, LANES)
    mine, other = pl.pallas_call(
        functools.partial(grad_kernel, rows, cols, chans, slots),
        in_specs=[VMEM] * 5 + [SMEM],
        out_specs=[VMEM] * 2,
        out_shape=[held(*pack)] * 2,
        scratch_shapes=[pltpu.VMEM((tall_x, LANES), f32)],
        compiler_params=ROOM,
        name="grad",
    )(*(here(v) for v in (features, beside, grad, got, loss)), valid_count)

    total = mine + swap(other)
    step = 1
    while step < gx:
        total = total + lax.ppermute(total, "gx", [(i, i ^ step) for i in range(gx)])
        step *= 2
    loss, weight, bias = pl.pallas_call(
        functools.partial(final_kernel, chans),
        in_specs=[VMEM] * 2,
        out_specs=[VMEM] * 3,
        out_shape=[shape(1, 1), shape(chans, width), shape(1, chans)],
        compiler_params=ROOM,
        name="final",
    )(here(total), here(swap(total)))
    return loss.reshape(1), weight.T, bias.reshape(chans)


def solution(mesh):
    return jax.shard_map(
        body,
        mesh=mesh,
        in_specs=(
            P(("groups", "gy"), "gx", None),
            P(),
            P(),
            P(("groups", "gy"), "gx"),
            P(("groups", "gy"), "gx"),
            P(("groups", "gy"), "gx"),
        ),
        out_specs=(P("groups"), P("groups", None), P("groups")),
        check_vma=False,
    )
```

```python
import functools
import math

import jax
import jax.numpy as jnp
import numpy as np
from jax import lax
from jax.experimental import pallas as pl
from jax.experimental.pallas import tpu as pltpu
from jax.sharding import PartitionSpec as P

PATCH = 14
HALF = PATCH // 2
STEP = 2 * PATCH
LANES = 128
SUB = 8
LOG2E = 1.0 / math.log(2.0)
LN2 = math.log(2.0)
FLOOR = -100.0
f32 = jnp.float32
bf16 = jnp.bfloat16
VMEM = pl.BlockSpec(memory_space=pltpu.VMEM)
ANY = pl.BlockSpec(memory_space=pl.ANY)
ROOM = pltpu.CompilerParams(vmem_limit_bytes=16 * 2**20)
SMEM = pl.BlockSpec(memory_space=pltpu.SMEM)


def whole(shape):
    return pl.BlockSpec(shape, lambda *ids: (0,) * len(shape))


def column_tables(cols):
    tables = np.zeros((2, cols + 1, cols * PATCH), np.float32)
    for q in range(cols * PATCH):
        i, k = divmod((q if q >= HALF else q + cols * PATCH) - HALF, PATCH)
        far = 2 * k + 1
        for end in range(2):
            if end and i == cols - 1:
                tables[end, i + (k >= HALF), q] = STEP
            else:
                tables[end, i, q] = STEP - far
                tables[end, i + 1, q] = far
    return tables


def split3(x):
    hi = x.astype(bf16)
    rest = x - hi.astype(f32)
    mid = rest.astype(bf16)
    return hi, mid, (rest - mid.astype(f32)).astype(bf16)


def stack3(x):
    cols = LANES // 2
    lane = lax.broadcasted_iota(jnp.int32, x.shape, 1)
    hi, mid, low = (part.astype(f32) for part in split3(x))
    first = jnp.where(lane < cols, hi, pltpu.roll(mid, cols, 1))
    second = jnp.where(lane == cols + 1, pltpu.roll(mid, 1, 1), pltpu.roll(low, 2, 1))
    second = jnp.where(lane == cols, hi, jnp.where(lane < cols + 3, second, 0.0))
    second = jnp.where(lane < cols, low, second)
    return jnp.concatenate([first.astype(bf16), second.astype(bf16)], axis=1)


def pack_kernel(
    rows, f_ref, lab_ref, mask_ref, w_ref, bias_ref, out_ref, head_ref, weight_ref, shift_ref, f_vmem, l_vmem, h_vmem, b_vmem, sem,
):
    width = f_vmem.shape[2]
    tiles = head_ref.shape[0] // SUB
    copies = [
        pltpu.make_async_copy(lab_ref.at[:, pl.ds(0, LANES)], l_vmem.at[0], sem.at[0]),
        pltpu.make_async_copy(mask_ref.at[:, pl.ds(0, LANES)], l_vmem.at[1], sem.at[1]),
        pltpu.make_async_copy(f_ref.at[:, pl.ds(0, SUB)], f_vmem, sem.at[2]),
        pltpu.make_async_copy(lab_ref.at[pl.ds(0, SUB)], h_vmem.at[0], sem.at[3]),
        pltpu.make_async_copy(mask_ref.at[pl.ds(0, SUB)], h_vmem.at[1], sem.at[4]),
        pltpu.make_async_copy(w_ref, weight_ref, sem.at[5]),
        pltpu.make_async_copy(bias_ref, b_vmem, sem.at[6]),
    ]
    for copy in copies:
        copy.start()
    at = lax.broadcasted_iota(jnp.int32, (SUB, LANES), 1)
    for copy in copies:
        copy.wait()
    for b in range(rows // SUB):
        strip = jnp.full((SUB, LANES), -1.0, f32)
        for j in range(PATCH):
            pick = pl.ds(b * SUB * PATCH + j, SUB, stride=PATCH)
            lab = jnp.where(l_vmem[1, pick, :] != 0, l_vmem[0, pick, :], -1).astype(f32)
            here = (at >= j * HALF) & (at < j * HALF + HALF)
            strip = jnp.where(here, pltpu.roll(lab, j * HALF, 1) if j else lab, strip)
        out_ref[b * SUB : b * SUB + SUB, :] = strip
    for i in range(rows):
        line = f_vmem[i].astype(f32)
        for k in range(width // LANES):
            out_ref[rows + k * rows + i : rows + k * rows + i + 1, :] = line[0:1, k * LANES : k * LANES + LANES]
    for t in range(tiles):
        lanes = slice(t * LANES, t * LANES + LANES)
        head_ref[t * SUB : t * SUB + SUB, :] = jnp.where(h_vmem[1, :, lanes] != 0, h_vmem[0, :, lanes], -1).astype(f32)
    chans = shift_ref.shape[0]
    bias = jnp.concatenate([b_vmem[...], jnp.zeros((1, LANES - chans), f32)], axis=1)
    shift_ref[...] = jnp.broadcast_to(bias, (LANES, LANES)).T[0:chans, :]


def score_of(w_ref, shift_ref, block):
    score = lax.dot_general(w_ref[...], block, (((1,), (1,)), ((), ())), preferred_element_type=f32)
    score = score + jnp.concatenate([shift_ref[...]] * (block.shape[0] // LANES), axis=1)
    return (score - jnp.max(score, axis=0, keepdims=True)) * (LOG2E / STEP)


def logits_kernel(rows, cols, chans, slots, per, f_ref, w_ref, shift_ref, head_ref, side_ref, x_ref, e_ref):
    x_ref[...] = jnp.zeros_like(x_ref)
    lane = lax.broadcasted_iota(jnp.int32, (chans, LANES), 1)
    for step in range(rows // per):
        score = score_of(w_ref, shift_ref, f_ref[step * per : step * per + per].reshape(per * cols, f_ref.shape[2]))
        for k in range(per):
            i, off = step * per + k, k * cols
            tile = score[:, off // LANES * LANES : off // LANES * LANES + LANES]
            if off % LANES:
                tile = pltpu.roll(tile, LANES - off % LANES, 1)
            tile = jnp.where(lane < cols, tile, 0.0)
            x_ref[pl.ds(i, chans, stride=slots), :] = tile
            if i == 0:
                e_ref[0:chans, :] = tile
    e_ref[chans : chans + head_ref.shape[0], :] = head_ref[...]
    e_ref[chans + head_ref.shape[0] :, :] = side_ref[0:SUB, :]


def beside_kernel(rows, chans, side_ref, w_ref, shift_ref, beside_ref, out_ref):
    width = w_ref.shape[1]
    side = jnp.concatenate(
        [side_ref[rows + k * rows : rows + k * rows + rows, :] for k in range(width // LANES)], axis=1
    ).astype(bf16)
    beside_ref[...] = side
    side = jnp.concatenate([side, jnp.zeros((LANES - rows, width), bf16)], axis=0)
    out_ref[0:chans, :] = score_of(w_ref, shift_ref, side)
    out_ref[chans:, :] = side_ref[0:SUB, :]


def two_sums(item):
    totals, runs = [], []
    for half in range(2):
        total = run = None
        for m in reversed(range(HALF)):
            v = item(half, m)
            total = v if total is None else total + v
            if m:
                run = total if run is None else run + total
        totals.append(total)
        runs.append(run)
    return totals[0], totals[1], runs[0] - runs[1], totals[0] - totals[1]


def tally(packed, c, h_ref):
    one, none, mid = (jnp.asarray(v, bf16) for v in (1, 0, 0.5))
    mark = jnp.asarray(c, bf16) if isinstance(c, int) else c.astype(f32).astype(bf16)
    up, down, run, lean = two_sums(lambda half, m: jnp.where(packed[half * HALF + m] == mark, one, none))
    h_ref[3 * c] = up
    h_ref[3 * c + 1] = down
    h_ref[3 * c + 2] = run + lean * mid


def softmax_fast(groups, chans, slots, fold, w_ref, p_ref, packed, h_ref):
    sums = [None] * (2 * groups * HALF)
    for c in range(chans):
        tally(packed, c, h_ref)
        for b in range(groups):
            row = c * slots + SUB * b
            upper = w_ref[row : row + SUB, :]
            lower = w_ref[row + 1 : row + 1 + SUB, :]
            slope = (lower - upper) * fold[b]
            twice = slope + slope
            for half, (p, ratio) in enumerate(((upper + slope, twice), (lower - slope, -twice))):
                p, ratio = jnp.exp2(p), jnp.exp2(ratio)
                for m in range(HALF):
                    k = (half * groups + b) * HALF + m
                    if m:
                        p = p * ratio
                    p_ref[c * len(sums) + k] = p
                    sums[k] = p if sums[k] is None else sums[k] + p
    return sums


def softmax_slow(groups, chans, slots, fold, w_ref, p_ref, labels, weights):
    count = len(labels)
    sums, losses = [], jnp.zeros((SUB, LANES), f32)
    for k in range(count):
        half, b, m = k // (groups * HALF), k // HALF % groups, k % HALF

        def score(c, half=half, b=b, m=m):
            row = c * slots + SUB * b
            near = w_ref[pl.ds(row + half, SUB), :]
            away = w_ref[pl.ds(row + 1 - half, SUB), :]
            return near + (away - near) * fold[b] * (2 * m + 1.0)

        top = lax.fori_loop(1, chans, lambda c, t, score=score: jnp.maximum(t, score(c)), score(0))

        def take(c, carry, k=k, top=top, score=score):
            total, picked = carry
            shifted = score(c) - top
            p = jnp.exp2(shifted)
            p_ref[c * count + k] = p
            return total + p, jnp.where(labels[k] == c, shifted, picked)

        zero = jnp.zeros((SUB, LANES), f32)
        total, picked = lax.fori_loop(0, chans, take, (zero, zero))
        sums.append(total)
        losses = losses - weights[k] * picked
    return sums, losses


def pixels(groups, chans, slots, fold, lab_ref, fast, prepare, w_ref, p_ref, s_ref, lhs_ref, h_ref):
    count = 2 * groups * HALF
    labels = []
    for half in range(2):
        for b in range(groups):
            for m in range(HALF):
                k = PATCH - 1 - m if half else m
                labels.append(lab_ref[pl.ds(b * SUB * PATCH + HALF + k, SUB, stride=PATCH), :])
    weights = [jnp.where(lab >= 0, 1.0, 0.0) for lab in labels]
    packed = [
        jnp.concatenate([labels[(half * groups + b) * HALF + m] for b in range(groups)], axis=0).astype(f32).astype(bf16)
        for half in range(2)
        for m in range(HALF)
    ]

    @pl.when(fast)
    def _():
        sums = softmax_fast(groups, chans, slots, fold, w_ref, p_ref, packed, h_ref)
        for k in range(count):
            s_ref[k] = sums[k]
        s_ref[count] = jnp.zeros((SUB, LANES), f32)
        prepare()

    @pl.when(jnp.logical_not(fast))
    def _():
        sums, losses = softmax_slow(groups, chans, slots, fold, w_ref, p_ref, labels, weights)
        for k in range(count):
            s_ref[k] = sums[k]
        s_ref[count] = losses
        lax.fori_loop(0, chans, lambda c, _: tally(packed, c, h_ref), None)
        prepare()

    loss = jnp.zeros((SUB, LANES), f32)
    scale = []
    for k in range(count):
        total = s_ref[k]
        loss = loss + weights[k] * jnp.log(total)
        scale.append(weights[k] / total)
    picked = jnp.zeros((SUB, LANES), f32)
    tall = groups * SUB
    for c in range(chans):
        hits = [h_ref[3 * c + k].astype(f32) for k in range(3)]
        parts = [[], []]
        for b in range(groups):
            row = c * slots + SUB * b
            up, down, lean = (v[b * SUB : b * SUB + SUB] for v in hits)
            lean = lean * (fold[b] * 2.0)
            up, down = up - lean, down + lean
            picked = picked + up * w_ref[row : row + SUB, :] + down * w_ref[row + 1 : row + 1 + SUB, :]
            above, below, run, lean = two_sums(
                lambda half, m: p_ref[c * count + (half * groups + b) * HALF + m] * scale[(half * groups + b) * HALF + m]
            )
            lean = (run + lean * 0.5) * (fold[b] * 2.0)
            parts[0].append((above - up) - lean)
            parts[1].append((below - down) + lean)
        for kind in range(2):
            g = jnp.concatenate(parts[kind], axis=0)
            hi = g.astype(bf16)
            at = (kind * chans + c) * tall
            lhs_ref[at : at + tall, 0:LANES] = hi
            lhs_ref[at : at + tall, LANES:] = (g - hi.astype(f32)).astype(bf16)
    return loss + LN2 * jnp.where(fast, -picked, s_ref[count])


def first_columns(rows, groups, chans, slots, last_row, own_ref, got_ref, w_ref, p_ref, lhs_ref):
    lane = lax.broadcasted_iota(jnp.int32, (SUB, LANES), 1)
    sub = lax.broadcasted_iota(jnp.int32, (SUB, LANES), 0)
    turn = HALF * HALF
    share = jnp.zeros((SUB, LANES), f32)
    for k in range(PATCH):
        share = jnp.where(lane >= k * HALF, (2 * k + 1.0) / STEP, share)
    end = jnp.where(last_row & (sub == SUB - 1), jnp.where(lane < turn, 0.0, 1.0), share)
    shares = [share] * (groups - 1) + [end]
    tall = groups * SUB
    loss = jnp.zeros((SUB, LANES), f32)
    scale, labels = [], []
    for b in range(groups):
        upper = own_ref[b * SUB : b * SUB + SUB, :]
        at = (b + 1) * SUB
        lower = got_ref[got_ref.shape[0] - SUB :, :] if at == rows else own_ref[at : at + SUB, :]
        lower = jnp.where(sub == SUB - 1, pltpu.roll(lower, SUB - 1, 0), pltpu.roll(upper, SUB - 1, 0))
        label = jnp.where(lane < turn, pltpu.roll(upper, LANES - turn, 1), pltpu.roll(lower, turn, 1))
        label = jnp.where(lane < PATCH * HALF, label, -1.0).astype(jnp.int32)
        top = None
        for c in range(chans):
            row = c * slots + SUB * b
            v = w_ref[row : row + SUB, :]
            v = v + (w_ref[row + 1 : row + 1 + SUB, :] - v) * shares[b]
            p_ref[c * groups + b] = v
            top = v if top is None else jnp.maximum(top, v)
        total = picked = jnp.zeros((SUB, LANES), f32)
        for c in range(chans):
            v = p_ref[c * groups + b] - top
            picked = jnp.where(label == c, v, picked)
            v = jnp.exp2(v)
            p_ref[c * groups + b] = v
            total = total + v
        weight = jnp.where(label >= 0, 1.0, 0.0)
        loss = loss + weight * (jnp.log(total) - LN2 * picked)
        scale.append(weight / total)
        labels.append(label)
    for c in range(chans):
        parts = [[], []]
        for b in range(groups):
            g = p_ref[c * groups + b] * scale[b] - jnp.where(labels[b] == c, 1.0, 0.0)
            below = g * shares[b]
            parts[0].append(g - below)
            parts[1].append(below)
        for kind in range(2):
            g = jnp.concatenate(parts[kind], axis=0)
            hi = g.astype(bf16)
            at = (kind * chans + c) * tall
            lhs_ref[at : at + tall, 0:LANES] = hi
            lhs_ref[at : at + tall, LANES:] = (g - hi.astype(f32)).astype(bf16)
    return loss


def inner_kernel(rows, cols, chans, slots, groups, part, begin, tiles, *refs):
    (got_ref, lift_ref, lift_end_ref, back_ref, back_end_ref, lab_ref, mask_ref), refs = refs[:7], refs[7:]
    if part == 0:
        (x_ref, own_ref, fill_ref, sum_ref, loss_ref, stack_ref, floor_out_ref), refs = refs[:7], refs[7:]
    elif part == 1:
        (sum_in_ref, loss_in_ref, stack_ref, floor_in_ref, sum_ref, loss_ref), refs = refs[:6], refs[6:]
    else:
        (x_ref, beyond_ref, corner_ref, strip_ref, sum_in_ref, loss_in_ref), refs = refs[:6], refs[6:]
        (out_ref, spill_ref, loss_ref), refs = refs[:3], refs[3:]
    (w_ref, p_ref, s_ref, lhs_ref, tile_ref, h_ref, floor_ref), refs = refs[:7], refs[7:]
    if part == 2:
        sum_ref, stack_ref = refs
    step = pl.program_id(0)
    steps = pl.num_programs(0)
    now = lax.rem(step, 2)
    which = lax.rem(step + begin, tiles)
    last_col = lax.axis_index("gx") == lax.axis_size("gx") - 1
    last_row = lax.axis_index("gy") == lax.axis_size("gy") - 1
    tall = rows * PATCH
    lane = lax.broadcasted_iota(jnp.int32, (SUB, LANES), 1)
    lanes = pl.ds(pl.multiple_of(which * LANES, LANES), LANES)

    def lift(at):
        lanes = pl.ds(pl.multiple_of(at * LANES, LANES), LANES)
        table = jnp.where(last_col, lift_end_ref[:, lanes], lift_ref[:, lanes])
        return jnp.dot(stack_ref[...], table, preferred_element_type=f32)

    @pl.when(step == 0)
    def _():
        if part == 0:
            sum_ref[...] = jnp.zeros_like(sum_ref)
            loss_ref[...] = jnp.zeros_like(loss_ref)
        else:
            sum_ref[...] = sum_in_ref[...]
            loss_ref[...] = loss_in_ref[...]
        if part != 1:
            w_ref[0] = x_ref[...]
            w_ref[0, pl.ds(rows, chans, stride=slots), :] = got_ref[0:chans, :]
            if part == 2:
                wide = lax.broadcasted_iota(jnp.int32, (chans, LANES), 1)
                for i in range(rows + 1):
                    column = beyond_ref[0:chans, :] if i < rows else corner_ref[0:chans, :]
                    column = pltpu.roll(column, cols - i if i < rows else cols, 1)
                    pick = pl.ds(i, chans, stride=slots)
                    w_ref[0, pick, :] = jnp.where(wide == cols, column, w_ref[0, pick, :])
            full = w_ref[0]
            floor_ref[0] = jnp.min(full) * STEP
            stack_ref[...] = stack3(full)
            if part == 0:
                floor_out_ref[...] = jnp.full((SUB, LANES), floor_ref[0], f32)
        else:
            floor_ref[0] = jnp.min(floor_in_ref[...])
        w_ref[0] = lift(which)

    tile_ref[0:tall, :] = jnp.where(mask_ref[:, lanes] != 0, lab_ref[:, lanes], -1)
    tile_ref[tall : tall + SUB, :] = got_ref[pl.ds(pl.multiple_of(chans + which * SUB, SUB), SUB), :].astype(jnp.int32)

    if part == 2:

        @pl.when(which == 0)
        def _():
            for j in range(PATCH):
                for b in range(groups):
                    pick = pl.ds(b * SUB * PATCH + j, SUB, stride=PATCH)
                    strip = strip_ref[b * SUB : b * SUB + SUB, :]
                    strip = pltpu.roll(strip, LANES - j * HALF, 1) if j else strip
                    strip = jnp.where(last_col, -1.0, strip)
                    tile_ref[pick, :] = jnp.where(lane < HALF, strip.astype(jnp.int32), tile_ref[pick, :])
            for j in range(HALF):
                strip = corner_ref[chans : chans + 1, :]
                strip = pltpu.roll(strip, LANES - j * HALF, 1) if j else strip
                strip = jnp.where(last_col, -1.0, strip)
                row = tile_ref[tall + j : tall + j + 1, :]
                tile_ref[tall + j : tall + j + 1, :] = jnp.where(lane[0:1] < HALF, strip.astype(jnp.int32), row)

    flat = jnp.full((SUB, LANES), 1.0 / STEP, f32)
    sub = lax.broadcasted_iota(jnp.int32, (SUB, LANES), 0)
    fold = [flat] * (groups - 1) + [jnp.where(last_row & (sub == SUB - 1), 0.0, flat)]
    fast = floor_ref[0] >= FLOOR

    def prepare():
        w_ref[1 - now] = lift(lax.rem(which + 1, tiles))

    loss_ref[...] += pixels(groups, chans, slots, fold, tile_ref, fast, prepare, w_ref.at[now], p_ref, s_ref, lhs_ref, h_ref)
    depth = 2 * LANES
    deep = pl.ds(pl.multiple_of(which * depth, depth), depth)
    table = jnp.where(last_col, back_end_ref[deep, :], back_ref[deep, :])
    sum_ref[...] += jnp.dot(lhs_ref[...], table, preferred_element_type=f32)

    if part == 0:

        @pl.when((step == steps - 1) & (lax.axis_index("gx") == 0))
        def _():
            depth = stack_ref.shape[1]
            w_ref[1 - now] = jnp.dot(stack_ref[...], fill_ref[0:depth, :], preferred_element_type=f32)
            loss_ref[...] += first_columns(rows, groups, chans, slots, last_row, own_ref, got_ref, w_ref.at[1 - now], p_ref, lhs_ref)
            sum_ref[...] += jnp.dot(lhs_ref[...], fill_ref[depth:, :], preferred_element_type=f32)

    if part == 2:

        @pl.when(step == steps - 1)
        def _():
            w_ref[0] = jnp.zeros_like(w_ref[0])
            high = groups * SUB
            for c in range(chans):
                for kind in range(2):
                    at = (kind * chans + c) * high
                    row = c * slots + kind
                    w_ref[0, row : row + high, :] += sum_ref[at : at + high, :]
            out_ref[...] = w_ref[0] * (1.0 / STEP)
            spill_ref[...] = out_ref[pl.ds(rows, chans, stride=slots), :]


def grad_kernel(
    rows, cols, chans, slots, f_ref, beside_ref, g_ref, got_ref, loss_ref, count_ref, mine_ref, other_ref, sum_ref,
):
    row = lax.axis_index("gy")
    sum_ref[...] = g_ref[...]
    sum_ref[pl.ds(0, chans, stride=slots), :] += got_ref[...]
    lane = lax.broadcasted_iota(jnp.int32, (chans, LANES), 1)
    share = LANES // cols
    edge = jnp.zeros((chans, LANES), f32)
    tiles = []
    total = jnp.zeros((chans, LANES), f32)
    for k in range(0, rows, share):
        tile = None
        for r in range(share):
            piece = sum_ref[pl.ds(k + r, chans, stride=slots), :]
            total = total + piece
            edge = jnp.where(lane == k + r, pltpu.roll(piece, (k + r - cols) % LANES, 1), edge)
            if r:
                piece = pltpu.roll(piece, r * cols, 1)
            tile = piece if tile is None else jnp.where(lane < r * cols, tile, piece)
        tiles.append(tile.astype(bf16))
    block = f_ref[...].reshape(rows * cols, f_ref.shape[2])
    out = jnp.dot(jnp.concatenate(tiles, axis=1), block, preferred_element_type=f32)
    beside = jnp.concatenate([beside_ref[...], jnp.zeros((LANES - rows, f_ref.shape[2]), bf16)], axis=0)
    out = out + jnp.dot(edge.astype(bf16), beside, preferred_element_type=f32)
    total = jnp.where(lane <= cols, total, 0.0)
    square = jnp.concatenate([total, jnp.zeros((LANES - chans, LANES), f32)], axis=0)
    bias = jnp.sum(square.T, axis=0, keepdims=True)
    at = lax.broadcasted_iota(jnp.int32, (SUB, LANES), 0)
    rest = jnp.where(at == 1, jnp.sum(loss_ref[...]), count_ref[0, 0].astype(f32))
    stats = jnp.where(at == 0, bias, jnp.where(at < 3, rest, 0.0))
    pieces = out.shape[1] // LANES // 2
    for k in range(pieces):
        low = out[:, k * LANES : k * LANES + LANES]
        high = out[:, (pieces + k) * LANES : (pieces + k + 1) * LANES]
        mine_ref[k * chans : k * chans + chans, :] = jnp.where(row == 0, low, high)
        other_ref[k * chans : k * chans + chans, :] = jnp.where(row == 0, high, low)
    mine_ref[pieces * chans :, :] = stats
    other_ref[pieces * chans :, :] = stats


def final_kernel(chans, y_ref, z_ref, loss_ref, weight_ref, bias_ref):
    pieces = y_ref.shape[0] // chans
    lower = lax.axis_index("gy") == 0
    stats = y_ref[pieces * chans :, :]
    total = stats[2:3, 0:1]
    for k in range(pieces):
        y = y_ref[k * chans : k * chans + chans, :]
        z = z_ref[k * chans : k * chans + chans, :]
        weight_ref[:, k * LANES : k * LANES + LANES] = jnp.where(lower, y, z) / total
        weight_ref[:, (pieces + k) * LANES : (pieces + k + 1) * LANES] = jnp.where(lower, z, y) / total
    loss_ref[...] = stats[1:2, 0:1] / total
    bias_ref[...] = stats[0:1, 0:chans] / total


def body(features, probe_weight, probe_bias, labels, valid_mask, valid_count):
    rows, cols, width = features.shape
    chans = probe_weight.shape[1]
    gx, gy = lax.axis_size("gx"), lax.axis_size("gy")
    if gy != 2 or rows % SUB or 2 * cols != LANES or cols * PATCH % LANES or width % (2 * LANES) or gx & (gx - 1):
        raise ValueError("unsupported tile")
    groups = rows // SUB
    slots = rows + SUB
    count = groups * HALF
    tiles = cols * PATCH // LANES
    tall = rows * PATCH
    depth = 2 * LANES

    def forward(table):
        out = np.zeros((depth, table.shape[1]), np.float32)
        for k in range(3):
            out[k * cols : k * cols + cols] = table[:cols]
            out[3 * cols + k] = table[cols]
        return out

    def backward(table):
        out = np.zeros((table.shape[1] // LANES, 2, LANES, LANES), np.float32)
        out[:, :, :, : cols + 1] = table.T.reshape(-1, 1, LANES, cols + 1)
        return out.reshape(-1, LANES)

    inside, ending = column_tables(cols)
    lift, lift_end, back, back_end = (
        jnp.asarray(t, bf16) for t in (forward(inside), forward(ending), backward(inside), backward(ending))
    )

    fill = np.zeros((2 * depth, LANES), np.float32)
    fill[[0, cols, 2 * cols]] = STEP
    for part in (depth, depth + LANES):
        fill[part : part + PATCH * HALF, 0] = STEP
    fill = jnp.asarray(fill, bf16)

    shape = lambda *dims: jax.ShapeDtypeStruct(dims, f32)
    held = lambda *dims, kind=f32: pltpu.VMEM(dims, kind)
    far = lambda v: pltpu.with_memory_space_constraint(v, pltpu.HBM)
    here = lambda v: pltpu.with_memory_space_constraint(v, pltpu.VMEM)
    ring = lambda v, axis: lax.ppermute(v, axis, [(i, (i - 1) % lax.axis_size(axis)) for i in range(lax.axis_size(axis))])
    swap = lambda v: lax.ppermute(v, "gy", [(0, 1), (1, 0)])
    tall_x = chans * slots

    own, head, weight, shift = pl.pallas_call(
        functools.partial(pack_kernel, rows),
        in_specs=[ANY] * 5,
        out_specs=[VMEM] * 4,
        out_shape=[
            held(rows + rows * width // LANES, LANES), held(tiles * SUB, LANES), held(chans, width, kind=bf16),
            held(chans, LANES),
        ],
        scratch_shapes=[
            pltpu.VMEM((rows, SUB, width), bf16),
            pltpu.VMEM((2, tall, LANES), jnp.int32),
            pltpu.VMEM((2, SUB, tiles * LANES), jnp.int32),
            pltpu.VMEM((1, chans), f32),
            pltpu.SemaphoreType.DMA((7,)),
        ],
        compiler_params=ROOM,
        name="pack",
    )(*(far(v) for v in (features, labels, valid_mask, probe_weight.T, probe_bias.reshape(1, chans))))
    side = lax.ppermute(own, "gx", [(i, i - 1) for i in range(1, gx)])
    x, edge = pl.pallas_call(
        functools.partial(logits_kernel, rows, cols, chans, slots, 4),
        in_specs=[VMEM] * 5,
        out_specs=[VMEM] * 2,
        out_shape=[held(tall_x, LANES), held(chans + tiles * SUB + SUB, LANES)],
        compiler_params=ROOM,
        name="logits",
    )(*(here(v) for v in (features, weight, shift, head, own)))
    got = ring(edge, "gy")

    sums = (2 * chans * rows, LANES)
    stacked = held(tall_x, depth, kind=bf16)

    def inner(part, begin, steps, *args):
        outs = [
            ([held(*sums), held(SUB, LANES), stacked, held(SUB, LANES)], [VMEM] * 4, [VMEM] * 3),
            ([held(*sums), held(SUB, LANES)], [VMEM] * 2, [VMEM] * 4),
            ([held(tall_x, LANES), held(chans, LANES), held(SUB, LANES)], [VMEM] * 3, [VMEM] * 6),
        ][part]
        return pl.pallas_call(
            functools.partial(inner_kernel, rows, cols, chans, slots, groups, part, begin, tiles),
            grid=(steps,),
            in_specs=[VMEM] * 7 + outs[2],
            out_specs=outs[1],
            out_shape=outs[0],
            scratch_shapes=[
                pltpu.VMEM((2, tall_x, LANES), f32),
                pltpu.VMEM((2 * chans * count, SUB, LANES), f32),
                pltpu.VMEM((2 * count + 1, SUB, LANES), f32),
                pltpu.VMEM((2 * chans * rows, depth), bf16),
                pltpu.VMEM((tall + SUB, LANES), jnp.int32),
                pltpu.VMEM((3 * chans, rows, LANES), bf16),
                pltpu.SMEM((1,), f32),
            ] + ([pltpu.VMEM(sums, f32), stacked] if part == 2 else []),
            cost_estimate=pl.CostEstimate(flops=10**9, bytes_accessed=2 * 10**6, transcendentals=10**6),
            compiler_params=ROOM,
            name=("inner_head", "inner_middle", "inner_tail")[part],
        )(*(here(v) for v in (got, lift, lift_end, back, back_end, labels, valid_mask)), *args)

    middle = tiles // 2 + 1
    total, loss, stack, floor = inner(0, 1, middle - 1, here(x), here(own), here(fill))
    side, total = lax.optimization_barrier((side, total))
    beside, beyond = pl.pallas_call(
        functools.partial(beside_kernel, rows, chans),
        in_specs=[VMEM] * 3,
        out_specs=[VMEM] * 2,
        out_shape=[held(rows, width, kind=bf16), held(chans + SUB, LANES)],
        compiler_params=ROOM,
        name="beside",
    )(here(side), here(weight), here(shift))
    corner = ring(beyond, "gy")
    total, loss = inner(1, middle, tiles - 1 - middle, *(here(v) for v in (total, loss, stack, floor)))
    grad, spill, loss = inner(2, tiles - 1, 2, *(here(v) for v in (x, beyond, corner, side, total, loss)))
    got = lax.ppermute(spill, "gy", [(i, (i + 1) % gy) for i in range(gy)])
    pack = (chans * width // 2 // LANES + SUB, LANES)
    mine, other = pl.pallas_call(
        functools.partial(grad_kernel, rows, cols, chans, slots),
        in_specs=[VMEM] * 5 + [SMEM],
        out_specs=[VMEM] * 2,
        out_shape=[held(*pack)] * 2,
        scratch_shapes=[pltpu.VMEM((tall_x, LANES), f32)],
        compiler_params=ROOM,
        name="grad",
    )(*(here(v) for v in (features, beside, grad, got, loss)), valid_count)

    total = mine + swap(other)
    step = 1
    while step < gx:
        total = total + lax.ppermute(total, "gx", [(i, i ^ step) for i in range(gx)])
        step *= 2
    loss, weight, bias = pl.pallas_call(
        functools.partial(final_kernel, chans),
        in_specs=[VMEM] * 2,
        out_specs=[VMEM] * 3,
        out_shape=[shape(1, 1), shape(chans, width), shape(1, chans)],
        compiler_params=ROOM,
        name="final",
    )(here(total), here(swap(total)))
    return loss.reshape(1), weight.T, bias.reshape(chans)


def solution(mesh):
    return jax.shard_map(
        body,
        mesh=mesh,
        in_specs=(
            P(("groups", "gy"), "gx", None),
            P(),
            P(),
            P(("groups", "gy"), "gx"),
            P(("groups", "gy"), "gx"),
            P(("groups", "gy"), "gx"),
        ),
        out_specs=(P("groups"), P("groups", None), P("groups")),
        check_vma=False,
    )
```

```python
import functools
import math

import jax
import jax.numpy as jnp
import numpy as np
from jax import lax
from jax.experimental import pallas as pl
from jax.experimental.pallas import tpu as pltpu
from jax.sharding import PartitionSpec as P


PATCH = 14
HALF = PATCH // 2
STEP = 2 * PATCH
LANES = 128
SUB = 8
LOG2E = 1.0 / math.log(2.0)
LN2 = math.log(2.0)
FLOOR = -100.0
f32 = jnp.float32
bf16 = jnp.bfloat16
VMEM = pl.BlockSpec(memory_space=pltpu.VMEM)
ANY = pl.BlockSpec(memory_space=pl.ANY)
ROOM = pltpu.CompilerParams(vmem_limit_bytes=16 * 2**20)
SMEM = pl.BlockSpec(memory_space=pltpu.SMEM)


def column_tables(cols):
    tables = np.zeros((2, cols + 1, cols * PATCH), np.float32)
    for q in range(cols * PATCH):
        i, k = divmod((q if q >= HALF else q + cols * PATCH) - HALF, PATCH)
        far = 2 * k + 1
        for end in range(2):
            if end and i == cols - 1:
                tables[end, i + (k >= HALF), q] = STEP
            else:
                tables[end, i, q] = STEP - far
                tables[end, i + 1, q] = far
    return tables


def split3(x):
    hi = x.astype(bf16)
    rest = x - hi.astype(f32)
    mid = rest.astype(bf16)
    return hi, mid, (rest - mid.astype(f32)).astype(bf16)


def stack3(x):
    cols = LANES // 2
    lane = lax.broadcasted_iota(jnp.int32, x.shape, 1)
    hi, mid, low = (part.astype(f32) for part in split3(x))
    first = jnp.where(lane < cols, hi, pltpu.roll(mid, cols, 1))
    second = jnp.where(lane == cols + 1, pltpu.roll(mid, 1, 1), pltpu.roll(low, 2, 1))
    second = jnp.where(lane == cols, hi, jnp.where(lane < cols + 3, second, 0.0))
    second = jnp.where(lane < cols, low, second)
    return jnp.concatenate([first.astype(bf16), second.astype(bf16)], axis=1)


def pack_kernel(
    rows, f_ref, lab_ref, mask_ref, w_ref, bias_ref, out_ref, head_ref, weight_ref, shift_ref, f_vmem, l_vmem, h_vmem, b_vmem, sem,
):
    width = f_vmem.shape[2]
    tiles = head_ref.shape[0] // SUB
    copies = [
        pltpu.make_async_copy(lab_ref.at[:, pl.ds(0, LANES)], l_vmem.at[0], sem.at[0]),
        pltpu.make_async_copy(mask_ref.at[:, pl.ds(0, LANES)], l_vmem.at[1], sem.at[1]),
        pltpu.make_async_copy(f_ref.at[:, pl.ds(0, SUB)], f_vmem, sem.at[2]),
        pltpu.make_async_copy(lab_ref.at[pl.ds(0, SUB)], h_vmem.at[0], sem.at[3]),
        pltpu.make_async_copy(mask_ref.at[pl.ds(0, SUB)], h_vmem.at[1], sem.at[4]),
        pltpu.make_async_copy(w_ref, weight_ref, sem.at[5]),
        pltpu.make_async_copy(bias_ref, b_vmem, sem.at[6]),
    ]
    for copy in copies:
        copy.start()
    at = lax.broadcasted_iota(jnp.int32, (SUB, LANES), 1)
    for copy in copies:
        copy.wait()
    for b in range(rows // SUB):
        strip = jnp.full((SUB, LANES), -1.0, f32)
        for j in range(PATCH):
            pick = pl.ds(b * SUB * PATCH + j, SUB, stride=PATCH)
            lab = jnp.where(l_vmem[1, pick, :] != 0, l_vmem[0, pick, :], -1).astype(f32)
            here = (at >= j * HALF) & (at < j * HALF + HALF)
            strip = jnp.where(here, pltpu.roll(lab, j * HALF, 1) if j else lab, strip)
        out_ref[b * SUB : b * SUB + SUB, :] = strip
    for i in range(rows):
        line = f_vmem[i].astype(f32)
        for k in range(width // LANES):
            out_ref[rows + k * rows + i : rows + k * rows + i + 1, :] = line[0:1, k * LANES : k * LANES + LANES]
    for t in range(tiles):
        lanes = slice(t * LANES, t * LANES + LANES)
        head_ref[t * SUB : t * SUB + SUB, :] = jnp.where(h_vmem[1, :, lanes] != 0, h_vmem[0, :, lanes], -1).astype(f32)
    chans = shift_ref.shape[0]
    bias = jnp.concatenate([b_vmem[...], jnp.zeros((1, LANES - chans), f32)], axis=1)
    shift_ref[...] = jnp.broadcast_to(bias, (LANES, LANES)).T[0:chans, :]


def score_of(w_ref, shift_ref, block):
    score = lax.dot_general(w_ref[...], block, (((1,), (1,)), ((), ())), preferred_element_type=f32)
    score = score + jnp.concatenate([shift_ref[...]] * (block.shape[0] // LANES), axis=1)
    return (score - jnp.max(score, axis=0, keepdims=True)) * (LOG2E / STEP)


def logits_kernel(rows, cols, chans, slots, per, f_ref, w_ref, shift_ref, head_ref, side_ref, x_ref, e_ref):
    x_ref[...] = jnp.zeros_like(x_ref)
    lane = lax.broadcasted_iota(jnp.int32, (chans, LANES), 1)
    for step in range(rows // per):
        score = score_of(w_ref, shift_ref, f_ref[step * per : step * per + per].reshape(per * cols, f_ref.shape[2]))
        for k in range(per):
            i, off = step * per + k, k * cols
            tile = score[:, off // LANES * LANES : off // LANES * LANES + LANES]
            if off % LANES:
                tile = pltpu.roll(tile, LANES - off % LANES, 1)
            tile = jnp.where(lane < cols, tile, 0.0)
            x_ref[pl.ds(i, chans, stride=slots), :] = tile
            if i == 0:
                e_ref[0:chans, :] = tile
    e_ref[chans : chans + head_ref.shape[0], :] = head_ref[...]
    e_ref[chans + head_ref.shape[0] :, :] = side_ref[0:SUB, :]


def beside_kernel(rows, chans, side_ref, w_ref, shift_ref, beside_ref, out_ref):
    width = w_ref.shape[1]
    side = jnp.concatenate(
        [side_ref[rows + k * rows : rows + k * rows + rows, :] for k in range(width // LANES)], axis=1
    ).astype(bf16)
    beside_ref[...] = side
    side = jnp.concatenate([side, jnp.zeros((LANES - rows, width), bf16)], axis=0)
    out_ref[0:chans, :] = score_of(w_ref, shift_ref, side)
    out_ref[chans:, :] = side_ref[0:SUB, :]


def two_sums(item):
    totals, runs = [], []
    for half in range(2):
        total = run = None
        for m in reversed(range(HALF)):
            v = item(half, m)
            total = v if total is None else total + v
            if m:
                run = total if run is None else run + total
        totals.append(total)
        runs.append(run)
    return totals[0], totals[1], runs[0] - runs[1], totals[0] - totals[1]


def tally(packed, c, h_ref):
    one, none, mid = (jnp.asarray(v, bf16) for v in (1, 0, 0.5))
    mark = jnp.asarray(c, bf16) if isinstance(c, int) else c.astype(f32).astype(bf16)
    up, down, run, lean = two_sums(lambda half, m: jnp.where(packed[half * HALF + m] == mark, one, none))
    h_ref[3 * c] = up
    h_ref[3 * c + 1] = down
    h_ref[3 * c + 2] = run + lean * mid


def softmax_fast(groups, chans, slots, fold, w_ref, p_ref):
    sums = [None] * (2 * groups * HALF)
    for b in range(groups):
        for c in range(chans):
            row = c * slots + SUB * b
            upper = w_ref[row : row + SUB, :]
            lower = w_ref[row + 1 : row + 1 + SUB, :]
            slope = (lower - upper) * fold[b]
            twice = slope + slope
            for half, (p, ratio) in enumerate(((upper + slope, twice), (lower - slope, -twice))):
                p, ratio = jnp.exp2(p), jnp.exp2(ratio)
                for m in range(HALF):
                    k = (half * groups + b) * HALF + m
                    if m:
                        p = p * ratio
                    p_ref[c * len(sums) + k] = p
                    sums[k] = p if sums[k] is None else sums[k] + p
    return sums


def softmax_slow(groups, chans, slots, fold, w_ref, p_ref, labels, weights):
    count = len(labels)
    sums, losses = [], jnp.zeros((SUB, LANES), f32)
    for k in range(count):
        half, b, m = k // (groups * HALF), k // HALF % groups, k % HALF

        def score(c, half=half, b=b, m=m):
            row = c * slots + SUB * b
            near = w_ref[pl.ds(row + half, SUB), :]
            away = w_ref[pl.ds(row + 1 - half, SUB), :]
            return near + (away - near) * fold[b] * (2 * m + 1.0)

        top = lax.fori_loop(1, chans, lambda c, t, score=score: jnp.maximum(t, score(c)), score(0))

        def take(c, carry, k=k, top=top, score=score):
            total, picked = carry
            shifted = score(c) - top
            p = jnp.exp2(shifted)
            p_ref[c * count + k] = p
            return total + p, jnp.where(labels[k] == c, shifted, picked)

        zero = jnp.zeros((SUB, LANES), f32)
        total, picked = lax.fori_loop(0, chans, take, (zero, zero))
        sums.append(total)
        losses = losses - weights[k] * picked
    return sums, losses


def pixels(groups, chans, slots, fold, lab_ref, fast, prepare, w_ref, p_ref, s_ref, lhs_ref, h_ref):
    count = 2 * groups * HALF
    labels = []
    for half in range(2):
        for b in range(groups):
            for m in range(HALF):
                k = PATCH - 1 - m if half else m
                labels.append(lab_ref[pl.ds(b * SUB * PATCH + HALF + k, SUB, stride=PATCH), :])
    weights = [jnp.where(lab >= 0, 1.0, 0.0) for lab in labels]
    packed = [
        jnp.concatenate([labels[(half * groups + b) * HALF + m] for b in range(groups)], axis=0).astype(f32).astype(bf16)
        for half in range(2)
        for m in range(HALF)
    ]

    @pl.when(fast)
    def _():
        sums = softmax_fast(groups, chans, slots, fold, w_ref, p_ref)
        for k in range(count):
            s_ref[k] = sums[k]
        s_ref[count] = jnp.zeros((SUB, LANES), f32)
        prepare()

    @pl.when(jnp.logical_not(fast))
    def _():
        sums, losses = softmax_slow(groups, chans, slots, fold, w_ref, p_ref, labels, weights)
        for k in range(count):
            s_ref[k] = sums[k]
        s_ref[count] = losses
        prepare()

    loss = jnp.zeros((SUB, LANES), f32)
    scale = []
    for k in range(count):
        total = s_ref[k]
        loss = loss + weights[k] * jnp.log(total)
        scale.append(weights[k] / total)
    picked = jnp.zeros((SUB, LANES), f32)
    tall = groups * SUB
    for c in range(chans):
        tally(packed, c, h_ref)
        hits = [h_ref[3 * c + k].astype(f32) for k in range(3)]
        parts = [[], []]
        for b in range(groups):
            row = c * slots + SUB * b
            up, down, lean = (v[b * SUB : b * SUB + SUB] for v in hits)
            lean = lean * (fold[b] * 2.0)
            up, down = up - lean, down + lean
            picked = picked + up * w_ref[row : row + SUB, :] + down * w_ref[row + 1 : row + 1 + SUB, :]
            above, below, run, lean = two_sums(
                lambda half, m: p_ref[c * count + (half * groups + b) * HALF + m] * scale[(half * groups + b) * HALF + m]
            )
            lean = (run + lean * 0.5) * (fold[b] * 2.0)
            parts[0].append((above - up) - lean)
            parts[1].append((below - down) + lean)
        for kind in range(2):
            g = jnp.concatenate(parts[kind], axis=0)
            hi = g.astype(bf16)
            at = (kind * chans + c) * tall
            lhs_ref[at : at + tall, 0:LANES] = hi
            lhs_ref[at : at + tall, LANES:] = (g - hi.astype(f32)).astype(bf16)
    return loss + LN2 * jnp.where(fast, -picked, s_ref[count])


def first_columns(rows, groups, chans, slots, last_row, own_ref, got_ref, w_ref, p_ref, lhs_ref):
    lane = lax.broadcasted_iota(jnp.int32, (SUB, LANES), 1)
    sub = lax.broadcasted_iota(jnp.int32, (SUB, LANES), 0)
    turn = HALF * HALF
    share = jnp.zeros((SUB, LANES), f32)
    for k in range(PATCH):
        share = jnp.where(lane >= k * HALF, (2 * k + 1.0) / STEP, share)
    end = jnp.where(last_row & (sub == SUB - 1), jnp.where(lane < turn, 0.0, 1.0), share)
    shares = [share] * (groups - 1) + [end]
    tall = groups * SUB
    loss = jnp.zeros((SUB, LANES), f32)
    scale, labels = [], []
    for b in range(groups):
        upper = own_ref[b * SUB : b * SUB + SUB, :]
        at = (b + 1) * SUB
        lower = got_ref[got_ref.shape[0] - SUB :, :] if at == rows else own_ref[at : at + SUB, :]
        lower = jnp.where(sub == SUB - 1, pltpu.roll(lower, SUB - 1, 0), pltpu.roll(upper, SUB - 1, 0))
        label = jnp.where(lane < turn, pltpu.roll(upper, LANES - turn, 1), pltpu.roll(lower, turn, 1))
        label = jnp.where(lane < PATCH * HALF, label, -1.0).astype(jnp.int32)
        top = None
        for c in range(chans):
            row = c * slots + SUB * b
            v = w_ref[row : row + SUB, :]
            v = v + (w_ref[row + 1 : row + 1 + SUB, :] - v) * shares[b]
            p_ref[c * groups + b] = v
            top = v if top is None else jnp.maximum(top, v)
        total = picked = jnp.zeros((SUB, LANES), f32)
        for c in range(chans):
            v = p_ref[c * groups + b] - top
            picked = jnp.where(label == c, v, picked)
            v = jnp.exp2(v)
            p_ref[c * groups + b] = v
            total = total + v
        weight = jnp.where(label >= 0, 1.0, 0.0)
        loss = loss + weight * (jnp.log(total) - LN2 * picked)
        scale.append(weight / total)
        labels.append(label)
    for c in range(chans):
        parts = [[], []]
        for b in range(groups):
            g = p_ref[c * groups + b] * scale[b] - jnp.where(labels[b] == c, 1.0, 0.0)
            below = g * shares[b]
            parts[0].append(g - below)
            parts[1].append(below)
        for kind in range(2):
            g = jnp.concatenate(parts[kind], axis=0)
            hi = g.astype(bf16)
            at = (kind * chans + c) * tall
            lhs_ref[at : at + tall, 0:LANES] = hi
            lhs_ref[at : at + tall, LANES:] = (g - hi.astype(f32)).astype(bf16)
    return loss


def inner_kernel(rows, cols, chans, slots, groups, part, begin, tiles, *refs):
    (got_ref, lift_ref, lift_end_ref, back_ref, back_end_ref, lab_ref, mask_ref), refs = refs[:7], refs[7:]
    if part == 0:
        (x_ref, own_ref, fill_ref, sum_ref, loss_ref, stack_ref, floor_out_ref), refs = refs[:7], refs[7:]
    elif part == 1:
        (sum_in_ref, loss_in_ref, stack_ref, floor_in_ref, sum_ref, loss_ref), refs = refs[:6], refs[6:]
    else:
        (x_ref, beyond_ref, corner_ref, strip_ref, sum_in_ref, loss_in_ref), refs = refs[:6], refs[6:]
        (out_ref, spill_ref, loss_ref), refs = refs[:3], refs[3:]
    (w_ref, p_ref, s_ref, lhs_ref, tile_ref, h_ref, floor_ref), refs = refs[:7], refs[7:]
    if part == 2:
        sum_ref, stack_ref = refs
    step = pl.program_id(0)
    steps = pl.num_programs(0)
    now = lax.rem(step, 2)
    which = lax.rem(step + begin, tiles)
    last_col = lax.axis_index("gx") == lax.axis_size("gx") - 1
    last_row = lax.axis_index("gy") == lax.axis_size("gy") - 1
    tall = rows * PATCH
    lane = lax.broadcasted_iota(jnp.int32, (SUB, LANES), 1)
    lanes = pl.ds(pl.multiple_of(which * LANES, LANES), LANES)

    def lift(at):
        lanes = pl.ds(pl.multiple_of(at * LANES, LANES), LANES)
        table = jnp.where(last_col, lift_end_ref[:, lanes], lift_ref[:, lanes])
        return jnp.dot(stack_ref[...], table, preferred_element_type=f32)

    @pl.when(step == 0)
    def _():
        if part == 0:
            sum_ref[...] = jnp.zeros_like(sum_ref)
            loss_ref[...] = jnp.zeros_like(loss_ref)
        else:
            sum_ref[...] = sum_in_ref[...]
            loss_ref[...] = loss_in_ref[...]
        if part != 1:
            w_ref[0] = x_ref[...]
            w_ref[0, pl.ds(rows, chans, stride=slots), :] = got_ref[0:chans, :]
            if part == 2:
                wide = lax.broadcasted_iota(jnp.int32, (chans, LANES), 1)
                for i in range(rows + 1):
                    column = beyond_ref[0:chans, :] if i < rows else corner_ref[0:chans, :]
                    column = pltpu.roll(column, cols - i if i < rows else cols, 1)
                    pick = pl.ds(i, chans, stride=slots)
                    w_ref[0, pick, :] = jnp.where(wide == cols, column, w_ref[0, pick, :])
            full = w_ref[0]
            floor_ref[0] = jnp.min(full) * STEP
            stack_ref[...] = stack3(full)
            if part == 0:
                floor_out_ref[...] = jnp.full((SUB, LANES), floor_ref[0], f32)
        else:
            floor_ref[0] = jnp.min(floor_in_ref[...])
        w_ref[0] = lift(which)

    tile_ref[0:tall, :] = jnp.where(mask_ref[:, lanes] != 0, lab_ref[:, lanes], -1)
    tile_ref[tall : tall + SUB, :] = got_ref[pl.ds(pl.multiple_of(chans + which * SUB, SUB), SUB), :].astype(jnp.int32)

    if part == 2:

        @pl.when(which == 0)
        def _():
            for j in range(PATCH):
                for b in range(groups):
                    pick = pl.ds(b * SUB * PATCH + j, SUB, stride=PATCH)
                    strip = strip_ref[b * SUB : b * SUB + SUB, :]
                    strip = pltpu.roll(strip, LANES - j * HALF, 1) if j else strip
                    strip = jnp.where(last_col, -1.0, strip)
                    tile_ref[pick, :] = jnp.where(lane < HALF, strip.astype(jnp.int32), tile_ref[pick, :])
            for j in range(HALF):
                strip = corner_ref[chans : chans + 1, :]
                strip = pltpu.roll(strip, LANES - j * HALF, 1) if j else strip
                strip = jnp.where(last_col, -1.0, strip)
                row = tile_ref[tall + j : tall + j + 1, :]
                tile_ref[tall + j : tall + j + 1, :] = jnp.where(lane[0:1] < HALF, strip.astype(jnp.int32), row)

    flat = jnp.full((SUB, LANES), 1.0 / STEP, f32)
    sub = lax.broadcasted_iota(jnp.int32, (SUB, LANES), 0)
    fold = [flat] * (groups - 1) + [jnp.where(last_row & (sub == SUB - 1), 0.0, flat)]
    fast = floor_ref[0] >= FLOOR

    def prepare():
        w_ref[1 - now] = lift(lax.rem(which + 1, tiles))

    loss_ref[...] += pixels(groups, chans, slots, fold, tile_ref, fast, prepare, w_ref.at[now], p_ref, s_ref, lhs_ref, h_ref)
    depth = 2 * LANES
    deep = pl.ds(pl.multiple_of(which * depth, depth), depth)
    table = jnp.where(last_col, back_end_ref[deep, :], back_ref[deep, :])
    sum_ref[...] += jnp.dot(lhs_ref[...], table, preferred_element_type=f32)

    if part == 0:

        @pl.when((step == steps - 1) & (lax.axis_index("gx") == 0))
        def _():
            depth = stack_ref.shape[1]
            w_ref[1 - now] = jnp.dot(stack_ref[...], fill_ref[0:depth, :], preferred_element_type=f32)
            loss_ref[...] += first_columns(rows, groups, chans, slots, last_row, own_ref, got_ref, w_ref.at[1 - now], p_ref, lhs_ref)
            sum_ref[...] += jnp.dot(lhs_ref[...], fill_ref[depth:, :], preferred_element_type=f32)

    if part == 2:

        @pl.when(step == steps - 1)
        def _():
            w_ref[0] = jnp.zeros_like(w_ref[0])
            high = groups * SUB
            for c in range(chans):
                for kind in range(2):
                    at = (kind * chans + c) * high
                    row = c * slots + kind
                    w_ref[0, row : row + high, :] += sum_ref[at : at + high, :]
            out_ref[...] = w_ref[0] * (1.0 / STEP)
            spill_ref[...] = out_ref[pl.ds(rows, chans, stride=slots), :]


def grad_kernel(
    rows, cols, chans, slots, f_ref, beside_ref, g_ref, got_ref, loss_ref, count_ref, mine_ref, other_ref, sum_ref,
):
    row = lax.axis_index("gy")
    sum_ref[...] = g_ref[...]
    sum_ref[pl.ds(0, chans, stride=slots), :] += got_ref[...]
    lane = lax.broadcasted_iota(jnp.int32, (chans, LANES), 1)
    share = LANES // cols
    edge = jnp.zeros((chans, LANES), f32)
    tiles = []
    total = jnp.zeros((chans, LANES), f32)
    for k in range(0, rows, share):
        tile = None
        for r in range(share):
            piece = sum_ref[pl.ds(k + r, chans, stride=slots), :]
            total = total + piece
            edge = jnp.where(lane == k + r, pltpu.roll(piece, (k + r - cols) % LANES, 1), edge)
            if r:
                piece = pltpu.roll(piece, r * cols, 1)
            tile = piece if tile is None else jnp.where(lane < r * cols, tile, piece)
        tiles.append(tile.astype(bf16))
    block = f_ref[...].reshape(rows * cols, f_ref.shape[2])
    out = jnp.dot(jnp.concatenate(tiles, axis=1), block, preferred_element_type=f32)
    beside = jnp.concatenate([beside_ref[...], jnp.zeros((LANES - rows, f_ref.shape[2]), bf16)], axis=0)
    out = out + jnp.dot(edge.astype(bf16), beside, preferred_element_type=f32)
    total = jnp.where(lane <= cols, total, 0.0)
    square = jnp.concatenate([total, jnp.zeros((LANES - chans, LANES), f32)], axis=0)
    bias = jnp.sum(square.T, axis=0, keepdims=True)
    at = lax.broadcasted_iota(jnp.int32, (SUB, LANES), 0)
    rest = jnp.where(at == 1, jnp.sum(loss_ref[...]), count_ref[0, 0].astype(f32))
    stats = jnp.where(at == 0, bias, jnp.where(at < 3, rest, 0.0))
    pieces = out.shape[1] // LANES // 2
    for k in range(pieces):
        low = out[:, k * LANES : k * LANES + LANES]
        high = out[:, (pieces + k) * LANES : (pieces + k + 1) * LANES]
        mine_ref[k * chans : k * chans + chans, :] = jnp.where(row == 0, low, high)
        other_ref[k * chans : k * chans + chans, :] = jnp.where(row == 0, high, low)
    mine_ref[pieces * chans :, :] = stats
    other_ref[pieces * chans :, :] = stats


def final_kernel(chans, y_ref, z_ref, loss_ref, weight_ref, bias_ref):
    pieces = y_ref.shape[0] // chans
    lower = lax.axis_index("gy") == 0
    stats = y_ref[pieces * chans :, :]
    total = stats[2:3, 0:1]
    for k in range(pieces):
        y = y_ref[k * chans : k * chans + chans, :]
        z = z_ref[k * chans : k * chans + chans, :]
        weight_ref[:, k * LANES : k * LANES + LANES] = jnp.where(lower, y, z) / total
        weight_ref[:, (pieces + k) * LANES : (pieces + k + 1) * LANES] = jnp.where(lower, z, y) / total
    loss_ref[...] = stats[1:2, 0:1] / total
    bias_ref[...] = stats[0:1, 0:chans] / total


def body(features, probe_weight, probe_bias, labels, valid_mask, valid_count):
    rows, cols, width = features.shape
    chans = probe_weight.shape[1]
    gx, gy = lax.axis_size("gx"), lax.axis_size("gy")
    if gy != 2 or rows % SUB or 2 * cols != LANES or cols * PATCH % LANES or width % (2 * LANES) or gx & (gx - 1):
        raise ValueError("unsupported tile")
    groups = rows // SUB
    slots = rows + SUB
    count = groups * HALF
    tiles = cols * PATCH // LANES
    tall = rows * PATCH
    depth = 2 * LANES

    def forward(table):
        out = np.zeros((depth, table.shape[1]), np.float32)
        for k in range(3):
            out[k * cols : k * cols + cols] = table[:cols]
            out[3 * cols + k] = table[cols]
        return out

    def backward(table):
        out = np.zeros((table.shape[1] // LANES, 2, LANES, LANES), np.float32)
        out[:, :, :, : cols + 1] = table.T.reshape(-1, 1, LANES, cols + 1)
        return out.reshape(-1, LANES)

    inside, ending = column_tables(cols)
    lift, lift_end, back, back_end = (
        jnp.asarray(t, bf16) for t in (forward(inside), forward(ending), backward(inside), backward(ending))
    )

    fill = np.zeros((2 * depth, LANES), np.float32)
    fill[[0, cols, 2 * cols]] = STEP
    for part in (depth, depth + LANES):
        fill[part : part + PATCH * HALF, 0] = STEP
    fill = jnp.asarray(fill, bf16)

    shape = lambda *dims: jax.ShapeDtypeStruct(dims, f32)
    held = lambda *dims, kind=f32: pltpu.VMEM(dims, kind)
    far = lambda v: pltpu.with_memory_space_constraint(v, pltpu.HBM)
    here = lambda v: pltpu.with_memory_space_constraint(v, pltpu.VMEM)
    ring = lambda v, axis: lax.ppermute(v, axis, [(i, (i - 1) % lax.axis_size(axis)) for i in range(lax.axis_size(axis))])
    swap = lambda v: lax.ppermute(v, "gy", [(0, 1), (1, 0)])
    tall_x = chans * slots

    own, head, weight, shift = pl.pallas_call(
        functools.partial(pack_kernel, rows),
        in_specs=[ANY] * 5,
        out_specs=[VMEM] * 4,
        out_shape=[
            held(rows + rows * width // LANES, LANES), held(tiles * SUB, LANES), held(chans, width, kind=bf16),
            held(chans, LANES),
        ],
        scratch_shapes=[
            pltpu.VMEM((rows, SUB, width), bf16),
            pltpu.VMEM((2, tall, LANES), jnp.int32),
            pltpu.VMEM((2, SUB, tiles * LANES), jnp.int32),
            pltpu.VMEM((1, chans), f32),
            pltpu.SemaphoreType.DMA((7,)),
        ],
        compiler_params=ROOM,
        name="pack",
    )(*(far(v) for v in (features, labels, valid_mask, probe_weight.T, probe_bias.reshape(1, chans))))
    side = lax.ppermute(own, "gx", [(i, i - 1) for i in range(1, gx)])
    x, edge = pl.pallas_call(
        functools.partial(logits_kernel, rows, cols, chans, slots, 4),
        in_specs=[VMEM] * 5,
        out_specs=[VMEM] * 2,
        out_shape=[held(tall_x, LANES), held(chans + tiles * SUB + SUB, LANES)],
        compiler_params=ROOM,
        name="logits",
    )(*(here(v) for v in (features, weight, shift, head, own)))
    got = ring(edge, "gy")

    sums = (2 * chans * rows, LANES)
    stacked = held(tall_x, depth, kind=bf16)

    def inner(part, begin, steps, *args):
        outs = [
            ([held(*sums), held(SUB, LANES), stacked, held(SUB, LANES)], [VMEM] * 4, [VMEM] * 3),
            ([held(*sums), held(SUB, LANES)], [VMEM] * 2, [VMEM] * 4),
            ([held(tall_x, LANES), held(chans, LANES), held(SUB, LANES)], [VMEM] * 3, [VMEM] * 6),
        ][part]
        return pl.pallas_call(
            functools.partial(inner_kernel, rows, cols, chans, slots, groups, part, begin, tiles),
            grid=(steps,),
            in_specs=[VMEM] * 7 + outs[2],
            out_specs=outs[1],
            out_shape=outs[0],
            scratch_shapes=[
                pltpu.VMEM((2, tall_x, LANES), f32),
                pltpu.VMEM((2 * chans * count, SUB, LANES), f32),
                pltpu.VMEM((2 * count + 1, SUB, LANES), f32),
                pltpu.VMEM((2 * chans * rows, depth), bf16),
                pltpu.VMEM((tall + SUB, LANES), jnp.int32),
                pltpu.VMEM((3 * chans, rows, LANES), bf16),
                pltpu.SMEM((1,), f32),
            ] + ([pltpu.VMEM(sums, f32), stacked] if part == 2 else []),
            cost_estimate=pl.CostEstimate(flops=10**9, bytes_accessed=2 * 10**6, transcendentals=10**6),
            compiler_params=ROOM,
        )(*(here(v) for v in (got, lift, lift_end, back, back_end, labels, valid_mask)), *args)

    middle = tiles // 2 + 1
    total, loss, stack, floor = inner(0, 1, middle - 1, here(x), here(own), here(fill))
    side, total = lax.optimization_barrier((side, total))
    beside, beyond = pl.pallas_call(
        functools.partial(beside_kernel, rows, chans),
        in_specs=[VMEM] * 3,
        out_specs=[VMEM] * 2,
        out_shape=[held(rows, width, kind=bf16), held(chans + SUB, LANES)],
        compiler_params=ROOM,
        name="beside",
    )(here(side), here(weight), here(shift))
    corner = ring(beyond, "gy")
    total, loss = inner(1, middle, tiles - 1 - middle, *(here(v) for v in (total, loss, stack, floor)))
    grad, spill, loss = inner(2, tiles - 1, 2, *(here(v) for v in (x, beyond, corner, side, total, loss)))
    got = lax.ppermute(spill, "gy", [(i, (i + 1) % gy) for i in range(gy)])
    pack = (chans * width // 2 // LANES + SUB, LANES)
    mine, other = pl.pallas_call(
        functools.partial(grad_kernel, rows, cols, chans, slots),
        in_specs=[VMEM] * 5 + [SMEM],
        out_specs=[VMEM] * 2,
        out_shape=[held(*pack)] * 2,
        scratch_shapes=[pltpu.VMEM((tall_x, LANES), f32)],
        compiler_params=ROOM,
        name="grad",
    )(*(here(v) for v in (features, beside, grad, got, loss)), valid_count)

    total = mine + swap(other)
    step = 1
    while step < gx:
        total = total + lax.ppermute(total, "gx", [(i, i ^ step) for i in range(gx)])
        step *= 2
    loss, weight, bias = pl.pallas_call(
        functools.partial(final_kernel, chans),
        in_specs=[VMEM] * 2,
        out_specs=[VMEM] * 3,
        out_shape=[shape(1, 1), shape(chans, width), shape(1, chans)],
        compiler_params=ROOM,
        name="final",
    )(here(total), here(swap(total)))
    return loss.reshape(1), weight.T, bias.reshape(chans)


def solution(mesh):
    return jax.shard_map(
        body,
        mesh=mesh,
        in_specs=(
            P(("groups", "gy"), "gx", None),
            P(),
            P(),
            P(("groups", "gy"), "gx"),
            P(("groups", "gy"), "gx"),
            P(("groups", "gy"), "gx"),
        ),
        out_specs=(P("groups"), P("groups", None), P("groups")),
        check_vma=False,
    )
```

```python
import functools
import math

import jax
import jax.numpy as jnp
import numpy as np
from jax import lax
from jax.experimental import pallas as pl
from jax.experimental.pallas import tpu as pltpu
from jax.sharding import PartitionSpec as P

PATCH = 14
HALF = PATCH // 2
STEP = 2 * PATCH
LANES = 128
SUB = 8
LOG2E = 1.0 / math.log(2.0)
LN2 = math.log(2.0)
FLOOR = -100.0
f32 = jnp.float32
bf16 = jnp.bfloat16
VMEM = pl.BlockSpec(memory_space=pltpu.VMEM)
ANY = pl.BlockSpec(memory_space=pl.ANY)
ROOM = pltpu.CompilerParams(vmem_limit_bytes=16 * 2**20)
SMEM = pl.BlockSpec(memory_space=pltpu.SMEM)


def whole(shape):
    return pl.BlockSpec(shape, lambda *ids: (0,) * len(shape))


def column_tables(cols):
    tables = np.zeros((2, cols + 1, cols * PATCH), np.float32)
    for q in range(cols * PATCH):
        i, k = divmod((q if q >= HALF else q + cols * PATCH) - HALF, PATCH)
        far = 2 * k + 1
        for end in range(2):
            if end and i == cols - 1:
                tables[end, i + (k >= HALF), q] = STEP
            else:
                tables[end, i, q] = STEP - far
                tables[end, i + 1, q] = far
    return tables


def split3(x):
    hi = x.astype(bf16)
    rest = x - hi.astype(f32)
    mid = rest.astype(bf16)
    return hi, mid, (rest - mid.astype(f32)).astype(bf16)


def stack3(x):
    cols = LANES // 2
    lane = lax.broadcasted_iota(jnp.int32, x.shape, 1)
    hi, mid, low = (part.astype(f32) for part in split3(x))
    first = jnp.where(lane < cols, hi, pltpu.roll(mid, cols, 1))
    second = jnp.where(lane == cols + 1, pltpu.roll(mid, 1, 1), pltpu.roll(low, 2, 1))
    second = jnp.where(lane == cols, hi, jnp.where(lane < cols + 3, second, 0.0))
    second = jnp.where(lane < cols, low, second)
    return jnp.concatenate([first.astype(bf16), second.astype(bf16)], axis=1)


def pack_kernel(
    rows, f_ref, lab_ref, mask_ref, w_ref, bias_ref, out_ref, head_ref, weight_ref, shift_ref, f_vmem, l_vmem, h_vmem, b_vmem, sem,
):
    width = f_vmem.shape[2]
    tiles = head_ref.shape[0] // SUB
    copies = [
        pltpu.make_async_copy(lab_ref.at[:, pl.ds(0, LANES)], l_vmem.at[0], sem.at[0]),
        pltpu.make_async_copy(mask_ref.at[:, pl.ds(0, LANES)], l_vmem.at[1], sem.at[1]),
        pltpu.make_async_copy(f_ref.at[:, pl.ds(0, SUB)], f_vmem, sem.at[2]),
        pltpu.make_async_copy(lab_ref.at[pl.ds(0, SUB)], h_vmem.at[0], sem.at[3]),
        pltpu.make_async_copy(mask_ref.at[pl.ds(0, SUB)], h_vmem.at[1], sem.at[4]),
        pltpu.make_async_copy(w_ref, weight_ref, sem.at[5]),
        pltpu.make_async_copy(bias_ref, b_vmem, sem.at[6]),
    ]
    for copy in copies:
        copy.start()
    at = lax.broadcasted_iota(jnp.int32, (SUB, LANES), 1)
    for copy in copies:
        copy.wait()
    for b in range(rows // SUB):
        strip = jnp.full((SUB, LANES), -1.0, f32)
        for j in range(PATCH):
            pick = pl.ds(b * SUB * PATCH + j, SUB, stride=PATCH)
            lab = jnp.where(l_vmem[1, pick, :] != 0, l_vmem[0, pick, :], -1).astype(f32)
            here = (at >= j * HALF) & (at < j * HALF + HALF)
            strip = jnp.where(here, pltpu.roll(lab, j * HALF, 1) if j else lab, strip)
        out_ref[b * SUB : b * SUB + SUB, :] = strip
    for i in range(rows):
        line = f_vmem[i].astype(f32)
        for k in range(width // LANES):
            out_ref[rows + k * rows + i : rows + k * rows + i + 1, :] = line[0:1, k * LANES : k * LANES + LANES]
    for t in range(tiles):
        lanes = slice(t * LANES, t * LANES + LANES)
        head_ref[t * SUB : t * SUB + SUB, :] = jnp.where(h_vmem[1, :, lanes] != 0, h_vmem[0, :, lanes], -1).astype(f32)
    chans = shift_ref.shape[0]
    bias = jnp.concatenate([b_vmem[...], jnp.zeros((1, LANES - chans), f32)], axis=1)
    shift_ref[...] = jnp.broadcast_to(bias, (LANES, LANES)).T[0:chans, :]


def score_of(w_ref, shift_ref, block):
    score = lax.dot_general(w_ref[...], block, (((1,), (1,)), ((), ())), preferred_element_type=f32)
    score = score + jnp.concatenate([shift_ref[...]] * (block.shape[0] // LANES), axis=1)
    return (score - jnp.max(score, axis=0, keepdims=True)) * (LOG2E / STEP)


def logits_kernel(rows, cols, chans, slots, per, f_ref, w_ref, shift_ref, head_ref, side_ref, x_ref, e_ref):
    x_ref[...] = jnp.zeros_like(x_ref)
    lane = lax.broadcasted_iota(jnp.int32, (chans, LANES), 1)
    for step in range(rows // per):
        score = score_of(w_ref, shift_ref, f_ref[step * per : step * per + per].reshape(per * cols, f_ref.shape[2]))
        for k in range(per):
            i, off = step * per + k, k * cols
            tile = score[:, off // LANES * LANES : off // LANES * LANES + LANES]
            if off % LANES:
                tile = pltpu.roll(tile, LANES - off % LANES, 1)
            tile = jnp.where(lane < cols, tile, 0.0)
            x_ref[pl.ds(i, chans, stride=slots), :] = tile
            if i == 0:
                e_ref[0:chans, :] = tile
    e_ref[chans : chans + head_ref.shape[0], :] = head_ref[...]
    e_ref[chans + head_ref.shape[0] :, :] = side_ref[0:SUB, :]


def beside_kernel(rows, chans, side_ref, w_ref, shift_ref, beside_ref, out_ref):
    width = w_ref.shape[1]
    side = jnp.concatenate(
        [side_ref[rows + k * rows : rows + k * rows + rows, :] for k in range(width // LANES)], axis=1
    ).astype(bf16)
    beside_ref[...] = side
    side = jnp.concatenate([side, jnp.zeros((LANES - rows, width), bf16)], axis=0)
    out_ref[0:chans, :] = score_of(w_ref, shift_ref, side)
    out_ref[chans:, :] = side_ref[0:SUB, :]


def two_sums(item):
    totals, runs = [], []
    for half in range(2):
        total = run = None
        for m in reversed(range(HALF)):
            v = item(half, m)
            total = v if total is None else total + v
            if m:
                run = total if run is None else run + total
        totals.append(total)
        runs.append(run)
    return totals[0], totals[1], runs[0] - runs[1], totals[0] - totals[1]


def tally(packed, c, h_ref):
    one, none, mid = (jnp.asarray(v, bf16) for v in (1, 0, 0.5))
    mark = jnp.asarray(c, bf16) if isinstance(c, int) else c.astype(f32).astype(bf16)
    up, down, run, lean = two_sums(lambda half, m: jnp.where(packed[half * HALF + m] == mark, one, none))
    h_ref[3 * c] = up
    h_ref[3 * c + 1] = down
    h_ref[3 * c + 2] = run + lean * mid


def softmax_fast(groups, chans, slots, fold, w_ref, p_ref, packed, h_ref):
    sums = [None] * (2 * groups * HALF)
    for c in range(chans):
        tally(packed, c, h_ref)
        for b in range(groups):
            row = c * slots + SUB * b
            upper = w_ref[row : row + SUB, :]
            lower = w_ref[row + 1 : row + 1 + SUB, :]
            slope = (lower - upper) * fold[b]
            twice = slope + slope
            for half, (p, ratio) in enumerate(((upper + slope, twice), (lower - slope, -twice))):
                p, ratio = jnp.exp2(p), jnp.exp2(ratio)
                for m in range(HALF):
                    k = (half * groups + b) * HALF + m
                    if m:
                        p = p * ratio
                    p_ref[c * len(sums) + k] = p
                    sums[k] = p if sums[k] is None else sums[k] + p
    return sums


def softmax_slow(groups, chans, slots, fold, w_ref, p_ref, labels, weights):
    count = len(labels)
    sums, losses = [], jnp.zeros((SUB, LANES), f32)
    for k in range(count):
        half, b, m = k // (groups * HALF), k // HALF % groups, k % HALF

        def score(c, half=half, b=b, m=m):
            row = c * slots + SUB * b
            near = w_ref[pl.ds(row + half, SUB), :]
            away = w_ref[pl.ds(row + 1 - half, SUB), :]
            return near + (away - near) * fold[b] * (2 * m + 1.0)

        top = lax.fori_loop(1, chans, lambda c, t, score=score: jnp.maximum(t, score(c)), score(0))

        def take(c, carry, k=k, top=top, score=score):
            total, picked = carry
            shifted = score(c) - top
            p = jnp.exp2(shifted)
            p_ref[c * count + k] = p
            return total + p, jnp.where(labels[k] == c, shifted, picked)

        zero = jnp.zeros((SUB, LANES), f32)
        total, picked = lax.fori_loop(0, chans, take, (zero, zero))
        sums.append(total)
        losses = losses - weights[k] * picked
    return sums, losses


def pixels(groups, chans, slots, fold, lab_ref, fast, prepare, w_ref, p_ref, s_ref, lhs_ref, h_ref):
    count = 2 * groups * HALF
    labels = []
    for half in range(2):
        for b in range(groups):
            for m in range(HALF):
                k = PATCH - 1 - m if half else m
                labels.append(lab_ref[pl.ds(b * SUB * PATCH + HALF + k, SUB, stride=PATCH), :])
    weights = [jnp.where(lab >= 0, 1.0, 0.0) for lab in labels]
    packed = [
        jnp.concatenate([labels[(half * groups + b) * HALF + m] for b in range(groups)], axis=0).astype(f32).astype(bf16)
        for half in range(2)
        for m in range(HALF)
    ]

    @pl.when(fast)
    def _():
        sums = softmax_fast(groups, chans, slots, fold, w_ref, p_ref, packed, h_ref)
        for k in range(count):
            s_ref[k] = sums[k]
        s_ref[count] = jnp.zeros((SUB, LANES), f32)
        prepare()

    @pl.when(jnp.logical_not(fast))
    def _():
        sums, losses = softmax_slow(groups, chans, slots, fold, w_ref, p_ref, labels, weights)
        for k in range(count):
            s_ref[k] = sums[k]
        s_ref[count] = losses
        lax.fori_loop(0, chans, lambda c, _: tally(packed, c, h_ref), None)
        prepare()

    loss = jnp.zeros((SUB, LANES), f32)
    scale = []
    for k in range(count):
        total = s_ref[k]
        loss = loss + weights[k] * jnp.log(total)
        scale.append(weights[k] / total)
    picked = jnp.zeros((SUB, LANES), f32)
    tall = groups * SUB
    for c in range(chans):
        hits = [h_ref[3 * c + k].astype(f32) for k in range(3)]
        parts = [[], []]
        for b in range(groups):
            row = c * slots + SUB * b
            up, down, lean = (v[b * SUB : b * SUB + SUB] for v in hits)
            lean = lean * (fold[b] * 2.0)
            up, down = up - lean, down + lean
            picked = picked + up * w_ref[row : row + SUB, :] + down * w_ref[row + 1 : row + 1 + SUB, :]
            above, below, run, lean = two_sums(
                lambda half, m: p_ref[c * count + (half * groups + b) * HALF + m] * scale[(half * groups + b) * HALF + m]
            )
            lean = (run + lean * 0.5) * (fold[b] * 2.0)
            parts[0].append((above - up) - lean)
            parts[1].append((below - down) + lean)
        for kind in range(2):
            g = jnp.concatenate(parts[kind], axis=0)
            hi = g.astype(bf16)
            at = (kind * chans + c) * tall
            lhs_ref[at : at + tall, 0:LANES] = hi
            lhs_ref[at : at + tall, LANES:] = (g - hi.astype(f32)).astype(bf16)
    return loss + LN2 * jnp.where(fast, -picked, s_ref[count])


def first_columns(rows, groups, chans, slots, last_row, own_ref, got_ref, w_ref, p_ref, lhs_ref):
    lane = lax.broadcasted_iota(jnp.int32, (SUB, LANES), 1)
    sub = lax.broadcasted_iota(jnp.int32, (SUB, LANES), 0)
    turn = HALF * HALF
    share = jnp.zeros((SUB, LANES), f32)
    for k in range(PATCH):
        share = jnp.where(lane >= k * HALF, (2 * k + 1.0) / STEP, share)
    end = jnp.where(last_row & (sub == SUB - 1), jnp.where(lane < turn, 0.0, 1.0), share)
    shares = [share] * (groups - 1) + [end]
    tall = groups * SUB
    loss = jnp.zeros((SUB, LANES), f32)
    scale, labels = [], []
    for b in range(groups):
        upper = own_ref[b * SUB : b * SUB + SUB, :]
        at = (b + 1) * SUB
        lower = got_ref[got_ref.shape[0] - SUB :, :] if at == rows else own_ref[at : at + SUB, :]
        lower = jnp.where(sub == SUB - 1, pltpu.roll(lower, SUB - 1, 0), pltpu.roll(upper, SUB - 1, 0))
        label = jnp.where(lane < turn, pltpu.roll(upper, LANES - turn, 1), pltpu.roll(lower, turn, 1))
        label = jnp.where(lane < PATCH * HALF, label, -1.0).astype(jnp.int32)
        top = None
        for c in range(chans):
            row = c * slots + SUB * b
            v = w_ref[row : row + SUB, :]
            v = v + (w_ref[row + 1 : row + 1 + SUB, :] - v) * shares[b]
            p_ref[c * groups + b] = v
            top = v if top is None else jnp.maximum(top, v)
        total = picked = jnp.zeros((SUB, LANES), f32)
        for c in range(chans):
            v = p_ref[c * groups + b] - top
            picked = jnp.where(label == c, v, picked)
            v = jnp.exp2(v)
            p_ref[c * groups + b] = v
            total = total + v
        weight = jnp.where(label >= 0, 1.0, 0.0)
        loss = loss + weight * (jnp.log(total) - LN2 * picked)
        scale.append(weight / total)
        labels.append(label)
    for c in range(chans):
        parts = [[], []]
        for b in range(groups):
            g = p_ref[c * groups + b] * scale[b] - jnp.where(labels[b] == c, 1.0, 0.0)
            below = g * shares[b]
            parts[0].append(g - below)
            parts[1].append(below)
        for kind in range(2):
            g = jnp.concatenate(parts[kind], axis=0)
            hi = g.astype(bf16)
            at = (kind * chans + c) * tall
            lhs_ref[at : at + tall, 0:LANES] = hi
            lhs_ref[at : at + tall, LANES:] = (g - hi.astype(f32)).astype(bf16)
    return loss


def inner_kernel(rows, cols, chans, slots, groups, part, begin, tiles, *refs):
    (got_ref, lift_ref, back_ref, lab_ref, mask_ref), refs = refs[:5], refs[5:]
    if part == 0:
        (x_ref, own_ref, fill_ref, sum_ref, loss_ref, stack_ref, floor_out_ref), refs = refs[:7], refs[7:]
    elif part == 1:
        (sum_in_ref, loss_in_ref, stack_ref, floor_in_ref, sum_ref, loss_ref), refs = refs[:6], refs[6:]
    else:
        (x_ref, beyond_ref, corner_ref, strip_ref, sum_in_ref, loss_in_ref, lift_end_ref, back_end_ref), refs = (
            refs[:8], refs[8:],
        )
        (out_ref, spill_ref, loss_ref), refs = refs[:3], refs[3:]
    (w_ref, p_ref, s_ref, lhs_ref, tile_ref, h_ref, floor_ref), refs = refs[:7], refs[7:]
    if part == 2:
        sum_ref, stack_ref = refs
    step = pl.program_id(0)
    steps = pl.num_programs(0)
    now = lax.rem(step, 2)
    which = lax.rem(step + begin, tiles)
    last_col = lax.axis_index("gx") == lax.axis_size("gx") - 1
    last_row = lax.axis_index("gy") == lax.axis_size("gy") - 1
    tall = rows * PATCH
    lane = lax.broadcasted_iota(jnp.int32, (SUB, LANES), 1)
    lanes = pl.ds(pl.multiple_of(which * LANES, LANES), LANES)

    def lift(at):
        lanes = pl.ds(pl.multiple_of(at * LANES, LANES), LANES)
        table = lift_ref[:, lanes]
        if part == 2:
            order = jnp.minimum(lax.rem(at + 1, tiles), 1)
            end = lift_end_ref[:, pl.ds(pl.multiple_of(order * LANES, LANES), LANES)]
            table = jnp.where(last_col, end, table)
        return jnp.dot(stack_ref[...], table, preferred_element_type=f32)

    @pl.when(step == 0)
    def _():
        if part == 0:
            sum_ref[...] = jnp.zeros_like(sum_ref)
            loss_ref[...] = jnp.zeros_like(loss_ref)
        else:
            sum_ref[...] = sum_in_ref[...]
            loss_ref[...] = loss_in_ref[...]
        if part != 1:
            w_ref[0] = x_ref[...]
            w_ref[0, pl.ds(rows, chans, stride=slots), :] = got_ref[0:chans, :]
            if part == 2:
                wide = lax.broadcasted_iota(jnp.int32, (chans, LANES), 1)
                for i in range(rows + 1):
                    column = beyond_ref[0:chans, :] if i < rows else corner_ref[0:chans, :]
                    column = pltpu.roll(column, cols - i if i < rows else cols, 1)
                    pick = pl.ds(i, chans, stride=slots)
                    w_ref[0, pick, :] = jnp.where(wide == cols, column, w_ref[0, pick, :])
            full = w_ref[0]
            floor_ref[0] = jnp.min(full) * STEP
            stack_ref[...] = stack3(full)
            if part == 0:
                floor_out_ref[...] = jnp.full((SUB, LANES), floor_ref[0], f32)
        else:
            floor_ref[0] = jnp.min(floor_in_ref[...])
        w_ref[0] = lift(which)

    tile_ref[0:tall, :] = jnp.where(mask_ref[:, lanes] != 0, lab_ref[:, lanes], -1)
    tile_ref[tall : tall + SUB, :] = got_ref[pl.ds(pl.multiple_of(chans + which * SUB, SUB), SUB), :].astype(jnp.int32)

    if part == 2:

        @pl.when(which == 0)
        def _():
            for j in range(PATCH):
                for b in range(groups):
                    pick = pl.ds(b * SUB * PATCH + j, SUB, stride=PATCH)
                    strip = strip_ref[b * SUB : b * SUB + SUB, :]
                    strip = pltpu.roll(strip, LANES - j * HALF, 1) if j else strip
                    strip = jnp.where(last_col, -1.0, strip)
                    tile_ref[pick, :] = jnp.where(lane < HALF, strip.astype(jnp.int32), tile_ref[pick, :])
            for j in range(HALF):
                strip = corner_ref[chans : chans + 1, :]
                strip = pltpu.roll(strip, LANES - j * HALF, 1) if j else strip
                strip = jnp.where(last_col, -1.0, strip)
                row = tile_ref[tall + j : tall + j + 1, :]
                tile_ref[tall + j : tall + j + 1, :] = jnp.where(lane[0:1] < HALF, strip.astype(jnp.int32), row)

    flat = jnp.full((SUB, LANES), 1.0 / STEP, f32)
    sub = lax.broadcasted_iota(jnp.int32, (SUB, LANES), 0)
    fold = [flat] * (groups - 1) + [jnp.where(last_row & (sub == SUB - 1), 0.0, flat)]
    fast = floor_ref[0] >= FLOOR

    def prepare():
        w_ref[1 - now] = lift(lax.rem(which + 1, tiles))

    loss_ref[...] += pixels(groups, chans, slots, fold, tile_ref, fast, prepare, w_ref.at[now], p_ref, s_ref, lhs_ref, h_ref)
    depth = 2 * LANES
    deep = pl.ds(pl.multiple_of(which * depth, depth), depth)
    table = back_ref[deep, :]
    if part == 2:
        end = back_end_ref[pl.ds(pl.multiple_of(lax.rem(which + 1, tiles) * depth, depth), depth), :]
        table = jnp.where(last_col, end, table)
    sum_ref[...] += jnp.dot(lhs_ref[...], table, preferred_element_type=f32)

    if part == 0:

        @pl.when((step == steps - 1) & (lax.axis_index("gx") == 0))
        def _():
            depth = stack_ref.shape[1]
            w_ref[1 - now] = jnp.dot(stack_ref[...], fill_ref[0:depth, :], preferred_element_type=f32)
            loss_ref[...] += first_columns(rows, groups, chans, slots, last_row, own_ref, got_ref, w_ref.at[1 - now], p_ref, lhs_ref)
            sum_ref[...] += jnp.dot(lhs_ref[...], fill_ref[depth:, :], preferred_element_type=f32)

    if part == 2:

        @pl.when(step == steps - 1)
        def _():
            w_ref[0] = jnp.zeros_like(w_ref[0])
            high = groups * SUB
            for c in range(chans):
                for kind in range(2):
                    at = (kind * chans + c) * high
                    row = c * slots + kind
                    w_ref[0, row : row + high, :] += sum_ref[at : at + high, :]
            out_ref[...] = w_ref[0] * (1.0 / STEP)
            spill_ref[...] = out_ref[pl.ds(rows, chans, stride=slots), :]


def grad_kernel(
    rows, cols, chans, slots, f_ref, beside_ref, g_ref, got_ref, loss_ref, count_ref, mine_ref, other_ref, sum_ref,
):
    row = lax.axis_index("gy")
    sum_ref[...] = g_ref[...]
    sum_ref[pl.ds(0, chans, stride=slots), :] += got_ref[...]
    lane = lax.broadcasted_iota(jnp.int32, (chans, LANES), 1)
    share = LANES // cols
    edge = jnp.zeros((chans, LANES), f32)
    tiles = []
    total = jnp.zeros((chans, LANES), f32)
    for k in range(0, rows, share):
        tile = None
        for r in range(share):
            piece = sum_ref[pl.ds(k + r, chans, stride=slots), :]
            total = total + piece
            edge = jnp.where(lane == k + r, pltpu.roll(piece, (k + r - cols) % LANES, 1), edge)
            if r:
                piece = pltpu.roll(piece, r * cols, 1)
            tile = piece if tile is None else jnp.where(lane < r * cols, tile, piece)
        tiles.append(tile.astype(bf16))
    block = f_ref[...].reshape(rows * cols, f_ref.shape[2])
    out = jnp.dot(jnp.concatenate(tiles, axis=1), block, preferred_element_type=f32)
    beside = jnp.concatenate([beside_ref[...], jnp.zeros((LANES - rows, f_ref.shape[2]), bf16)], axis=0)
    out = out + jnp.dot(edge.astype(bf16), beside, preferred_element_type=f32)
    total = jnp.where(lane <= cols, total, 0.0)
    square = jnp.concatenate([total, jnp.zeros((LANES - chans, LANES), f32)], axis=0)
    bias = jnp.sum(square.T, axis=0, keepdims=True)
    at = lax.broadcasted_iota(jnp.int32, (SUB, LANES), 0)
    rest = jnp.where(at == 1, jnp.sum(loss_ref[...]), count_ref[0, 0].astype(f32))
    stats = jnp.where(at == 0, bias, jnp.where(at < 3, rest, 0.0))
    pieces = out.shape[1] // LANES // 2
    for k in range(pieces):
        low = out[:, k * LANES : k * LANES + LANES]
        high = out[:, (pieces + k) * LANES : (pieces + k + 1) * LANES]
        mine_ref[k * chans : k * chans + chans, :] = jnp.where(row == 0, low, high)
        other_ref[k * chans : k * chans + chans, :] = jnp.where(row == 0, high, low)
    mine_ref[pieces * chans :, :] = stats
    other_ref[pieces * chans :, :] = stats


def final_kernel(chans, y_ref, z_ref, loss_ref, weight_ref, bias_ref):
    pieces = y_ref.shape[0] // chans
    lower = lax.axis_index("gy") == 0
    stats = y_ref[pieces * chans :, :]
    total = stats[2:3, 0:1]
    for k in range(pieces):
        y = y_ref[k * chans : k * chans + chans, :]
        z = z_ref[k * chans : k * chans + chans, :]
        weight_ref[:, k * LANES : k * LANES + LANES] = jnp.where(lower, y, z) / total
        weight_ref[:, (pieces + k) * LANES : (pieces + k + 1) * LANES] = jnp.where(lower, z, y) / total
    loss_ref[...] = stats[1:2, 0:1] / total
    bias_ref[...] = stats[0:1, 0:chans] / total


def body(features, probe_weight, probe_bias, labels, valid_mask, valid_count):
    rows, cols, width = features.shape
    chans = probe_weight.shape[1]
    gx, gy = lax.axis_size("gx"), lax.axis_size("gy")
    if gy != 2 or rows % SUB or 2 * cols != LANES or cols * PATCH % LANES or width % (2 * LANES) or gx & (gx - 1):
        raise ValueError("unsupported tile")
    groups = rows // SUB
    slots = rows + SUB
    count = groups * HALF
    tiles = cols * PATCH // LANES
    tall = rows * PATCH
    depth = 2 * LANES

    def forward(table):
        out = np.zeros((depth, table.shape[1]), np.float32)
        for k in range(3):
            out[k * cols : k * cols + cols] = table[:cols]
            out[3 * cols + k] = table[cols]
        return out

    def backward(table):
        out = np.zeros((table.shape[1] // LANES, 2, LANES, LANES), np.float32)
        out[:, :, :, : cols + 1] = table.T.reshape(-1, 1, LANES, cols + 1)
        return out.reshape(-1, LANES)

    inside, ending = column_tables(cols)
    ending = np.concatenate([ending[:, -LANES:], ending[:, :LANES]], axis=1)
    lift, lift_end, back, back_end = (
        jnp.asarray(t, bf16) for t in (forward(inside), forward(ending), backward(inside), backward(ending))
    )

    fill = np.zeros((2 * depth, LANES), np.float32)
    fill[[0, cols, 2 * cols]] = STEP
    for part in (depth, depth + LANES):
        fill[part : part + PATCH * HALF, 0] = STEP
    fill = jnp.asarray(fill, bf16)

    shape = lambda *dims: jax.ShapeDtypeStruct(dims, f32)
    held = lambda *dims, kind=f32: pltpu.VMEM(dims, kind)
    far = lambda v: pltpu.with_memory_space_constraint(v, pltpu.HBM)
    here = lambda v: pltpu.with_memory_space_constraint(v, pltpu.VMEM)
    ring = lambda v, axis: lax.ppermute(v, axis, [(i, (i - 1) % lax.axis_size(axis)) for i in range(lax.axis_size(axis))])
    swap = lambda v: lax.ppermute(v, "gy", [(0, 1), (1, 0)])
    tall_x = chans * slots

    own, head, weight, shift = pl.pallas_call(
        functools.partial(pack_kernel, rows),
        in_specs=[ANY] * 5,
        out_specs=[VMEM] * 4,
        out_shape=[
            held(rows + rows * width // LANES, LANES), held(tiles * SUB, LANES), held(chans, width, kind=bf16),
            held(chans, LANES),
        ],
        scratch_shapes=[
            pltpu.VMEM((rows, SUB, width), bf16),
            pltpu.VMEM((2, tall, LANES), jnp.int32),
            pltpu.VMEM((2, SUB, tiles * LANES), jnp.int32),
            pltpu.VMEM((1, chans), f32),
            pltpu.SemaphoreType.DMA((7,)),
        ],
        compiler_params=ROOM,
        name="pack",
    )(*(far(v) for v in (features, labels, valid_mask, probe_weight.T, probe_bias.reshape(1, chans))))
    side = lax.ppermute(own, "gx", [(i, i - 1) for i in range(1, gx)])
    x, edge = pl.pallas_call(
        functools.partial(logits_kernel, rows, cols, chans, slots, 4),
        in_specs=[VMEM] * 5,
        out_specs=[VMEM] * 2,
        out_shape=[held(tall_x, LANES), held(chans + tiles * SUB + SUB, LANES)],
        compiler_params=ROOM,
        name="logits",
    )(*(here(v) for v in (features, weight, shift, head, own)))
    got = ring(edge, "gy")

    sums = (2 * chans * rows, LANES)
    stacked = held(tall_x, depth, kind=bf16)

    def inner(part, begin, steps, *args):
        outs = [
            ([held(*sums), held(SUB, LANES), stacked, held(SUB, LANES)], [VMEM] * 4, [VMEM] * 3),
            ([held(*sums), held(SUB, LANES)], [VMEM] * 2, [VMEM] * 4),
            ([held(tall_x, LANES), held(chans, LANES), held(SUB, LANES)], [VMEM] * 3, [VMEM] * 8),
        ][part]
        return pl.pallas_call(
            functools.partial(inner_kernel, rows, cols, chans, slots, groups, part, begin, tiles),
            grid=(steps,),
            in_specs=[VMEM] * 5 + outs[2],
            out_specs=outs[1],
            out_shape=outs[0],
            scratch_shapes=[
                pltpu.VMEM((2, tall_x, LANES), f32),
                pltpu.VMEM((2 * chans * count, SUB, LANES), f32),
                pltpu.VMEM((2 * count + 1, SUB, LANES), f32),
                pltpu.VMEM((2 * chans * rows, depth), bf16),
                pltpu.VMEM((tall + SUB, LANES), jnp.int32),
                pltpu.VMEM((3 * chans, rows, LANES), bf16),
                pltpu.SMEM((1,), f32),
            ] + ([pltpu.VMEM(sums, f32), stacked] if part == 2 else []),
            cost_estimate=pl.CostEstimate(flops=10**9, bytes_accessed=2 * 10**6, transcendentals=10**6),
            compiler_params=ROOM,
            name=("inner_head", "inner_middle", "inner_tail")[part],
        )(*(here(v) for v in (got, lift, back, labels, valid_mask)), *args)

    middle = tiles // 2 + 1
    total, loss, stack, floor = inner(0, 1, middle - 1, here(x), here(own), here(fill))
    side, total = lax.optimization_barrier((side, total))
    beside, beyond = pl.pallas_call(
        functools.partial(beside_kernel, rows, chans),
        in_specs=[VMEM] * 3,
        out_specs=[VMEM] * 2,
        out_shape=[held(rows, width, kind=bf16), held(chans + SUB, LANES)],
        compiler_params=ROOM,
        name="beside",
    )(here(side), here(weight), here(shift))
    corner = ring(beyond, "gy")
    total, loss = inner(1, middle, tiles - 1 - middle, *(here(v) for v in (total, loss, stack, floor)))
    grad, spill, loss = inner(2, tiles - 1, 2, *(here(v) for v in (x, beyond, corner, side, total, loss, lift_end, back_end)))
    got = lax.ppermute(spill, "gy", [(i, (i + 1) % gy) for i in range(gy)])
    pack = (chans * width // 2 // LANES + SUB, LANES)
    mine, other = pl.pallas_call(
        functools.partial(grad_kernel, rows, cols, chans, slots),
        in_specs=[VMEM] * 5 + [SMEM],
        out_specs=[VMEM] * 2,
        out_shape=[held(*pack)] * 2,
        scratch_shapes=[pltpu.VMEM((tall_x, LANES), f32)],
        compiler_params=ROOM,
        name="grad",
    )(*(here(v) for v in (features, beside, grad, got, loss)), valid_count)

    total = mine + swap(other)
    step = 1
    while step < gx:
        total = total + lax.ppermute(total, "gx", [(i, i ^ step) for i in range(gx)])
        step *= 2
    loss, weight, bias = pl.pallas_call(
        functools.partial(final_kernel, chans),
        in_specs=[VMEM] * 2,
        out_specs=[VMEM] * 3,
        out_shape=[shape(1, 1), shape(chans, width), shape(1, chans)],
        compiler_params=ROOM,
        name="final",
    )(here(total), here(swap(total)))
    return loss.reshape(1), weight.T, bias.reshape(chans)


def solution(mesh):
    return jax.shard_map(
        body,
        mesh=mesh,
        in_specs=(
            P(("groups", "gy"), "gx", None),
            P(),
            P(),
            P(("groups", "gy"), "gx"),
            P(("groups", "gy"), "gx"),
            P(("groups", "gy"), "gx"),
        ),
        out_specs=(P("groups"), P("groups", None), P("groups")),
        check_vma=False,
    )
```

```python
import functools
import math

import jax
import jax.numpy as jnp
import numpy as np
from jax import lax
from jax.experimental import pallas as pl
from jax.experimental.pallas import tpu as pltpu
from jax.sharding import PartitionSpec as P

PATCH = 14
HALF = PATCH // 2
STEP = 2 * PATCH
LANES = 128
SUB = 8
LOG2E = 1.0 / math.log(2.0)
LN2 = math.log(2.0)
FLOOR = -100.0
f32 = jnp.float32
bf16 = jnp.bfloat16
VMEM = pl.BlockSpec(memory_space=pltpu.VMEM)
ANY = pl.BlockSpec(memory_space=pl.ANY)
ROOM = pltpu.CompilerParams(vmem_limit_bytes=16 * 2**20)
SMEM = pl.BlockSpec(memory_space=pltpu.SMEM)


def whole(shape):
    return pl.BlockSpec(shape, lambda *ids: (0,) * len(shape))


def column_tables(cols):
    tables = np.zeros((2, cols + 1, cols * PATCH), np.float32)
    for q in range(cols * PATCH):
        i, k = divmod((q if q >= HALF else q + cols * PATCH) - HALF, PATCH)
        far = 2 * k + 1
        for end in range(2):
            if end and i == cols - 1:
                tables[end, i + (k >= HALF), q] = STEP
            else:
                tables[end, i, q] = STEP - far
                tables[end, i + 1, q] = far
    return tables


def split3(x):
    hi = x.astype(bf16)
    rest = x - hi.astype(f32)
    mid = rest.astype(bf16)
    return hi, mid, (rest - mid.astype(f32)).astype(bf16)


def stack3(x):
    cols = LANES // 2
    lane = lax.broadcasted_iota(jnp.int32, x.shape, 1)
    hi, mid, low = (part.astype(f32) for part in split3(x))
    first = jnp.where(lane < cols, hi, pltpu.roll(mid, cols, 1))
    second = jnp.where(lane == cols + 1, pltpu.roll(mid, 1, 1), pltpu.roll(low, 2, 1))
    second = jnp.where(lane == cols, hi, jnp.where(lane < cols + 3, second, 0.0))
    second = jnp.where(lane < cols, low, second)
    return jnp.concatenate([first.astype(bf16), second.astype(bf16)], axis=1)


def pack_kernel(
    rows, f_ref, lab_ref, mask_ref, w_ref, bias_ref, out_ref, head_ref, weight_ref, shift_ref, f_vmem, l_vmem, h_vmem, b_vmem, sem,
):
    width = f_vmem.shape[2]
    tiles = head_ref.shape[0] // SUB
    copies = [
        pltpu.make_async_copy(lab_ref.at[:, pl.ds(0, LANES)], l_vmem.at[0], sem.at[0]),
        pltpu.make_async_copy(mask_ref.at[:, pl.ds(0, LANES)], l_vmem.at[1], sem.at[1]),
        pltpu.make_async_copy(f_ref.at[:, pl.ds(0, SUB)], f_vmem, sem.at[2]),
        pltpu.make_async_copy(lab_ref.at[pl.ds(0, SUB)], h_vmem.at[0], sem.at[3]),
        pltpu.make_async_copy(mask_ref.at[pl.ds(0, SUB)], h_vmem.at[1], sem.at[4]),
        pltpu.make_async_copy(w_ref, weight_ref, sem.at[5]),
        pltpu.make_async_copy(bias_ref, b_vmem, sem.at[6]),
    ]
    for copy in copies:
        copy.start()
    at = lax.broadcasted_iota(jnp.int32, (SUB, LANES), 1)
    for copy in copies:
        copy.wait()
    for b in range(rows // SUB):
        strip = jnp.full((SUB, LANES), -1.0, f32)
        for j in range(PATCH):
            pick = pl.ds(b * SUB * PATCH + j, SUB, stride=PATCH)
            lab = jnp.where(l_vmem[1, pick, :] != 0, l_vmem[0, pick, :], -1).astype(f32)
            here = (at >= j * HALF) & (at < j * HALF + HALF)
            strip = jnp.where(here, pltpu.roll(lab, j * HALF, 1) if j else lab, strip)
        out_ref[b * SUB : b * SUB + SUB, :] = strip
    for i in range(rows):
        line = f_vmem[i].astype(f32)
        for k in range(width // LANES):
            out_ref[rows + k * rows + i : rows + k * rows + i + 1, :] = line[0:1, k * LANES : k * LANES + LANES]
    for t in range(tiles):
        lanes = slice(t * LANES, t * LANES + LANES)
        head_ref[t * SUB : t * SUB + SUB, :] = jnp.where(h_vmem[1, :, lanes] != 0, h_vmem[0, :, lanes], -1).astype(f32)
    chans = shift_ref.shape[0]
    bias = jnp.concatenate([b_vmem[...], jnp.zeros((1, LANES - chans), f32)], axis=1)
    shift_ref[...] = jnp.broadcast_to(bias, (LANES, LANES)).T[0:chans, :]


def score_of(w_ref, shift_ref, block):
    score = lax.dot_general(w_ref[...], block, (((1,), (1,)), ((), ())), preferred_element_type=f32)
    score = score + jnp.concatenate([shift_ref[...]] * (block.shape[0] // LANES), axis=1)
    return (score - jnp.max(score, axis=0, keepdims=True)) * (LOG2E / STEP)


def logits_kernel(rows, cols, chans, slots, per, f_ref, w_ref, shift_ref, head_ref, side_ref, x_ref, e_ref):
    x_ref[...] = jnp.zeros_like(x_ref)
    lane = lax.broadcasted_iota(jnp.int32, (chans, LANES), 1)
    for step in range(rows // per):
        score = score_of(w_ref, shift_ref, f_ref[step * per : step * per + per].reshape(per * cols, f_ref.shape[2]))
        for k in range(per):
            i, off = step * per + k, k * cols
            tile = score[:, off // LANES * LANES : off // LANES * LANES + LANES]
            if off % LANES:
                tile = pltpu.roll(tile, LANES - off % LANES, 1)
            tile = jnp.where(lane < cols, tile, 0.0)
            x_ref[pl.ds(i, chans, stride=slots), :] = tile
            if i == 0:
                e_ref[0:chans, :] = tile
    e_ref[chans : chans + head_ref.shape[0], :] = head_ref[...]
    e_ref[chans + head_ref.shape[0] :, :] = side_ref[0:SUB, :]


def beside_kernel(rows, chans, side_ref, w_ref, shift_ref, beside_ref, out_ref):
    width = w_ref.shape[1]
    side = jnp.concatenate(
        [side_ref[rows + k * rows : rows + k * rows + rows, :] for k in range(width // LANES)], axis=1
    ).astype(bf16)
    beside_ref[...] = side
    side = jnp.concatenate([side, jnp.zeros((LANES - rows, width), bf16)], axis=0)
    out_ref[0:chans, :] = score_of(w_ref, shift_ref, side)
    out_ref[chans:, :] = side_ref[0:SUB, :]


def two_sums(item):
    totals, runs = [], []
    for half in range(2):
        total = run = None
        for m in reversed(range(HALF)):
            v = item(half, m)
            total = v if total is None else total + v
            if m:
                run = total if run is None else run + total
        totals.append(total)
        runs.append(run)
    return totals[0], totals[1], runs[0] - runs[1], totals[0] - totals[1]


def tally(packed, c, h_ref):
    one, none, mid = (jnp.asarray(v, bf16) for v in (1, 0, 0.5))
    mark = jnp.asarray(c, bf16) if isinstance(c, int) else c.astype(f32).astype(bf16)
    up, down, run, lean = two_sums(lambda half, m: jnp.where(packed[half * HALF + m] == mark, one, none))
    h_ref[3 * c] = up
    h_ref[3 * c + 1] = down
    h_ref[3 * c + 2] = run + lean * mid


def softmax_fast(groups, chans, slots, fold, w_ref, p_ref, packed, h_ref):
    sums = [None] * (2 * groups * HALF)
    for c in range(chans):
        tally(packed, c, h_ref)
        for b in range(groups):
            row = c * slots + SUB * b
            upper = w_ref[row : row + SUB, :]
            lower = w_ref[row + 1 : row + 1 + SUB, :]
            slope = (lower - upper) * fold[b]
            twice = slope + slope
            for half, (p, ratio) in enumerate(((upper + slope, twice), (lower - slope, -twice))):
                p, ratio = jnp.exp2(p), jnp.exp2(ratio)
                for m in range(HALF):
                    k = (half * groups + b) * HALF + m
                    if m:
                        p = p * ratio
                    p_ref[c * len(sums) + k] = p
                    sums[k] = p if sums[k] is None else sums[k] + p
    return sums


def softmax_slow(groups, chans, slots, fold, w_ref, p_ref, labels, weights):
    count = len(labels)
    sums, losses = [], jnp.zeros((SUB, LANES), f32)
    for k in range(count):
        half, b, m = k // (groups * HALF), k // HALF % groups, k % HALF

        def score(c, half=half, b=b, m=m):
            row = c * slots + SUB * b
            near = w_ref[pl.ds(row + half, SUB), :]
            away = w_ref[pl.ds(row + 1 - half, SUB), :]
            return near + (away - near) * fold[b] * (2 * m + 1.0)

        top = lax.fori_loop(1, chans, lambda c, t, score=score: jnp.maximum(t, score(c)), score(0))

        def take(c, carry, k=k, top=top, score=score):
            total, picked = carry
            shifted = score(c) - top
            p = jnp.exp2(shifted)
            p_ref[c * count + k] = p
            return total + p, jnp.where(labels[k] == c, shifted, picked)

        zero = jnp.zeros((SUB, LANES), f32)
        total, picked = lax.fori_loop(0, chans, take, (zero, zero))
        sums.append(total)
        losses = losses - weights[k] * picked
    return sums, losses


def pixels(groups, chans, slots, fold, lab_ref, fast, prepare, w_ref, p_ref, s_ref, lhs_ref, h_ref):
    count = 2 * groups * HALF
    labels = []
    for half in range(2):
        for b in range(groups):
            for m in range(HALF):
                k = PATCH - 1 - m if half else m
                labels.append(lab_ref[pl.ds(b * SUB * PATCH + HALF + k, SUB, stride=PATCH), :])
    weights = [jnp.where(lab >= 0, 1.0, 0.0) for lab in labels]
    packed = [
        jnp.concatenate([labels[(half * groups + b) * HALF + m] for b in range(groups)], axis=0).astype(f32).astype(bf16)
        for half in range(2)
        for m in range(HALF)
    ]

    @pl.when(fast)
    def _():
        sums = softmax_fast(groups, chans, slots, fold, w_ref, p_ref, packed, h_ref)
        for k in range(count):
            s_ref[k] = sums[k]
        s_ref[count] = jnp.zeros((SUB, LANES), f32)
        prepare()

    @pl.when(jnp.logical_not(fast))
    def _():
        sums, losses = softmax_slow(groups, chans, slots, fold, w_ref, p_ref, labels, weights)
        for k in range(count):
            s_ref[k] = sums[k]
        s_ref[count] = losses
        lax.fori_loop(0, chans, lambda c, _: tally(packed, c, h_ref), None)
        prepare()

    loss = jnp.zeros((SUB, LANES), f32)
    scale = []
    for k in range(count):
        total = s_ref[k]
        loss = loss + weights[k] * jnp.log(total)
        scale.append(weights[k] / total)
    picked = jnp.zeros((SUB, LANES), f32)
    tall = groups * SUB
    for c in range(chans):
        hits = [h_ref[3 * c + k].astype(f32) for k in range(3)]
        parts = [[], []]
        for b in range(groups):
            row = c * slots + SUB * b
            up, down, lean = (v[b * SUB : b * SUB + SUB] for v in hits)
            lean = lean * (fold[b] * 2.0)
            up, down = up - lean, down + lean
            picked = picked + up * w_ref[row : row + SUB, :] + down * w_ref[row + 1 : row + 1 + SUB, :]
            above, below, run, lean = two_sums(
                lambda half, m: p_ref[c * count + (half * groups + b) * HALF + m] * scale[(half * groups + b) * HALF + m]
            )
            lean = (run + lean * 0.5) * (fold[b] * 2.0)
            parts[0].append((above - up) - lean)
            parts[1].append((below - down) + lean)
        for kind in range(2):
            g = jnp.concatenate(parts[kind], axis=0)
            hi = g.astype(bf16)
            at = (kind * chans + c) * tall
            lhs_ref[at : at + tall, 0:LANES] = hi
            lhs_ref[at : at + tall, LANES:] = (g - hi.astype(f32)).astype(bf16)
    return loss + LN2 * jnp.where(fast, -picked, s_ref[count])


def first_columns(rows, groups, chans, slots, last_row, own_ref, got_ref, w_ref, p_ref, lhs_ref):
    lane = lax.broadcasted_iota(jnp.int32, (SUB, LANES), 1)
    sub = lax.broadcasted_iota(jnp.int32, (SUB, LANES), 0)
    turn = HALF * HALF
    share = jnp.zeros((SUB, LANES), f32)
    for k in range(PATCH):
        share = jnp.where(lane >= k * HALF, (2 * k + 1.0) / STEP, share)
    end = jnp.where(last_row & (sub == SUB - 1), jnp.where(lane < turn, 0.0, 1.0), share)
    shares = [share] * (groups - 1) + [end]
    tall = groups * SUB
    loss = jnp.zeros((SUB, LANES), f32)
    scale, labels = [], []
    for b in range(groups):
        upper = own_ref[b * SUB : b * SUB + SUB, :]
        at = (b + 1) * SUB
        lower = got_ref[got_ref.shape[0] - SUB :, :] if at == rows else own_ref[at : at + SUB, :]
        lower = jnp.where(sub == SUB - 1, pltpu.roll(lower, SUB - 1, 0), pltpu.roll(upper, SUB - 1, 0))
        label = jnp.where(lane < turn, pltpu.roll(upper, LANES - turn, 1), pltpu.roll(lower, turn, 1))
        label = jnp.where(lane < PATCH * HALF, label, -1.0).astype(jnp.int32)
        top = None
        for c in range(chans):
            row = c * slots + SUB * b
            v = w_ref[row : row + SUB, :]
            v = v + (w_ref[row + 1 : row + 1 + SUB, :] - v) * shares[b]
            p_ref[c * groups + b] = v
            top = v if top is None else jnp.maximum(top, v)
        total = picked = jnp.zeros((SUB, LANES), f32)
        for c in range(chans):
            v = p_ref[c * groups + b] - top
            picked = jnp.where(label == c, v, picked)
            v = jnp.exp2(v)
            p_ref[c * groups + b] = v
            total = total + v
        weight = jnp.where(label >= 0, 1.0, 0.0)
        loss = loss + weight * (jnp.log(total) - LN2 * picked)
        scale.append(weight / total)
        labels.append(label)
    for c in range(chans):
        parts = [[], []]
        for b in range(groups):
            g = p_ref[c * groups + b] * scale[b] - jnp.where(labels[b] == c, 1.0, 0.0)
            below = g * shares[b]
            parts[0].append(g - below)
            parts[1].append(below)
        for kind in range(2):
            g = jnp.concatenate(parts[kind], axis=0)
            hi = g.astype(bf16)
            at = (kind * chans + c) * tall
            lhs_ref[at : at + tall, 0:LANES] = hi
            lhs_ref[at : at + tall, LANES:] = (g - hi.astype(f32)).astype(bf16)
    return loss


def inner_kernel(rows, cols, chans, slots, groups, part, begin, tiles, *refs):
    (got_ref, lift_ref, back_ref, lab_ref, mask_ref), refs = refs[:5], refs[5:]
    if part == 0:
        (x_ref, own_ref, fill_ref, sum_ref, loss_ref, stack_ref, floor_out_ref), refs = refs[:7], refs[7:]
    elif part == 1:
        (sum_in_ref, loss_in_ref, stack_ref, floor_in_ref, sum_ref, loss_ref), refs = refs[:6], refs[6:]
    else:
        (x_ref, beyond_ref, corner_ref, strip_ref, sum_in_ref, loss_in_ref, lift_end_ref, back_end_ref), refs = (
            refs[:8], refs[8:],
        )
        (out_ref, spill_ref, loss_ref), refs = refs[:3], refs[3:]
    (w_ref, p_ref, s_ref, lhs_ref, tile_ref, h_ref, floor_ref), refs = refs[:7], refs[7:]
    if part == 2:
        sum_ref, stack_ref = refs
    step = pl.program_id(0)
    steps = pl.num_programs(0)
    now = lax.rem(step, 2)
    which = lax.rem(step + begin, tiles)
    last_col = lax.axis_index("gx") == lax.axis_size("gx") - 1
    last_row = lax.axis_index("gy") == lax.axis_size("gy") - 1
    tall = rows * PATCH
    lane = lax.broadcasted_iota(jnp.int32, (SUB, LANES), 1)
    lanes = pl.ds(pl.multiple_of(which * LANES, LANES), LANES)

    def lift(at):
        lanes = pl.ds(pl.multiple_of(at * LANES, LANES), LANES)
        table = lift_ref[:, lanes]
        if part == 2:
            order = jnp.minimum(lax.rem(at + 1, tiles), 1)
            end = lift_end_ref[:, pl.ds(pl.multiple_of(order * LANES, LANES), LANES)]
            table = jnp.where(last_col, end, table)
        return jnp.dot(stack_ref[...], table, preferred_element_type=f32)

    @pl.when(step == 0)
    def _():
        if part == 0:
            sum_ref[...] = jnp.zeros_like(sum_ref)
            loss_ref[...] = jnp.zeros_like(loss_ref)
        else:
            sum_ref[...] = sum_in_ref[...]
            loss_ref[...] = loss_in_ref[...]
        if part != 1:
            w_ref[0] = x_ref[...]
            w_ref[0, pl.ds(rows, chans, stride=slots), :] = got_ref[0:chans, :]
            if part == 2:
                wide = lax.broadcasted_iota(jnp.int32, (chans, LANES), 1)
                for i in range(rows + 1):
                    column = beyond_ref[0:chans, :] if i < rows else corner_ref[0:chans, :]
                    column = pltpu.roll(column, cols - i if i < rows else cols, 1)
                    pick = pl.ds(i, chans, stride=slots)
                    w_ref[0, pick, :] = jnp.where(wide == cols, column, w_ref[0, pick, :])
            full = w_ref[0]
            floor_ref[0] = jnp.min(full) * STEP
            stack_ref[...] = stack3(full)
            if part == 0:
                floor_out_ref[...] = jnp.full((SUB, LANES), floor_ref[0], f32)
        else:
            floor_ref[0] = jnp.min(floor_in_ref[...])
        w_ref[0] = lift(which)

    tile_ref[0:tall, :] = jnp.where(mask_ref[:, lanes] != 0, lab_ref[:, lanes], -1)
    tile_ref[tall : tall + SUB, :] = got_ref[pl.ds(pl.multiple_of(chans + which * SUB, SUB), SUB), :].astype(jnp.int32)

    if part == 2:

        @pl.when(which == 0)
        def _():
            for j in range(PATCH):
                for b in range(groups):
                    pick = pl.ds(b * SUB * PATCH + j, SUB, stride=PATCH)
                    strip = strip_ref[b * SUB : b * SUB + SUB, :]
                    strip = pltpu.roll(strip, LANES - j * HALF, 1) if j else strip
                    strip = jnp.where(last_col, -1.0, strip)
                    tile_ref[pick, :] = jnp.where(lane < HALF, strip.astype(jnp.int32), tile_ref[pick, :])
            for j in range(HALF):
                strip = corner_ref[chans : chans + 1, :]
                strip = pltpu.roll(strip, LANES - j * HALF, 1) if j else strip
                strip = jnp.where(last_col, -1.0, strip)
                row = tile_ref[tall + j : tall + j + 1, :]
                tile_ref[tall + j : tall + j + 1, :] = jnp.where(lane[0:1] < HALF, strip.astype(jnp.int32), row)

    flat = jnp.full((SUB, LANES), 1.0 / STEP, f32)
    sub = lax.broadcasted_iota(jnp.int32, (SUB, LANES), 0)
    fold = [flat] * (groups - 1) + [jnp.where(last_row & (sub == SUB - 1), 0.0, flat)]
    fast = floor_ref[0] >= FLOOR

    def prepare():
        w_ref[1 - now] = lift(lax.rem(which + 1, tiles))

    loss_ref[...] += pixels(groups, chans, slots, fold, tile_ref, fast, prepare, w_ref.at[now], p_ref, s_ref, lhs_ref, h_ref)
    depth = 2 * LANES
    deep = pl.ds(pl.multiple_of(which * depth, depth), depth)
    table = back_ref[deep, :]
    if part == 2:
        end = back_end_ref[pl.ds(pl.multiple_of(lax.rem(which + 1, tiles) * depth, depth), depth), :]
        table = jnp.where(last_col, end, table)
    sum_ref[...] += jnp.dot(lhs_ref[...], table, preferred_element_type=f32)

    if part == 0:

        @pl.when((step == steps - 1) & (lax.axis_index("gx") == 0))
        def _():
            depth = stack_ref.shape[1]
            w_ref[1 - now] = jnp.dot(stack_ref[...], fill_ref[0:depth, :], preferred_element_type=f32)
            loss_ref[...] += first_columns(rows, groups, chans, slots, last_row, own_ref, got_ref, w_ref.at[1 - now], p_ref, lhs_ref)
            sum_ref[...] += jnp.dot(lhs_ref[...], fill_ref[depth:, :], preferred_element_type=f32)

    if part == 2:

        @pl.when(step == steps - 1)
        def _():
            w_ref[0] = jnp.zeros_like(w_ref[0])
            high = groups * SUB
            for c in range(chans):
                for kind in range(2):
                    at = (kind * chans + c) * high
                    row = c * slots + kind
                    w_ref[0, row : row + high, :] += sum_ref[at : at + high, :]
            out_ref[...] = w_ref[0] * (1.0 / STEP)
            spill_ref[...] = out_ref[pl.ds(rows, chans, stride=slots), :]


def grad_kernel(
    rows, cols, chans, slots, f_ref, beside_ref, g_ref, got_ref, loss_ref, count_ref, mine_ref, other_ref, sum_ref,
):
    row = lax.axis_index("gy")
    sum_ref[...] = g_ref[...]
    sum_ref[pl.ds(0, chans, stride=slots), :] += got_ref[...]
    lane = lax.broadcasted_iota(jnp.int32, (chans, LANES), 1)
    share = LANES // cols
    edge = jnp.zeros((chans, LANES), f32)
    tiles = []
    total = jnp.zeros((chans, LANES), f32)
    for k in range(0, rows, share):
        tile = None
        for r in range(share):
            piece = sum_ref[pl.ds(k + r, chans, stride=slots), :]
            total = total + piece
            edge = jnp.where(lane == k + r, pltpu.roll(piece, (k + r - cols) % LANES, 1), edge)
            if r:
                piece = pltpu.roll(piece, r * cols, 1)
            tile = piece if tile is None else jnp.where(lane < r * cols, tile, piece)
        tiles.append(tile.astype(bf16))
    block = f_ref[...].reshape(rows * cols, f_ref.shape[2])
    out = jnp.dot(jnp.concatenate(tiles, axis=1), block, preferred_element_type=f32)
    beside = jnp.concatenate([beside_ref[...], jnp.zeros((LANES - rows, f_ref.shape[2]), bf16)], axis=0)
    out = out + jnp.dot(edge.astype(bf16), beside, preferred_element_type=f32)
    total = jnp.where(lane <= cols, total, 0.0)
    square = jnp.concatenate([total, jnp.zeros((LANES - chans, LANES), f32)], axis=0)
    bias = jnp.sum(square.T, axis=0, keepdims=True)
    at = lax.broadcasted_iota(jnp.int32, (SUB, LANES), 0)
    rest = jnp.where(at == 1, jnp.sum(loss_ref[...]), count_ref[0, 0].astype(f32))
    stats = jnp.where(at == 0, bias, jnp.where(at < 3, rest, 0.0))
    pieces = out.shape[1] // LANES // 2
    for k in range(pieces):
        low = out[:, k * LANES : k * LANES + LANES]
        high = out[:, (pieces + k) * LANES : (pieces + k + 1) * LANES]
        mine_ref[k * chans : k * chans + chans, :] = jnp.where(row == 0, low, high)
        other_ref[k * chans : k * chans + chans, :] = jnp.where(row == 0, high, low)
    mine_ref[pieces * chans :, :] = stats
    other_ref[pieces * chans :, :] = stats


def final_kernel(chans, y_ref, z_ref, loss_ref, weight_ref, bias_ref):
    pieces = y_ref.shape[0] // chans
    lower = lax.axis_index("gy") == 0
    stats = y_ref[pieces * chans :, :]
    total = stats[2:3, 0:1]
    for k in range(pieces):
        y = y_ref[k * chans : k * chans + chans, :]
        z = z_ref[k * chans : k * chans + chans, :]
        weight_ref[:, k * LANES : k * LANES + LANES] = jnp.where(lower, y, z) / total
        weight_ref[:, (pieces + k) * LANES : (pieces + k + 1) * LANES] = jnp.where(lower, z, y) / total
    loss_ref[...] = stats[1:2, 0:1] / total
    bias_ref[...] = stats[0:1, 0:chans] / total


def body(features, probe_weight, probe_bias, labels, valid_mask, valid_count):
    rows, cols, width = features.shape
    chans = probe_weight.shape[1]
    gx, gy = lax.axis_size("gx"), lax.axis_size("gy")
    if gy != 2 or rows % SUB or 2 * cols != LANES or cols * PATCH % LANES or width % (2 * LANES) or gx & (gx - 1):
        raise ValueError("unsupported tile")
    groups = rows // SUB
    slots = rows + SUB
    count = groups * HALF
    tiles = cols * PATCH // LANES
    tall = rows * PATCH
    depth = 2 * LANES

    def forward(table):
        out = np.zeros((depth, table.shape[1]), np.float32)
        for k in range(3):
            out[k * cols : k * cols + cols] = table[:cols]
            out[3 * cols + k] = table[cols]
        return out

    def backward(table):
        out = np.zeros((table.shape[1] // LANES, 2, LANES, LANES), np.float32)
        out[:, :, :, : cols + 1] = table.T.reshape(-1, 1, LANES, cols + 1)
        return out.reshape(-1, LANES)

    inside, ending = column_tables(cols)
    ending = np.concatenate([ending[:, -LANES:], ending[:, :LANES]], axis=1)
    lift, lift_end, back, back_end = (
        jnp.asarray(t, bf16) for t in (forward(inside), forward(ending), backward(inside), backward(ending))
    )

    fill = np.zeros((2 * depth, LANES), np.float32)
    fill[[0, cols, 2 * cols]] = STEP
    for part in (depth, depth + LANES):
        fill[part : part + PATCH * HALF, 0] = STEP
    fill = jnp.asarray(fill, bf16)

    shape = lambda *dims: jax.ShapeDtypeStruct(dims, f32)
    held = lambda *dims, kind=f32: pltpu.VMEM(dims, kind)
    far = lambda v: pltpu.with_memory_space_constraint(v, pltpu.HBM)
    here = lambda v: pltpu.with_memory_space_constraint(v, pltpu.VMEM)
    ring = lambda v, axis: lax.ppermute(v, axis, [(i, (i - 1) % lax.axis_size(axis)) for i in range(lax.axis_size(axis))])
    swap = lambda v: lax.ppermute(v, "gy", [(0, 1), (1, 0)])
    tall_x = chans * slots

    own, head, weight, shift = pl.pallas_call(
        functools.partial(pack_kernel, rows),
        in_specs=[ANY] * 5,
        out_specs=[VMEM] * 4,
        out_shape=[
            held(rows + rows * width // LANES, LANES), held(tiles * SUB, LANES), held(chans, width, kind=bf16),
            held(chans, LANES),
        ],
        scratch_shapes=[
            pltpu.VMEM((rows, SUB, width), bf16),
            pltpu.VMEM((2, tall, LANES), jnp.int32),
            pltpu.VMEM((2, SUB, tiles * LANES), jnp.int32),
            pltpu.VMEM((1, chans), f32),
            pltpu.SemaphoreType.DMA((7,)),
        ],
        compiler_params=ROOM,
        name="pack",
    )(*(far(v) for v in (features, labels, valid_mask, probe_weight.T, probe_bias.reshape(1, chans))))
    side = lax.ppermute(own, "gx", [(i, i - 1) for i in range(1, gx)])
    x, edge = pl.pallas_call(
        functools.partial(logits_kernel, rows, cols, chans, slots, 4),
        in_specs=[VMEM] * 5,
        out_specs=[VMEM] * 2,
        out_shape=[held(tall_x, LANES), held(chans + tiles * SUB + SUB, LANES)],
        compiler_params=ROOM,
        name="logits",
    )(*(here(v) for v in (features, weight, shift, head, own)))
    got = ring(edge, "gy")

    sums = (2 * chans * rows, LANES)
    stacked = held(tall_x, depth, kind=bf16)

    def inner(part, begin, steps, *args):
        outs = [
            ([held(*sums), held(SUB, LANES), stacked, held(SUB, LANES)], [VMEM] * 4, [VMEM] * 3),
            ([held(*sums), held(SUB, LANES)], [VMEM] * 2, [VMEM] * 4),
            ([held(tall_x, LANES), held(chans, LANES), held(SUB, LANES)], [VMEM] * 3, [VMEM] * 8),
        ][part]
        return pl.pallas_call(
            functools.partial(inner_kernel, rows, cols, chans, slots, groups, part, begin, tiles),
            grid=(steps,),
            in_specs=[VMEM] * 5 + outs[2],
            out_specs=outs[1],
            out_shape=outs[0],
            scratch_shapes=[
                pltpu.VMEM((2, tall_x, LANES), f32),
                pltpu.VMEM((2 * chans * count, SUB, LANES), f32),
                pltpu.VMEM((2 * count + 1, SUB, LANES), f32),
                pltpu.VMEM((2 * chans * rows, depth), bf16),
                pltpu.VMEM((tall + SUB, LANES), jnp.int32),
                pltpu.VMEM((3 * chans, rows, LANES), bf16),
                pltpu.SMEM((1,), f32),
            ] + ([pltpu.VMEM(sums, f32), stacked] if part == 2 else []),
            cost_estimate=pl.CostEstimate(flops=10**9, bytes_accessed=2 * 10**6, transcendentals=10**6),
            compiler_params=ROOM,
            name=("inner_head", "inner_middle", "inner_tail")[part],
        )(*(here(v) for v in (got, lift, back, labels, valid_mask)), *args)

    middle = tiles // 2 + 2
    total, loss, stack, floor = inner(0, 1, middle - 1, here(x), here(own), here(fill))
    side, total = lax.optimization_barrier((side, total))
    beside, beyond = pl.pallas_call(
        functools.partial(beside_kernel, rows, chans),
        in_specs=[VMEM] * 3,
        out_specs=[VMEM] * 2,
        out_shape=[held(rows, width, kind=bf16), held(chans + SUB, LANES)],
        compiler_params=ROOM,
        name="beside",
    )(here(side), here(weight), here(shift))
    corner = ring(beyond, "gy")
    total, loss = inner(1, middle, tiles - 1 - middle, *(here(v) for v in (total, loss, stack, floor)))
    grad, spill, loss = inner(2, tiles - 1, 2, *(here(v) for v in (x, beyond, corner, side, total, loss, lift_end, back_end)))
    got = lax.ppermute(spill, "gy", [(i, (i + 1) % gy) for i in range(gy)])
    pack = (chans * width // 2 // LANES + SUB, LANES)
    mine, other = pl.pallas_call(
        functools.partial(grad_kernel, rows, cols, chans, slots),
        in_specs=[VMEM] * 5 + [SMEM],
        out_specs=[VMEM] * 2,
        out_shape=[held(*pack)] * 2,
        scratch_shapes=[pltpu.VMEM((tall_x, LANES), f32)],
        compiler_params=ROOM,
        name="grad",
    )(*(here(v) for v in (features, beside, grad, got, loss)), valid_count)

    total = mine + swap(other)
    steps = [1 << k for k in range(gx.bit_length() - 1)]
    for one, two in zip(steps, steps[1::-1] + steps[2:]):
        pairs = [(gy * i + g, gy * (i ^ (two if g else one)) + g) for i in range(gx) for g in range(gy)]
        total = total + lax.ppermute(total, ("gx", "gy"), pairs)
    loss, weight, bias = pl.pallas_call(
        functools.partial(final_kernel, chans),
        in_specs=[VMEM] * 2,
        out_specs=[VMEM] * 3,
        out_shape=[shape(1, 1), shape(chans, width), shape(1, chans)],
        compiler_params=ROOM,
        name="final",
    )(here(total), here(swap(total)))
    return loss.reshape(1), weight.T, bias.reshape(chans)


def solution(mesh):
    return jax.shard_map(
        body,
        mesh=mesh,
        in_specs=(
            P(("groups", "gy"), "gx", None),
            P(),
            P(),
            P(("groups", "gy"), "gx"),
            P(("groups", "gy"), "gx"),
            P(("groups", "gy"), "gx"),
        ),
        out_specs=(P("groups"), P("groups", None), P("groups")),
        check_vma=False,
    )
```

```python
import functools
import math

import jax
import jax.numpy as jnp
import numpy as np
from jax import lax
from jax.experimental import pallas as pl
from jax.experimental.pallas import tpu as pltpu
from jax.sharding import PartitionSpec as P

PATCH = 14
HALF = PATCH // 2
STEP = 2 * PATCH
LANES = 128
SUB = 8
LOG2E = 1.0 / math.log(2.0)
LN2 = math.log(2.0)
FLOOR = -100.0
f32 = jnp.float32
bf16 = jnp.bfloat16
VMEM = pl.BlockSpec(memory_space=pltpu.VMEM)
ANY = pl.BlockSpec(memory_space=pl.ANY)
ROOM = pltpu.CompilerParams(vmem_limit_bytes=16 * 2**20)
SMEM = pl.BlockSpec(memory_space=pltpu.SMEM)


def whole(shape):
    return pl.BlockSpec(shape, lambda *ids: (0,) * len(shape))


def column_tables(cols):
    tables = np.zeros((2, cols + 1, cols * PATCH), np.float32)
    for q in range(cols * PATCH):
        i, k = divmod((q if q >= HALF else q + cols * PATCH) - HALF, PATCH)
        far = 2 * k + 1
        for end in range(2):
            if end and i == cols - 1:
                tables[end, i + (k >= HALF), q] = STEP
            else:
                tables[end, i, q] = STEP - far
                tables[end, i + 1, q] = far
    return tables


def split3(x):
    hi = x.astype(bf16)
    rest = x - hi.astype(f32)
    mid = rest.astype(bf16)
    return hi, mid, (rest - mid.astype(f32)).astype(bf16)


def stack3(x):
    cols = LANES // 2
    lane = lax.broadcasted_iota(jnp.int32, x.shape, 1)
    hi, mid, low = (part.astype(f32) for part in split3(x))
    first = jnp.where(lane < cols, hi, pltpu.roll(mid, cols, 1))
    second = jnp.where(lane == cols + 1, pltpu.roll(mid, 1, 1), pltpu.roll(low, 2, 1))
    second = jnp.where(lane == cols, hi, jnp.where(lane < cols + 3, second, 0.0))
    second = jnp.where(lane < cols, low, second)
    return jnp.concatenate([first.astype(bf16), second.astype(bf16)], axis=1)


def pack_kernel(
    rows, f_ref, lab_ref, mask_ref, w_ref, bias_ref, out_ref, head_ref, weight_ref, shift_ref, f_vmem, l_vmem, h_vmem, b_vmem, sem,
):
    width = f_vmem.shape[2]
    tiles = head_ref.shape[0] // SUB
    copies = [
        pltpu.make_async_copy(lab_ref.at[:, pl.ds(0, LANES)], l_vmem.at[0], sem.at[0]),
        pltpu.make_async_copy(mask_ref.at[:, pl.ds(0, LANES)], l_vmem.at[1], sem.at[1]),
        pltpu.make_async_copy(f_ref.at[:, pl.ds(0, SUB)], f_vmem, sem.at[2]),
        pltpu.make_async_copy(lab_ref.at[pl.ds(0, SUB)], h_vmem.at[0], sem.at[3]),
        pltpu.make_async_copy(mask_ref.at[pl.ds(0, SUB)], h_vmem.at[1], sem.at[4]),
        pltpu.make_async_copy(w_ref, weight_ref, sem.at[5]),
        pltpu.make_async_copy(bias_ref, b_vmem, sem.at[6]),
    ]
    for copy in copies:
        copy.start()
    at = lax.broadcasted_iota(jnp.int32, (SUB, LANES), 1)
    for copy in copies[:2]:
        copy.wait()
    for b in range(rows // SUB):
        strip = jnp.full((SUB, LANES), -1.0, f32)
        for j in range(PATCH):
            pick = pl.ds(b * SUB * PATCH + j, SUB, stride=PATCH)
            lab = jnp.where(l_vmem[1, pick, :] != 0, l_vmem[0, pick, :], -1).astype(f32)
            here = (at >= j * HALF) & (at < j * HALF + HALF)
            strip = jnp.where(here, pltpu.roll(lab, j * HALF, 1) if j else lab, strip)
        out_ref[b * SUB : b * SUB + SUB, :] = strip
    copies[2].wait()
    for i in range(rows):
        line = f_vmem[i].astype(f32)
        for k in range(width // LANES):
            out_ref[rows + k * rows + i : rows + k * rows + i + 1, :] = line[0:1, k * LANES : k * LANES + LANES]
    for copy in copies[3:]:
        copy.wait()
    for t in range(tiles):
        lanes = slice(t * LANES, t * LANES + LANES)
        head_ref[t * SUB : t * SUB + SUB, :] = jnp.where(h_vmem[1, :, lanes] != 0, h_vmem[0, :, lanes], -1).astype(f32)
    chans = shift_ref.shape[0]
    bias = jnp.concatenate([b_vmem[...], jnp.zeros((1, LANES - chans), f32)], axis=1)
    shift_ref[...] = jnp.broadcast_to(bias, (LANES, LANES)).T[0:chans, :]


def score_of(w_ref, shift_ref, block):
    score = lax.dot_general(w_ref[...], block, (((1,), (1,)), ((), ())), preferred_element_type=f32)
    score = score + jnp.concatenate([shift_ref[...]] * (block.shape[0] // LANES), axis=1)
    return (score - jnp.max(score, axis=0, keepdims=True)) * (LOG2E / STEP)


def logits_kernel(rows, cols, chans, slots, per, f_ref, w_ref, shift_ref, head_ref, side_ref, x_ref, e_ref):
    x_ref[...] = jnp.zeros_like(x_ref)
    lane = lax.broadcasted_iota(jnp.int32, (chans, LANES), 1)
    for step in range(rows // per):
        score = score_of(w_ref, shift_ref, f_ref[step * per : step * per + per].reshape(per * cols, f_ref.shape[2]))
        for k in range(per):
            i, off = step * per + k, k * cols
            tile = score[:, off // LANES * LANES : off // LANES * LANES + LANES]
            if off % LANES:
                tile = pltpu.roll(tile, LANES - off % LANES, 1)
            tile = jnp.where(lane < cols, tile, 0.0)
            x_ref[pl.ds(i, chans, stride=slots), :] = tile
            if i == 0:
                e_ref[0:chans, :] = tile
    e_ref[chans : chans + head_ref.shape[0], :] = head_ref[...]
    e_ref[chans + head_ref.shape[0] :, :] = side_ref[0:SUB, :]


def beside_kernel(rows, chans, side_ref, w_ref, shift_ref, beside_ref, out_ref):
    width = w_ref.shape[1]
    side = jnp.concatenate(
        [side_ref[rows + k * rows : rows + k * rows + rows, :] for k in range(width // LANES)], axis=1
    ).astype(bf16)
    beside_ref[...] = side
    side = jnp.concatenate([side, jnp.zeros((LANES - rows, width), bf16)], axis=0)
    out_ref[0:chans, :] = score_of(w_ref, shift_ref, side)
    out_ref[chans:, :] = side_ref[0:SUB, :]


def two_sums(item):
    totals, runs = [], []
    for half in range(2):
        total = run = None
        for m in reversed(range(HALF)):
            v = item(half, m)
            total = v if total is None else total + v
            if m:
                run = total if run is None else run + total
        totals.append(total)
        runs.append(run)
    return totals[0], totals[1], runs[0] - runs[1], totals[0] - totals[1]


def tally(packed, c, h_ref):
    one, none, mid = (jnp.asarray(v, bf16) for v in (1, 0, 0.5))
    mark = jnp.asarray(c, bf16) if isinstance(c, int) else c.astype(f32).astype(bf16)
    up, down, run, lean = two_sums(lambda half, m: jnp.where(packed[half * HALF + m] == mark, one, none))
    h_ref[3 * c] = up
    h_ref[3 * c + 1] = down
    h_ref[3 * c + 2] = run + lean * mid


def softmax_fast(groups, chans, slots, fold, w_ref, p_ref, packed, h_ref):
    sums = [None] * (2 * groups * HALF)
    for c in range(chans):
        tally(packed, c, h_ref)
        for b in range(groups):
            row = c * slots + SUB * b
            upper = w_ref[row : row + SUB, :]
            lower = w_ref[row + 1 : row + 1 + SUB, :]
            slope = (lower - upper) * fold[b]
            twice = slope + slope
            for half, (p, ratio) in enumerate(((upper + slope, twice), (lower - slope, -twice))):
                p, ratio = jnp.exp2(p), jnp.exp2(ratio)
                for m in range(HALF):
                    k = (half * groups + b) * HALF + m
                    if m:
                        p = p * ratio
                    p_ref[c * len(sums) + k] = p
                    sums[k] = p if sums[k] is None else sums[k] + p
    return sums


def softmax_slow(groups, chans, slots, fold, w_ref, p_ref, labels, weights):
    count = len(labels)
    sums, losses = [], jnp.zeros((SUB, LANES), f32)
    for k in range(count):
        half, b, m = k // (groups * HALF), k // HALF % groups, k % HALF

        def score(c, half=half, b=b, m=m):
            row = c * slots + SUB * b
            near = w_ref[pl.ds(row + half, SUB), :]
            away = w_ref[pl.ds(row + 1 - half, SUB), :]
            return near + (away - near) * fold[b] * (2 * m + 1.0)

        top = lax.fori_loop(1, chans, lambda c, t, score=score: jnp.maximum(t, score(c)), score(0))

        def take(c, carry, k=k, top=top, score=score):
            total, picked = carry
            shifted = score(c) - top
            p = jnp.exp2(shifted)
            p_ref[c * count + k] = p
            return total + p, jnp.where(labels[k] == c, shifted, picked)

        zero = jnp.zeros((SUB, LANES), f32)
        total, picked = lax.fori_loop(0, chans, take, (zero, zero))
        sums.append(total)
        losses = losses - weights[k] * picked
    return sums, losses


def pixels(groups, chans, slots, fold, lab_ref, fast, prepare, w_ref, p_ref, s_ref, lhs_ref, h_ref):
    count = 2 * groups * HALF
    labels = []
    for half in range(2):
        for b in range(groups):
            for m in range(HALF):
                k = PATCH - 1 - m if half else m
                labels.append(lab_ref[pl.ds(b * SUB * PATCH + HALF + k, SUB, stride=PATCH), :])
    weights = [jnp.where(lab >= 0, 1.0, 0.0) for lab in labels]
    packed = [
        jnp.concatenate([labels[(half * groups + b) * HALF + m] for b in range(groups)], axis=0).astype(f32).astype(bf16)
        for half in range(2)
        for m in range(HALF)
    ]

    @pl.when(fast)
    def _():
        sums = softmax_fast(groups, chans, slots, fold, w_ref, p_ref, packed, h_ref)
        for k in range(count):
            s_ref[k] = sums[k]
        s_ref[count] = jnp.zeros((SUB, LANES), f32)
        prepare()

    @pl.when(jnp.logical_not(fast))
    def _():
        sums, losses = softmax_slow(groups, chans, slots, fold, w_ref, p_ref, labels, weights)
        for k in range(count):
            s_ref[k] = sums[k]
        s_ref[count] = losses
        lax.fori_loop(0, chans, lambda c, _: tally(packed, c, h_ref), None)
        prepare()

    loss = jnp.zeros((SUB, LANES), f32)
    scale = []
    for k in range(count):
        total = s_ref[k]
        loss = loss + weights[k] * jnp.log(total)
        scale.append(weights[k] / total)
    picked = jnp.zeros((SUB, LANES), f32)
    tall = groups * SUB
    for c in range(chans):
        hits = [h_ref[3 * c + k].astype(f32) for k in range(3)]
        parts = [[], []]
        for b in range(groups):
            row = c * slots + SUB * b
            up, down, lean = (v[b * SUB : b * SUB + SUB] for v in hits)
            lean = lean * (fold[b] * 2.0)
            up, down = up - lean, down + lean
            picked = picked + up * w_ref[row : row + SUB, :] + down * w_ref[row + 1 : row + 1 + SUB, :]
            above, below, run, lean = two_sums(
                lambda half, m: p_ref[c * count + (half * groups + b) * HALF + m] * scale[(half * groups + b) * HALF + m]
            )
            lean = (run + lean * 0.5) * (fold[b] * 2.0)
            parts[0].append((above - up) - lean)
            parts[1].append((below - down) + lean)
        for kind in range(2):
            g = jnp.concatenate(parts[kind], axis=0)
            hi = g.astype(bf16)
            at = (kind * chans + c) * tall
            lhs_ref[at : at + tall, 0:LANES] = hi
            lhs_ref[at : at + tall, LANES:] = (g - hi.astype(f32)).astype(bf16)
    return loss + LN2 * jnp.where(fast, -picked, s_ref[count])


def first_columns(rows, groups, chans, slots, last_row, own_ref, got_ref, w_ref, p_ref, lhs_ref):
    lane = lax.broadcasted_iota(jnp.int32, (SUB, LANES), 1)
    sub = lax.broadcasted_iota(jnp.int32, (SUB, LANES), 0)
    turn = HALF * HALF
    share = jnp.zeros((SUB, LANES), f32)
    for k in range(PATCH):
        share = jnp.where(lane >= k * HALF, (2 * k + 1.0) / STEP, share)
    end = jnp.where(last_row & (sub == SUB - 1), jnp.where(lane < turn, 0.0, 1.0), share)
    shares = [share] * (groups - 1) + [end]
    tall = groups * SUB
    loss = jnp.zeros((SUB, LANES), f32)
    scale, labels = [], []
    for b in range(groups):
        upper = own_ref[b * SUB : b * SUB + SUB, :]
        at = (b + 1) * SUB
        lower = got_ref[got_ref.shape[0] - SUB :, :] if at == rows else own_ref[at : at + SUB, :]
        lower = jnp.where(sub == SUB - 1, pltpu.roll(lower, SUB - 1, 0), pltpu.roll(upper, SUB - 1, 0))
        label = jnp.where(lane < turn, pltpu.roll(upper, LANES - turn, 1), pltpu.roll(lower, turn, 1))
        label = jnp.where(lane < PATCH * HALF, label, -1.0).astype(jnp.int32)
        top = None
        for c in range(chans):
            row = c * slots + SUB * b
            v = w_ref[row : row + SUB, :]
            v = v + (w_ref[row + 1 : row + 1 + SUB, :] - v) * shares[b]
            p_ref[c * groups + b] = v
            top = v if top is None else jnp.maximum(top, v)
        total = picked = jnp.zeros((SUB, LANES), f32)
        for c in range(chans):
            v = p_ref[c * groups + b] - top
            picked = jnp.where(label == c, v, picked)
            v = jnp.exp2(v)
            p_ref[c * groups + b] = v
            total = total + v
        weight = jnp.where(label >= 0, 1.0, 0.0)
        loss = loss + weight * (jnp.log(total) - LN2 * picked)
        scale.append(weight / total)
        labels.append(label)
    for c in range(chans):
        parts = [[], []]
        for b in range(groups):
            g = p_ref[c * groups + b] * scale[b] - jnp.where(labels[b] == c, 1.0, 0.0)
            below = g * shares[b]
            parts[0].append(g - below)
            parts[1].append(below)
        for kind in range(2):
            g = jnp.concatenate(parts[kind], axis=0)
            hi = g.astype(bf16)
            at = (kind * chans + c) * tall
            lhs_ref[at : at + tall, 0:LANES] = hi
            lhs_ref[at : at + tall, LANES:] = (g - hi.astype(f32)).astype(bf16)
    return loss


def inner_kernel(rows, cols, chans, slots, groups, part, begin, tiles, *refs):
    (got_ref, lift_ref, back_ref, lab_ref, mask_ref), refs = refs[:5], refs[5:]
    if part == 0:
        (x_ref, own_ref, fill_ref, sum_ref, loss_ref, stack_ref, floor_out_ref), refs = refs[:7], refs[7:]
    elif part == 1:
        (sum_in_ref, loss_in_ref, stack_ref, floor_in_ref, sum_ref, loss_ref), refs = refs[:6], refs[6:]
    else:
        (x_ref, beyond_ref, corner_ref, strip_ref, sum_in_ref, loss_in_ref, lift_end_ref, back_end_ref), refs = (
            refs[:8], refs[8:],
        )
        (out_ref, spill_ref, loss_ref), refs = refs[:3], refs[3:]
    (w_ref, p_ref, s_ref, lhs_ref, tile_ref, h_ref, floor_ref), refs = refs[:7], refs[7:]
    if part == 2:
        sum_ref, stack_ref = refs
    step = pl.program_id(0)
    steps = pl.num_programs(0)
    now = lax.rem(step, 2)
    which = lax.rem(step + begin, tiles)
    last_col = lax.axis_index("gx") == lax.axis_size("gx") - 1
    last_row = lax.axis_index("gy") == lax.axis_size("gy") - 1
    tall = rows * PATCH
    lane = lax.broadcasted_iota(jnp.int32, (SUB, LANES), 1)
    lanes = pl.ds(pl.multiple_of(which * LANES, LANES), LANES)

    def lift(at):
        lanes = pl.ds(pl.multiple_of(at * LANES, LANES), LANES)
        table = lift_ref[:, lanes]
        if part == 2:
            order = jnp.minimum(lax.rem(at + 1, tiles), 1)
            end = lift_end_ref[:, pl.ds(pl.multiple_of(order * LANES, LANES), LANES)]
            table = jnp.where(last_col, end, table)
        return jnp.dot(stack_ref[...], table, preferred_element_type=f32)

    @pl.when(step == 0)
    def _():
        if part == 0:
            sum_ref[...] = jnp.zeros_like(sum_ref)
            loss_ref[...] = jnp.zeros_like(loss_ref)
        else:
            sum_ref[...] = sum_in_ref[...]
            loss_ref[...] = loss_in_ref[...]
        if part != 1:
            w_ref[0] = x_ref[...]
            w_ref[0, pl.ds(rows, chans, stride=slots), :] = got_ref[0:chans, :]
            if part == 2:
                wide = lax.broadcasted_iota(jnp.int32, (chans, LANES), 1)
                for i in range(rows + 1):
                    column = beyond_ref[0:chans, :] if i < rows else corner_ref[0:chans, :]
                    column = pltpu.roll(column, cols - i if i < rows else cols, 1)
                    pick = pl.ds(i, chans, stride=slots)
                    w_ref[0, pick, :] = jnp.where(wide == cols, column, w_ref[0, pick, :])
            full = w_ref[0]
            floor_ref[0] = jnp.min(full) * STEP
            stack_ref[...] = stack3(full)
            if part == 0:
                floor_out_ref[...] = jnp.full((SUB, LANES), floor_ref[0], f32)
        else:
            floor_ref[0] = jnp.min(floor_in_ref[...])
        w_ref[0] = lift(which)

    tile_ref[0:tall, :] = jnp.where(mask_ref[:, lanes] != 0, lab_ref[:, lanes], -1)
    tile_ref[tall : tall + SUB, :] = got_ref[pl.ds(pl.multiple_of(chans + which * SUB, SUB), SUB), :].astype(jnp.int32)

    if part == 2:

        @pl.when(which == 0)
        def _():
            for j in range(PATCH):
                for b in range(groups):
                    pick = pl.ds(b * SUB * PATCH + j, SUB, stride=PATCH)
                    strip = strip_ref[b * SUB : b * SUB + SUB, :]
                    strip = pltpu.roll(strip, LANES - j * HALF, 1) if j else strip
                    strip = jnp.where(last_col, -1.0, strip)
                    tile_ref[pick, :] = jnp.where(lane < HALF, strip.astype(jnp.int32), tile_ref[pick, :])
            for j in range(HALF):
                strip = corner_ref[chans : chans + 1, :]
                strip = pltpu.roll(strip, LANES - j * HALF, 1) if j else strip
                strip = jnp.where(last_col, -1.0, strip)
                row = tile_ref[tall + j : tall + j + 1, :]
                tile_ref[tall + j : tall + j + 1, :] = jnp.where(lane[0:1] < HALF, strip.astype(jnp.int32), row)

    flat = jnp.full((SUB, LANES), 1.0 / STEP, f32)
    sub = lax.broadcasted_iota(jnp.int32, (SUB, LANES), 0)
    fold = [flat] * (groups - 1) + [jnp.where(last_row & (sub == SUB - 1), 0.0, flat)]
    fast = floor_ref[0] >= FLOOR

    def prepare():
        w_ref[1 - now] = lift(lax.rem(which + 1, tiles))

    loss_ref[...] += pixels(groups, chans, slots, fold, tile_ref, fast, prepare, w_ref.at[now], p_ref, s_ref, lhs_ref, h_ref)
    depth = 2 * LANES
    deep = pl.ds(pl.multiple_of(which * depth, depth), depth)
    table = back_ref[deep, :]
    if part == 2:
        end = back_end_ref[pl.ds(pl.multiple_of(lax.rem(which + 1, tiles) * depth, depth), depth), :]
        table = jnp.where(last_col, end, table)
    sum_ref[...] += jnp.dot(lhs_ref[...], table, preferred_element_type=f32)

    if part == 0:

        @pl.when((step == steps - 1) & (lax.axis_index("gx") == 0))
        def _():
            depth = stack_ref.shape[1]
            w_ref[1 - now] = jnp.dot(stack_ref[...], fill_ref[0:depth, :], preferred_element_type=f32)
            loss_ref[...] += first_columns(rows, groups, chans, slots, last_row, own_ref, got_ref, w_ref.at[1 - now], p_ref, lhs_ref)
            sum_ref[...] += jnp.dot(lhs_ref[...], fill_ref[depth:, :], preferred_element_type=f32)

    if part == 2:

        @pl.when(step == steps - 1)
        def _():
            w_ref[0] = jnp.zeros_like(w_ref[0])
            high = groups * SUB
            for c in range(chans):
                for kind in range(2):
                    at = (kind * chans + c) * high
                    row = c * slots + kind
                    w_ref[0, row : row + high, :] += sum_ref[at : at + high, :]
            out_ref[...] = w_ref[0] * (1.0 / STEP)
            spill_ref[...] = out_ref[pl.ds(rows, chans, stride=slots), :]


def grad_kernel(
    rows, cols, chans, slots, f_ref, beside_ref, g_ref, got_ref, loss_ref, count_ref, mine_ref, other_ref, sum_ref,
):
    row = lax.axis_index("gy")
    sum_ref[...] = g_ref[...]
    sum_ref[pl.ds(0, chans, stride=slots), :] += got_ref[...]
    lane = lax.broadcasted_iota(jnp.int32, (chans, LANES), 1)
    share = LANES // cols
    edge = jnp.zeros((chans, LANES), f32)
    tiles = []
    total = jnp.zeros((chans, LANES), f32)
    for k in range(0, rows, share):
        tile = None
        for r in range(share):
            piece = sum_ref[pl.ds(k + r, chans, stride=slots), :]
            total = total + piece
            edge = jnp.where(lane == k + r, pltpu.roll(piece, (k + r - cols) % LANES, 1), edge)
            if r:
                piece = pltpu.roll(piece, r * cols, 1)
            tile = piece if tile is None else jnp.where(lane < r * cols, tile, piece)
        tiles.append(tile.astype(bf16))
    block = f_ref[...].reshape(rows * cols, f_ref.shape[2])
    out = jnp.dot(jnp.concatenate(tiles, axis=1), block, preferred_element_type=f32)
    beside = jnp.concatenate([beside_ref[...], jnp.zeros((LANES - rows, f_ref.shape[2]), bf16)], axis=0)
    out = out + jnp.dot(edge.astype(bf16), beside, preferred_element_type=f32)
    total = jnp.where(lane <= cols, total, 0.0)
    square = jnp.concatenate([total, jnp.zeros((LANES - chans, LANES), f32)], axis=0)
    bias = jnp.sum(square.T, axis=0, keepdims=True)
    at = lax.broadcasted_iota(jnp.int32, (SUB, LANES), 0)
    rest = jnp.where(at == 1, jnp.sum(loss_ref[...]), count_ref[0, 0].astype(f32))
    stats = jnp.where(at == 0, bias, jnp.where(at < 3, rest, 0.0))
    pieces = out.shape[1] // LANES // 2
    for k in range(pieces):
        low = out[:, k * LANES : k * LANES + LANES]
        high = out[:, (pieces + k) * LANES : (pieces + k + 1) * LANES]
        mine_ref[k * chans : k * chans + chans, :] = jnp.where(row == 0, low, high)
        other_ref[k * chans : k * chans + chans, :] = jnp.where(row == 0, high, low)
    mine_ref[pieces * chans :, :] = stats
    other_ref[pieces * chans :, :] = stats


def final_kernel(chans, y_ref, z_ref, loss_ref, weight_ref, bias_ref):
    pieces = y_ref.shape[0] // chans
    lower = lax.axis_index("gy") == 0
    stats = y_ref[pieces * chans :, :]
    total = stats[2:3, 0:1]
    for k in range(pieces):
        y = y_ref[k * chans : k * chans + chans, :]
        z = z_ref[k * chans : k * chans + chans, :]
        weight_ref[:, k * LANES : k * LANES + LANES] = jnp.where(lower, y, z) / total
        weight_ref[:, (pieces + k) * LANES : (pieces + k + 1) * LANES] = jnp.where(lower, z, y) / total
    loss_ref[...] = stats[1:2, 0:1] / total
    bias_ref[...] = stats[0:1, 0:chans] / total


def body(features, probe_weight, probe_bias, labels, valid_mask, valid_count):
    rows, cols, width = features.shape
    chans = probe_weight.shape[1]
    gx, gy = lax.axis_size("gx"), lax.axis_size("gy")
    if gy != 2 or rows % SUB or 2 * cols != LANES or cols * PATCH % LANES or width % (2 * LANES) or gx & (gx - 1):
        raise ValueError("unsupported tile")
    groups = rows // SUB
    slots = rows + SUB
    count = groups * HALF
    tiles = cols * PATCH // LANES
    tall = rows * PATCH
    depth = 2 * LANES

    def forward(table):
        out = np.zeros((depth, table.shape[1]), np.float32)
        for k in range(3):
            out[k * cols : k * cols + cols] = table[:cols]
            out[3 * cols + k] = table[cols]
        return out

    def backward(table):
        out = np.zeros((table.shape[1] // LANES, 2, LANES, LANES), np.float32)
        out[:, :, :, : cols + 1] = table.T.reshape(-1, 1, LANES, cols + 1)
        return out.reshape(-1, LANES)

    inside, ending = column_tables(cols)
    ending = np.concatenate([ending[:, -LANES:], ending[:, :LANES]], axis=1)
    lift, lift_end, back, back_end = (
        jnp.asarray(t, bf16) for t in (forward(inside), forward(ending), backward(inside), backward(ending))
    )

    fill = np.zeros((2 * depth, LANES), np.float32)
    fill[[0, cols, 2 * cols]] = STEP
    for part in (depth, depth + LANES):
        fill[part : part + PATCH * HALF, 0] = STEP
    fill = jnp.asarray(fill, bf16)

    shape = lambda *dims: jax.ShapeDtypeStruct(dims, f32)
    held = lambda *dims, kind=f32: pltpu.VMEM(dims, kind)
    far = lambda v: pltpu.with_memory_space_constraint(v, pltpu.HBM)
    here = lambda v: pltpu.with_memory_space_constraint(v, pltpu.VMEM)
    ring = lambda v, axis: lax.ppermute(v, axis, [(i, (i - 1) % lax.axis_size(axis)) for i in range(lax.axis_size(axis))])
    swap = lambda v: lax.ppermute(v, "gy", [(0, 1), (1, 0)])
    tall_x = chans * slots

    own, head, weight, shift = pl.pallas_call(
        functools.partial(pack_kernel, rows),
        in_specs=[ANY] * 5,
        out_specs=[VMEM] * 4,
        out_shape=[
            held(rows + rows * width // LANES, LANES), held(tiles * SUB, LANES), held(chans, width, kind=bf16),
            held(chans, LANES),
        ],
        scratch_shapes=[
            pltpu.VMEM((rows, SUB, width), bf16),
            pltpu.VMEM((2, tall, LANES), jnp.int32),
            pltpu.VMEM((2, SUB, tiles * LANES), jnp.int32),
            pltpu.VMEM((1, chans), f32),
            pltpu.SemaphoreType.DMA((7,)),
        ],
        compiler_params=ROOM,
        name="pack",
    )(*(far(v) for v in (features, labels, valid_mask, probe_weight.T, probe_bias.reshape(1, chans))))
    side = lax.ppermute(own, "gx", [(i, i - 1) for i in range(1, gx)])
    x, edge = pl.pallas_call(
        functools.partial(logits_kernel, rows, cols, chans, slots, 4),
        in_specs=[VMEM] * 5,
        out_specs=[VMEM] * 2,
        out_shape=[held(tall_x, LANES), held(chans + tiles * SUB + SUB, LANES)],
        compiler_params=ROOM,
        name="logits",
    )(*(here(v) for v in (features, weight, shift, head, own)))
    got = ring(edge, "gy")

    sums = (2 * chans * rows, LANES)
    stacked = held(tall_x, depth, kind=bf16)

    def inner(part, begin, steps, *args):
        outs = [
            ([held(*sums), held(SUB, LANES), stacked, held(SUB, LANES)], [VMEM] * 4, [VMEM] * 3),
            ([held(*sums), held(SUB, LANES)], [VMEM] * 2, [VMEM] * 4),
            ([held(tall_x, LANES), held(chans, LANES), held(SUB, LANES)], [VMEM] * 3, [VMEM] * 8),
        ][part]
        return pl.pallas_call(
            functools.partial(inner_kernel, rows, cols, chans, slots, groups, part, begin, tiles),
            grid=(steps,),
            in_specs=[VMEM] * 5 + outs[2],
            out_specs=outs[1],
            out_shape=outs[0],
            scratch_shapes=[
                pltpu.VMEM((2, tall_x, LANES), f32),
                pltpu.VMEM((2 * chans * count, SUB, LANES), f32),
                pltpu.VMEM((2 * count + 1, SUB, LANES), f32),
                pltpu.VMEM((2 * chans * rows, depth), bf16),
                pltpu.VMEM((tall + SUB, LANES), jnp.int32),
                pltpu.VMEM((3 * chans, rows, LANES), bf16),
                pltpu.SMEM((1,), f32),
            ] + ([pltpu.VMEM(sums, f32), stacked] if part == 2 else []),
            cost_estimate=pl.CostEstimate(flops=10**9, bytes_accessed=2 * 10**6, transcendentals=10**6),
            compiler_params=ROOM,
            name=("inner_head", "inner_middle", "inner_tail")[part],
        )(*(here(v) for v in (got, lift, back, labels, valid_mask)), *args)

    middle = tiles // 2 + 2
    total, loss, stack, floor = inner(0, 1, middle - 1, here(x), here(own), here(fill))
    side, total = lax.optimization_barrier((side, total))
    beside, beyond = pl.pallas_call(
        functools.partial(beside_kernel, rows, chans),
        in_specs=[VMEM] * 3,
        out_specs=[VMEM] * 2,
        out_shape=[held(rows, width, kind=bf16), held(chans + SUB, LANES)],
        compiler_params=ROOM,
        name="beside",
    )(here(side), here(weight), here(shift))
    corner = ring(beyond, "gy")
    total, loss = inner(1, middle, tiles - 1 - middle, *(here(v) for v in (total, loss, stack, floor)))
    grad, spill, loss = inner(2, tiles - 1, 2, *(here(v) for v in (x, beyond, corner, side, total, loss, lift_end, back_end)))
    got = lax.ppermute(spill, "gy", [(i, (i + 1) % gy) for i in range(gy)])
    pack = (chans * width // 2 // LANES + SUB, LANES)
    mine, other = pl.pallas_call(
        functools.partial(grad_kernel, rows, cols, chans, slots),
        in_specs=[VMEM] * 5 + [SMEM],
        out_specs=[VMEM] * 2,
        out_shape=[held(*pack)] * 2,
        scratch_shapes=[pltpu.VMEM((tall_x, LANES), f32)],
        compiler_params=ROOM,
        name="grad",
    )(*(here(v) for v in (features, beside, grad, got, loss)), valid_count)

    total = mine + swap(other)
    steps = [1 << k for k in range(gx.bit_length() - 1)]
    for one, two in zip(steps, steps[1::-1] + steps[2:]):
        pairs = [(gy * i + g, gy * (i ^ (two if g else one)) + g) for i in range(gx) for g in range(gy)]
        total = total + lax.ppermute(total, ("gx", "gy"), pairs)
    loss, weight, bias = pl.pallas_call(
        functools.partial(final_kernel, chans),
        in_specs=[VMEM] * 2,
        out_specs=[VMEM] * 3,
        out_shape=[shape(1, 1), shape(chans, width), shape(1, chans)],
        compiler_params=ROOM,
        name="final",
    )(here(total), here(swap(total)))
    return loss.reshape(1), weight.T, bias.reshape(chans)


def solution(mesh):
    return jax.shard_map(
        body,
        mesh=mesh,
        in_specs=(
            P(("groups", "gy"), "gx", None),
            P(),
            P(),
            P(("groups", "gy"), "gx"),
            P(("groups", "gy"), "gx"),
            P(("groups", "gy"), "gx"),
        ),
        out_specs=(P("groups"), P("groups", None), P("groups")),
        check_vma=False,
    )
```
